128 devices in a mesh: face: 8 (over x, core), sub: 16 (over y, z).
Axes of the slice: x: 4, y: 4, z: 4, core: 2. Of those that a mesh axis runs over, the one named last changes fastest.
Arguments:
- grid_latent: bfloat16 [65536, 512], P(('face', 'sub')), may hold values from -6 to 6
- mesh_latent: bfloat16 [16384, 512], P(('face', 'sub')), may hold values from -6 to 6
- edge_latent: bfloat16 [131072, 512], P(('face', 'sub')), may hold values from -6 to 6
- mesh_cotangent: bfloat16 [16384, 512], P(('face', 'sub')), may hold values from -6 to 6
- edge_cotangent: bfloat16 [131072, 512], P(('face', 'sub')), may hold values from -6 to 6
- grid_send: int32 [128, 4, 256], P(('face', 'sub')), may hold values from 0 to 511
- grid_slot: int32 [131072], P(('face', 'sub')), may hold values from 0 to 1535, as said below
- grid_target: int32 [131072], P(('face', 'sub')), may hold values from 0 to 127
- mesh_halo: int32 [128, 4, 64], P(('face', 'sub')), may hold values from 0 to 127
- mesh_send: int32 [128, 128, 4], P(('face', 'sub')), may hold values from 0 to 127
- mesh_slot: int32 [131072], P(('face', 'sub')), may hold values from 0 to 895, as said below
- mesh_target: int32 [131072], P(('face', 'sub')), may hold values from 0 to 127
- weights: bfloat16 [10, 512, 512], replicated, may hold values from -0.25 to 0.25
Outputs:
- mesh_update: bfloat16 [16384, 512], P(('face', 'sub'))
- grid_grad: bfloat16 [65536, 512], P(('face', 'sub'))
- mesh_grad: bfloat16 [16384, 512], P(('face', 'sub'))
- edge_grad: bfloat16 [131072, 512], P(('face', 'sub'))
- weight_grads: bfloat16 [10, 512, 512], replicated
The draws below stay inside these ranges and needn't reach their ends.
Inputs may be any that keep to these rules, and one draw needn't show every extreme that they name: grid_slot[e] names the edge device's own 512 grid rows or, above them, the 256 rows listed by each of its four neighbours in direction order. grid_target[e] is local to the edge's device. grid_send[q, k] lists local rows of device q for the device d with nb(d, k) = q; a row may appear in several slots. mesh_slot[e] names the own 128 mesh rows, then the 64 rows listed by each of the four neighbours, then 4 far rows from each device, source major. mesh_target[e] is local to the edge's device. mesh_halo[q, k] lists local rows of device q for its neighbour in direction k. mesh_send[q, d] lists local rows of device q for far edges of device d.
All inputs are finite; a program needn't handle non-finite values.
Results may differ from the reference program's by a relative error of at most 0.016.
Values may be sent and summed in bfloat16 or wider, within the bound.
No kernel may reach another device: no remote copies, remote signals or barrier semaphores. Data moves between devices by JAX's collectives and lax.ppermute only.
A program may use at most 128 MiB of HBM per device.

```python
import jax
import jax.numpy as jnp
from jax import lax

LATENT = 512
M_DEV = 128
G_DEV = 512
E1_DEV = 1024
E2_DEV = 1024
HALO_G = 256
HALO_M = 64
CAP_M = 4
PEERS = 128
GRID = 65536
MESH = 16384
E1_TOTAL = 131072
E2_TOTAL = 131072
N_FACE = 8
N_SUB = 16


def draw_grid_slot(key, part):
    count = E1_DEV * PEERS
    choose = jax.random.randint(jax.random.fold_in(key, 11), (count,), 0, 10)
    own = jax.random.randint(jax.random.fold_in(key, 12), (count,), 0, G_DEV)
    near = jax.random.randint(jax.random.fold_in(key, 13), (count,), G_DEV, G_DEV + 4 * HALO_G)
    return jnp.where(choose < 6, own, near).astype(jnp.int32)


def draw_mesh_slot(key, part):
    count = E2_DEV * PEERS
    choose = jax.random.randint(jax.random.fold_in(key, 21), (count,), 0, 6)
    own = jax.random.randint(jax.random.fold_in(key, 22), (count,), 0, M_DEV)
    near = jax.random.randint(jax.random.fold_in(key, 23), (count,), M_DEV, M_DEV + 4 * HALO_M)
    distant = jax.random.randint(jax.random.fold_in(key, 24), (count,), M_DEV + 4 * HALO_M, M_DEV + 4 * HALO_M + CAP_M * PEERS)
    return jnp.where(choose < 3, own, jnp.where(choose < 5, near, distant)).astype(jnp.int32)


def with_ends(result, key, low, high):
    place = [jax.random.randint(jax.random.fold_in(key, axis), (), 0, length) for axis, length in enumerate(result.shape)]
    widest = result.shape.index(max(result.shape))
    beside = place[:widest] + [(place[widest] + 1) % result.shape[widest]] + place[widest + 1:]
    return result.at[tuple(place)].set(low).at[tuple(beside)].set(high)


def levels(rng, shape, split, smallest, largest):
    def one(dim, parts):
        heights = jax.random.uniform(jax.random.fold_in(jax.random.fold_in(rng, 6), dim), (parts,), jnp.float32, smallest / len(split), largest / len(split))
        return jnp.repeat(jnp.exp(heights), shape[dim] // parts).reshape((-1,) + (1,) * (len(shape) - dim - 1))

    gain = one(*split[0])
    for cut in split[1:]:
        gain = gain * one(*cut)
    return gain


def centred(stream_key, dims, width, limit, split=(), held_as=jnp.bfloat16):
    factor_of = levels(stream_key, dims, split, -0.22, 0.18) if split else 1.0
    drawn = jax.random.normal(stream_key, dims, jnp.float32) * width * factor_of
    return jnp.minimum(jnp.maximum(drawn, -limit), limit).astype(held_as)


def setup_inputs(seed: int = 0) -> dict:
    splits = jax.random.split(jax.random.key(seed), 14)
    return {
        "grid_latent": centred(splits[0], (GRID, LATENT), 1.0, 6.0, ((0, 128),)),
        "mesh_latent": centred(splits[1], (MESH, LATENT), 1.0, 6.0, ((0, 128),)),
        "edge_latent": centred(splits[2], (E2_TOTAL, LATENT), 1.0, 6.0, ((0, 128),)),
        "mesh_cotangent": centred(splits[3], (MESH, LATENT), 1.0, 6.0, ((0, 128),)),
        "edge_cotangent": centred(splits[4], (E2_TOTAL, LATENT), 1.0, 6.0, ((0, 128),)),
        "grid_send": with_ends(jax.random.randint(splits[5], (PEERS, 4, HALO_G), 0, G_DEV), jax.random.fold_in(splits[5], 1), 0, G_DEV - 1).astype(jnp.int32),
        "grid_slot": draw_grid_slot(jax.random.fold_in(splits[13], 71), 0),
        "grid_target": with_ends(jax.random.randint(splits[7], (E1_TOTAL,), 0, M_DEV), jax.random.fold_in(splits[7], 1), 0, M_DEV - 1).astype(jnp.int32),
        "mesh_halo": with_ends(jax.random.randint(splits[8], (PEERS, 4, HALO_M), 0, M_DEV), jax.random.fold_in(splits[8], 1), 0, M_DEV - 1).astype(jnp.int32),
        "mesh_send": with_ends(jax.random.randint(splits[9], (PEERS, PEERS, CAP_M), 0, M_DEV), jax.random.fold_in(splits[9], 1), 0, M_DEV - 1).astype(jnp.int32),
        "mesh_slot": draw_mesh_slot(jax.random.fold_in(splits[13], 71), 0),
        "mesh_target": with_ends(jax.random.randint(splits[11], (E2_TOTAL,), 0, M_DEV), jax.random.fold_in(splits[11], 1), 0, M_DEV - 1).astype(jnp.int32),
        "weights": centred(splits[12], (10, LATENT, LATENT), LATENT ** -0.5, 0.25),
    }


norm_eps = 1e-05

def layer_norm(values):
    centre = values - lax.optimization_barrier(jnp.mean(values, axis=-1, keepdims=True))
    spread = lax.optimization_barrier(jnp.mean(centre * centre, axis=-1, keepdims=True))
    return centre * lax.rsqrt(spread + norm_eps)

def layer_norm_back(values, upstream):
    centre = values - lax.optimization_barrier(jnp.mean(values, axis=-1, keepdims=True))
    inverse = lax.rsqrt(lax.optimization_barrier(jnp.mean(centre * centre, axis=-1, keepdims=True)) + norm_eps)
    normed = centre * inverse
    return inverse * (upstream - lax.optimization_barrier(jnp.mean(upstream, axis=-1, keepdims=True)) - normed * lax.optimization_barrier(jnp.mean(upstream * normed, axis=-1, keepdims=True)))

def swish_slope(values):
    sigmoid_values = jax.nn.sigmoid(values)
    return sigmoid_values * (1.0 + values * (1.0 - sigmoid_values))

def product(former, latter):
    return jnp.dot(former, latter, preferred_element_type=jnp.float32)

def outer_sum(former, latter):
    return lax.dot_general(former, latter, (((0,), (0,)), ((), ())), preferred_element_type=jnp.float32)

def back_product(former, latter):
    return lax.dot_general(former, latter, (((1,), (1,)), ((), ())), preferred_element_type=jnp.float32)

def neighbour_device(device, block):
    face_index = device // N_SUB
    sub_index = device % N_SUB
    sub_step = jnp.where(block == 0, -1, jnp.where(block == 1, 1, 0))
    face_step = jnp.where(block == 2, -1, jnp.where(block == 3, 1, 0))
    return ((face_index + face_step) % N_FACE * N_SUB + (sub_index + sub_step) % N_SUB).astype(jnp.int32)

def slot_partials(values, slot_ids, slot_count, local_count):
    sums = jax.ops.segment_sum(values, slot_ids, num_segments=slot_count)
    rounded = lax.optimization_barrier(sums.astype(jnp.bfloat16)).astype(jnp.float32)
    keep = (jnp.arange(slot_count, dtype=jnp.int32) < local_count)[:, None]
    return jnp.where(keep, sums, rounded)

def reference(grid_latent, mesh_latent, edge_latent, mesh_cotangent, edge_cotangent, grid_send, grid_slot, grid_target, mesh_halo, mesh_send, mesh_slot, mesh_target, weights):
    peer_count = N_FACE * N_SUB
    grid_slot_count = G_DEV + 4 * HALO_G
    mesh_slot_count = M_DEV + 4 * HALO_M + CAP_M * peer_count
    device_ids = jnp.arange(peer_count, dtype=jnp.int32)
    grid_slots = grid_slot.reshape(peer_count, E1_DEV)
    grid_targets = grid_target.reshape(peer_count, E1_DEV)
    mesh_slots = mesh_slot.reshape(peer_count, E2_DEV)
    mesh_targets = mesh_target.reshape(peer_count, E2_DEV)
    edge_blocks = edge_latent.reshape(peer_count, E2_DEV, LATENT)
    edge_cots = edge_cotangent.reshape(peer_count, E2_DEV, LATENT)

    def grid_rows_of(slot_ids, device):
        halo = jnp.maximum(slot_ids - G_DEV, 0)
        block = jnp.minimum(halo // HALO_G, 3)
        source = neighbour_device(device, block)
        remote = source * G_DEV + grid_send[source, block, halo % HALO_G]
        return jnp.where(slot_ids < G_DEV, device * G_DEV + slot_ids, remote).astype(jnp.int32)

    def mesh_rows_of(slot_ids, device):
        halo = jnp.maximum(slot_ids - M_DEV, 0)
        block = jnp.minimum(halo // HALO_M, 3)
        source = neighbour_device(device, block)
        near = source * M_DEV + mesh_halo[source, block, halo % HALO_M]
        distant_slot = jnp.maximum(slot_ids - M_DEV - 4 * HALO_M, 0)
        owner = distant_slot // CAP_M
        distant = owner * M_DEV + mesh_send[owner, device, distant_slot % CAP_M]
        return jnp.where(slot_ids < M_DEV, device * M_DEV + slot_ids, jnp.where(slot_ids < M_DEV + 4 * HALO_M, near, distant)).astype(jnp.int32)
    grid_project = product(grid_latent, weights[0]).astype(jnp.bfloat16)
    encode_receive = product(mesh_latent, weights[1]).reshape(peer_count, M_DEV, LATENT)

    def encode_edges(device, slot_ids, targets, receive):
        senders = grid_rows_of(slot_ids, device)
        pre_act = jnp.take(grid_project, senders, axis=0).astype(jnp.float32) + jnp.take(receive, targets, axis=0)
        hidden = jax.nn.silu(pre_act).astype(jnp.bfloat16)
        linear = product(hidden, weights[2])
        return (pre_act, hidden, linear)

    def encode_total(inputs):
        device, slot_ids, targets, receive = inputs
        linear = encode_edges(device, slot_ids, targets, receive)[2]
        message = layer_norm(linear).astype(jnp.bfloat16)
        return jax.ops.segment_sum(message.astype(jnp.float32), targets, num_segments=M_DEV)
    encoder_total = lax.map(encode_total, (device_ids, grid_slots, grid_targets, encode_receive)).reshape(-1, LATENT)
    mesh_middle = (mesh_latent.astype(jnp.float32) + encoder_total).astype(jnp.bfloat16)
    sender_rows = product(mesh_middle, weights[4]).astype(jnp.bfloat16)
    process_receive = product(mesh_middle, weights[5]).reshape(peer_count, M_DEV, LATENT)

    def process_edges(device, slot_ids, targets, receive, edges):
        senders = mesh_rows_of(slot_ids, device)
        pre_act = product(edges, weights[3]) + jnp.take(sender_rows, senders, axis=0).astype(jnp.float32) + jnp.take(receive, targets, axis=0)
        hidden = jax.nn.silu(pre_act).astype(jnp.bfloat16)
        linear = product(hidden, weights[6])
        return (pre_act, hidden, linear)

    def process_total_block(inputs):
        device, slot_ids, targets, receive, edges = inputs
        linear = process_edges(device, slot_ids, targets, receive, edges)[2]
        update = layer_norm(linear).astype(jnp.bfloat16)
        return jax.ops.segment_sum(update.astype(jnp.float32), targets, num_segments=M_DEV)
    process_total = lax.map(process_total_block, (device_ids, mesh_slots, mesh_targets, process_receive, edge_blocks)).reshape(-1, LATENT)
    process_round = process_total.astype(jnp.bfloat16)
    update_pre = product(mesh_middle, weights[7]) + product(process_round, weights[8])
    update_hidden = jax.nn.silu(update_pre).astype(jnp.bfloat16)
    update_linear = product(update_hidden, weights[9])
    mesh_update = (mesh_middle.astype(jnp.float32) + layer_norm(update_linear)).astype(jnp.bfloat16)
    outer_cot = mesh_cotangent.astype(jnp.float32)
    cot_linear = layer_norm_back(update_linear, outer_cot).astype(jnp.bfloat16)
    grad_update_output = outer_sum(update_hidden, cot_linear)
    cot_update = (back_product(cot_linear, weights[9]) * swish_slope(update_pre)).astype(jnp.bfloat16)
    grad_update_self = outer_sum(mesh_middle, cot_update)
    grad_update_message = outer_sum(process_round, cot_update)
    cot_total = back_product(cot_update, weights[8]).reshape(peer_count, M_DEV, LATENT)
    mesh_slot_ids = jnp.arange(mesh_slot_count, dtype=jnp.int32)
    grid_slot_ids = jnp.arange(grid_slot_count, dtype=jnp.int32)

    def process_back(carry, inputs):
        grads_edge, grads_output, sender_acc = carry
        device, slot_ids, targets, receive, edges, edge_cot, total_cot = inputs
        pre_act, hidden, linear = process_edges(device, slot_ids, targets, receive, edges)
        cot_edge = jnp.take(total_cot, targets, axis=0) + edge_cot.astype(jnp.float32)
        cot_plinear = layer_norm_back(linear, cot_edge).astype(jnp.bfloat16)
        grads_output = grads_output + outer_sum(hidden, cot_plinear)
        cot_process = back_product(cot_plinear, weights[6]) * swish_slope(pre_act)
        cot_round = cot_process.astype(jnp.bfloat16)
        grads_edge = grads_edge + outer_sum(edges, cot_round)
        edge_grad_block = (edge_cot.astype(jnp.float32) + back_product(cot_round, weights[3])).astype(jnp.bfloat16)
        cot_receive = jax.ops.segment_sum(cot_process, targets, num_segments=M_DEV).astype(jnp.bfloat16)
        partials = slot_partials(cot_process, slot_ids, mesh_slot_count, M_DEV)
        sender_acc = sender_acc.at[mesh_rows_of(mesh_slot_ids, device)].add(partials)
        return ((grads_edge, grads_output, sender_acc), (edge_grad_block, cot_receive))
    zero_square = jnp.zeros((LATENT, LATENT), jnp.float32)
    start_carry = (zero_square, zero_square, jnp.zeros((M_DEV * peer_count, LATENT), jnp.float32))
    process_carry, process_outs = lax.scan(process_back, start_carry, (device_ids, mesh_slots, mesh_targets, process_receive, edge_blocks, edge_cots, cot_total))
    grad_process_edge, grad_process_output, sender_acc = process_carry
    edge_grad = process_outs[0].reshape(-1, LATENT)
    cot_receive = process_outs[1].reshape(-1, LATENT)
    cot_sender = sender_acc.astype(jnp.bfloat16)
    grad_process_receiver = outer_sum(mesh_middle, cot_receive)
    grad_process_sender = outer_sum(mesh_middle, cot_sender)
    cot_middle = outer_cot + back_product(cot_update, weights[7]) + back_product(cot_receive, weights[5]) + back_product(cot_sender, weights[4])
    cot_blocks = cot_middle.reshape(peer_count, M_DEV, LATENT)

    def encode_back(carry, inputs):
        grads_output, grid_acc = carry
        device, slot_ids, targets, receive, middle_cot = inputs
        pre_act, hidden, linear = encode_edges(device, slot_ids, targets, receive)
        cot_message = jnp.take(middle_cot, targets, axis=0)
        cot_elinear = layer_norm_back(linear, cot_message).astype(jnp.bfloat16)
        grads_output = grads_output + outer_sum(hidden, cot_elinear)
        cot_encoder = back_product(cot_elinear, weights[2]) * swish_slope(pre_act)
        cot_mesh_receive = jax.ops.segment_sum(cot_encoder, targets, num_segments=M_DEV).astype(jnp.bfloat16)
        partials = slot_partials(cot_encoder, slot_ids, grid_slot_count, G_DEV)
        grid_acc = grid_acc.at[grid_rows_of(grid_slot_ids, device)].add(partials)
        return ((grads_output, grid_acc), cot_mesh_receive)
    encode_carry, cot_mesh_receive = lax.scan(encode_back, (zero_square, jnp.zeros((G_DEV * peer_count, LATENT), jnp.float32)), (device_ids, grid_slots, grid_targets, encode_receive, cot_blocks))
    grad_encode_output, grid_acc = encode_carry
    cot_mesh_receive = cot_mesh_receive.reshape(-1, LATENT)
    grad_encode_receiver = outer_sum(mesh_latent, cot_mesh_receive)
    mesh_grad = (cot_middle + back_product(cot_mesh_receive, weights[1])).astype(jnp.bfloat16)
    cot_grid = grid_acc.astype(jnp.bfloat16)
    grad_encode_sender = outer_sum(grid_latent, cot_grid)
    grid_grad = back_product(cot_grid, weights[0]).astype(jnp.bfloat16)
    encode_scale = 1.0 / (E1_DEV * peer_count) ** 0.5
    process_scale = 1.0 / (E2_DEV * peer_count) ** 0.5
    update_scale = 1.0 / (M_DEV * peer_count) ** 0.5
    weight_grads = jnp.stack([grad_encode_sender * encode_scale, grad_encode_receiver * encode_scale, grad_encode_output * encode_scale, grad_process_edge * process_scale, grad_process_sender * process_scale, grad_process_receiver * process_scale, grad_process_output * process_scale, grad_update_self * update_scale, grad_update_message * update_scale, grad_update_output * update_scale]).astype(jnp.bfloat16)
    return (mesh_update, grid_grad, mesh_grad, edge_grad, weight_grads)
```

```python
import functools

import jax
import jax.numpy as jnp
from jax import lax
from jax.experimental import pallas as pl
from jax.experimental.pallas import tpu as pltpu
from jax.sharding import PartitionSpec as P

norm_eps = 1e-05
f32 = jnp.float32
bf16 = jnp.bfloat16
AXES = ("face", "sub")
CHUNK = 256


def shifted(value, axis, steps):
    count = lax.axis_size(axis)
    pairs = [(source, (source + steps) % count) for source in range(count)]
    return lax.ppermute(value, axis, pairs)


def outgoing_rows(blocks):
    routes = (("sub", 1), ("sub", -1), ("face", 1), ("face", -1))
    return [shifted(block, axis, step) for block, (axis, step) in zip(blocks, routes)]


def returned_rows(blocks):
    routes = (("sub", -1), ("sub", 1), ("face", -1), ("face", 1))
    return [shifted(block, axis, step) for block, (axis, step) in zip(blocks, routes)]


def dot(a, b):
    return jnp.dot(a, b, preferred_element_type=f32)


def dot_nt(a, b):
    return lax.dot_general(a, b, (((1,), (1,)), ((), ())), preferred_element_type=f32)


def dot_tn(a, b):
    return lax.dot_general(a, b, (((0,), (0,)), ((), ())), preferred_element_type=f32)


def halves(values):
    upper = values.astype(bf16)
    return upper, (values - upper.astype(f32)).astype(bf16)


def mean(values):
    return jnp.sum(values, axis=-1, keepdims=True) * (1.0 / values.shape[-1])


def norm_parts(values):
    centre = values - mean(values)
    inverse = lax.rsqrt(mean(centre * centre) + norm_eps)
    return centre * inverse, inverse


def norm_back(normed, inverse, upstream):
    return inverse * (upstream - mean(upstream) - normed * mean(upstream * normed))


def sigmoid(values):
    return 1.0 / (1.0 + jnp.exp(-values))


def silu(values):
    return values * sigmoid(values)


def slope(values):
    s = sigmoid(values)
    return s * (1.0 + values * (1.0 - s))


def pick_rows(row, offset, count):
    column = jnp.transpose(jnp.broadcast_to(row, (128, 128))) - offset
    lane = lax.broadcasted_iota(jnp.int32, (128, 128), 1)
    return jnp.concatenate(
        [jnp.where(column == lane + 128 * b, 1.0, 0.0).astype(bf16) for b in range(count // 128)],
        axis=1,
    )


def pick(ref, first, rows, offset, count):
    return jnp.concatenate(
        [pick_rows(ref[pl.ds(first + r, 1), :], offset, count) for r in range(rows)], axis=0
    )


def put(ref, first, rows, offset, count):
    place = lax.broadcasted_iota(jnp.int32, (count, 128), 0) + offset
    return jnp.concatenate(
        [
            jnp.where(place == jnp.broadcast_to(ref[pl.ds(first + r, 1), :], (count, 128)), 1.0, 0.0).astype(bf16)
            for r in range(rows)
        ],
        axis=1,
    )


def chunks(count, body):
    def step(i, carry):
        body(i, pl.ds(pl.multiple_of(i * CHUNK, CHUNK), CHUNK))
        return carry

    lax.fori_loop(0, count, step, 0)


def call(body, outs, args, weights=None, picks=(), scratch=(), flops=10**9, vmem=40 << 20, name=None):
    whole = pl.BlockSpec(memory_space=pltpu.VMEM)
    in_specs = [whole] * len(args)
    for k in picks:
        in_specs.append(
            pl.BlockSpec((None, weights.shape[1], weights.shape[2]), functools.partial(lambda k, i: (k, 0, 0), k))
        )
    shapes = [jax.ShapeDtypeStruct(s, d) for s, d in outs]
    total = sum(a.size * a.dtype.itemsize for a in args) + sum(s.size * s.dtype.itemsize for s in shapes)
    total += len(picks) * 512 * 1024
    return pl.pallas_call(
        body,
        grid=(1,),
        out_shape=shapes,
        in_specs=in_specs,
        out_specs=[whole] * len(shapes),
        scratch_shapes=list(scratch),
        compiler_params=pltpu.CompilerParams(vmem_limit_bytes=vmem),
        cost_estimate=pl.CostEstimate(flops=flops, bytes_accessed=total, transcendentals=0),
        name=name,
    )(*args, *([weights] * len(picks)))


def project_body(grid, table, w0, project, out0, out1, out2, out3):
    chunks(2, lambda i, s: project.__setitem__((s, slice(None)), dot(grid[s, :], w0[...]).astype(bf16)))
    for k, out in enumerate((out0, out1, out2, out3)):
        out[...] = dot(pick(table, 2 * k, 2, 0, 512), project[...]).astype(bf16)


def encode_own_body(project, slot, target, mesh, edge, w1, w3, own, edge_pre):
    upper, lower = halves(dot(mesh[...], w1[...]))

    def step(i, s):
        receiver = pick(target, 2 * i, 2, 0, 128)
        own[s, :] = (
            dot(pick(slot, 2 * i, 2, 0, 512), project[...]) + dot(receiver, upper) + dot(receiver, lower)
        )
        edge_pre[s, :] = dot(edge[s, :], w3[...])

    chunks(4, step)


def far_slots(slot):
    far = slot - 384
    return jnp.where(slot < 384, slot, 384 + (far & 3) * 128 + (far >> 2))


def encode_body(
    own, in0, in1, in2, in3, slot, target, mesh, halo, far, w2, w4,
    pre_out, linear_out, hidden_out, middle_out, sender_out, h0, h1, h2, h3, far_out,
    total, wide,
):
    total[...] = jnp.zeros_like(total)

    def step(i, s):
        pre = own[s, :]
        for k, block in enumerate((in0, in1, in2, in3)):
            pre = pre + dot(pick(slot, 2 * i, 2, 512 + 256 * k, 256), block[...])
        pre_out[s, :] = pre
        hidden = silu(pre).astype(bf16)
        hidden_out[s, :] = hidden
        linear = dot(hidden, w2[...])
        linear_out[s, :] = linear
        message = norm_parts(linear)[0].astype(bf16)
        total[...] += dot(put(target, 2 * i, 2, 0, 128), message)

    chunks(4, step)
    middle = (mesh[...].astype(f32) + total[...]).astype(bf16)
    middle_out[...] = middle
    sender = dot(middle, w4[...]).astype(bf16)
    sender_out[...] = sender
    rows = dot(pick(halo, 0, 2, 0, 128), sender).astype(bf16)
    for k, out in enumerate((h0, h1, h2, h3)):
        out[...] = rows[64 * k : 64 * k + 64, :]
    for r in range(4):
        picked = dot(pick(far, r, 1, 0, 128), sender)
        for c in range(4):
            wide[pl.ds(4 * c + r, 128, stride=16), :] = picked[:, 128 * c : 128 * c + 128]
    far_out[...] = wide[...].astype(bf16)


def process_own_body(middle, sender, edge_pre, slot, target, w5, w7, own, update_own):
    upper, lower = halves(dot(middle[...], w5[...]))
    update_own[...] = dot(middle[...], w7[...])

    def step(i, s):
        receiver = pick(target, 2 * i, 2, 0, 128)
        own[s, :] = (
            edge_pre[s, :] + dot(pick(slot, 2 * i, 2, 0, 128), sender[...]) + dot(receiver, upper) + dot(receiver, lower)
        )

    chunks(4, step)


def gather_far(wide, source, first):
    for r in range(4):
        for c in range(4):
            source[first + 128 * r : first + 128 * r + 128, 128 * c : 128 * c + 128] = wide[
                pl.ds(4 * c + r, 128, stride=16), :
            ].astype(bf16)


def process_body(
    own, in0, in1, in2, in3, far_in, slot, target, middle, update_own, mesh_cot, edge_cot, w6, w8, w9,
    mesh_update, hidden_out, round_out, uhidden_out, cot_linear_out, cot_update_out, plinear_out, cround_out,
    receive_out, sender_own, h0, h1, h2, h3, far_out,
    source, pre_s, normed_s, inverse_s, lower_s, total, wide, slots,
):
    slots[...] = far_slots(slot[...])
    for k, block in enumerate((in0, in1, in2, in3)):
        source[64 * k : 64 * k + 64, :] = block[...]
    wide[...] = far_in[...].astype(f32)
    gather_far(wide, source, 256)
    total[...] = jnp.zeros_like(total)

    def forward(i, s):
        pre = own[s, :] + dot(pick(slots, 2 * i, 2, 128, 768), source[...])
        pre_s[s, :] = pre
        hidden = silu(pre).astype(bf16)
        hidden_out[s, :] = hidden
        normed, inverse = norm_parts(dot(hidden, w6[...]))
        normed_s[s, :] = normed
        inverse_s[s, :] = jnp.broadcast_to(inverse, (CHUNK, 128))
        total[...] += dot(put(target, 2 * i, 2, 0, 128), normed.astype(bf16))

    chunks(4, forward)
    rounded = total[...].astype(bf16)
    round_out[...] = rounded
    pre = update_own[...] + dot(rounded, w8[...])
    uhidden = silu(pre).astype(bf16)
    uhidden_out[...] = uhidden
    normed, inverse = norm_parts(dot(uhidden, w9[...]))
    mesh_update[...] = (middle[...].astype(f32) + normed).astype(bf16)
    cot_linear = norm_back(normed, inverse, mesh_cot[...].astype(f32)).astype(bf16)
    cot_linear_out[...] = cot_linear
    cot_update = (dot_nt(cot_linear, w9[...]) * slope(pre)).astype(bf16)
    cot_update_out[...] = cot_update
    upper, lower = halves(dot_nt(cot_update, w8[...]))

    def backward(i, s):
        receiver = pick(target, 2 * i, 2, 0, 128)
        upstream = dot(receiver, upper) + dot(receiver, lower) + edge_cot[s, :].astype(f32)
        cot = norm_back(normed_s[s, :], inverse_s[s, 0:1], upstream).astype(bf16)
        plinear_out[s, :] = cot
        high, low = halves(dot_nt(cot, w6[...]) * slope(pre_s[s, :]))
        cround_out[s, :] = high
        lower_s[s, :] = low

    chunks(4, backward)
    kept = jnp.concatenate([put(target, 0, 8, 0, 128), put(slots, 0, 8, 0, 128)], axis=0)
    kept = dot(kept, cround_out[...]) + dot(kept, lower_s[...])
    receive_out[...] = kept[0:128, :].astype(bf16)
    sender_own[...] = kept[128:256, :]
    spread = put(slots, 0, 8, 128, 256)
    spread = (dot(spread, cround_out[...]) + dot(spread, lower_s[...])).astype(bf16)
    for k, out in enumerate((h0, h1, h2, h3)):
        out[...] = spread[64 * k : 64 * k + 64, :]
    for half in range(2):
        spread = put(slots, 0, 8, 384 + 256 * half, 256)
        spread = dot(spread, cround_out[...]) + dot(spread, lower_s[...])
        for q in range(2):
            for c in range(4):
                wide[pl.ds(4 * c + 2 * half + q, 128, stride=16), :] = spread[
                    128 * q : 128 * q + 128, 128 * c : 128 * c + 128
                ]
    far_out[...] = wide[...].astype(bf16)


def process_grads_body(
    scales, edge, cround, hidden, plinear, middle, receive, cot_update, rounded, uhidden, cot_linear, edge_cot, mesh_cot,
    w3, w5, w7, edge_grad, middle_part, grads,
):
    pairs = ((edge, cround), (middle, receive), (hidden, plinear), (middle, cot_update), (rounded, cot_update), (uhidden, cot_linear))
    for k, (x, y) in enumerate(pairs):
        grads[k] = (dot_tn(x[...], y[...]) * scales[k]).astype(bf16)
    middle_part[...] = mesh_cot[...].astype(f32) + dot_nt(cot_update[...], w7[...]) + dot_nt(receive[...], w5[...])

    def step(i, s):
        edge_grad[s, :] = (edge_cot[s, :].astype(f32) + dot_nt(cround[s, :], w3[...])).astype(bf16)

    chunks(4, step)


def encode_back_body(
    in0, in1, in2, in3, far_in, halo, far, sender_own, middle_part, pre, linear, slot, target, w2, w4,
    cot_sender_out, cot_middle_out, elinear_out, upper_out, lower_out, g0, g1, g2, g3,
    source, wide,
):
    for k, block in enumerate((in0, in1, in2, in3)):
        source[64 * k : 64 * k + 64, :] = block[...]
    wide[...] = far_in[...].astype(f32)
    gather_far(wide, source, 256)
    owners = jnp.concatenate([put(halo, 0, 2, 0, 128), put(far, 0, 4, 0, 128)], axis=1)
    cot_sender = (sender_own[...] + dot(owners, source[...])).astype(bf16)
    cot_sender_out[...] = cot_sender
    cot_middle = middle_part[...] + dot_nt(cot_sender, w4[...])
    cot_middle_out[...] = cot_middle
    upper, lower = halves(cot_middle)

    def step(i, s):
        receiver = pick(target, 2 * i, 2, 0, 128)
        normed, inverse = norm_parts(linear[s, :])
        cot = norm_back(normed, inverse, dot(receiver, upper) + dot(receiver, lower)).astype(bf16)
        elinear_out[s, :] = cot
        high, low = halves(dot_nt(cot, w2[...]) * slope(pre[s, :]))
        upper_out[s, :] = high
        lower_out[s, :] = low

    chunks(4, step)
    for k, out in enumerate((g0, g1, g2, g3)):
        spread = put(slot, 0, 8, 512 + 256 * k, 256)
        out[...] = (dot(spread, upper_out[...]) + dot(spread, lower_out[...])).astype(bf16)


def encode_grads_body(
    scales, upper, lower, slot, target, cot_middle, mesh, middle, cot_sender, hidden, elinear, w1,
    grid_own, mesh_grad, grads,
):
    grads[0] = (dot_tn(hidden[...], elinear[...]) * scales[1]).astype(bf16)
    grads[1] = (dot_tn(middle[...], cot_sender[...]) * scales[2]).astype(bf16)
    kept = put(target, 0, 8, 0, 128)
    receive = (dot(kept, upper[...]) + dot(kept, lower[...])).astype(bf16)
    grads[2] = (dot_tn(mesh[...], receive) * scales[0]).astype(bf16)
    mesh_grad[...] = (cot_middle[...] + dot_nt(receive, w1[...])).astype(bf16)
    for k in range(2):
        kept = put(slot, 0, 8, 256 * k, 256)
        grid_own[256 * k : 256 * k + 256, :] = dot(kept, upper[...]) + dot(kept, lower[...])


def grid_back_body(scales, grid_own, in0, in1, in2, in3, table, grid, w0, grid_grad, grads, cot):
    def step(i, s):
        total = grid_own[s, :]
        for k, block in enumerate((in0, in1, in2, in3)):
            total = total + dot(put(table, 2 * k, 2, i * CHUNK, 256), block[...])
        total = total.astype(bf16)
        cot[s, :] = total
        grid_grad[s, :] = dot_nt(total, w0[...]).astype(bf16)

    chunks(2, step)
    grads[...] = (dot_tn(grid[...], cot[...]) * scales[0]).astype(bf16)


def scaled(body, scales):
    return functools.partial(body, scales)


def on_device(
    grid_latent, mesh_latent, edge_latent, mesh_cotangent, edge_cotangent, grid_send, grid_slot, grid_target,
    mesh_halo, mesh_send, mesh_slot, mesh_target, weights,
):
    peers = lax.axis_size("face") * lax.axis_size("sub")
    mesh_rows, latent = mesh_latent.shape
    edges = grid_slot.shape[0]
    grid_scale = 1.0 / (edges * peers) ** 0.5
    edge_scale = 1.0 / (mesh_slot.shape[0] * peers) ** 0.5
    node_scale = 1.0 / (mesh_rows * peers) ** 0.5
    grid_table = grid_send.reshape(8, 128)
    halo_table = mesh_halo.reshape(2, 128)
    far_table = mesh_send[0].T
    gslot, gtarget = grid_slot.reshape(8, 128), grid_target.reshape(8, 128)
    mslot, mtarget = mesh_slot.reshape(8, 128), mesh_target.reshape(8, 128)
    big, small, halo = (edges, latent), (mesh_rows, latent), (64, latent)
    vm = pltpu.VMEM

    project, *outgoing = call(
        project_body, [((512, latent), bf16)] + [((256, latent), bf16)] * 4,
        (grid_latent, grid_table), weights, (0,), name="project",
    )
    arrived = outgoing_rows(outgoing)
    own, edge_pre = call(
        encode_own_body, [(big, f32)] * 2, (project, gslot, gtarget, mesh_latent, edge_latent),
        weights, (1, 3), flops=2 * 10**9, name="encode_own",
    )
    pre, linear, hidden, middle, sender, *halos, far_out = call(
        encode_body,
        [(big, f32), (big, f32), (big, bf16), (small, bf16), (small, bf16)] + [(halo, bf16)] * 4 + [((2048, 128), bf16)],
        (own, *arrived, gslot, gtarget, mesh_latent, halo_table, far_table), weights, (2, 4),
        scratch=(vm(small, f32), vm((2048, 128), f32)), flops=2 * 10**9, name="encode",
    )
    far_in = lax.all_to_all(far_out.reshape(peers, 16, 128), AXES, 0, 0, tiled=True).reshape(2048, 128)
    halo_in = outgoing_rows(halos)
    own, update_own = call(
        process_own_body, [(big, f32), (small, f32)], (middle, sender, edge_pre, mslot, mtarget),
        weights, (5, 7), name="process_own",
    )
    (
        mesh_update, phidden, rounded, uhidden, cot_linear, cot_update, plinear, cround, receive, sender_own,
        *halos, far_out,
    ) = call(
        process_body,
        [(small, bf16), (big, bf16)] + [(small, bf16)] * 4 + [(big, bf16)] * 2
        + [(small, bf16), (small, f32)] + [(halo, bf16)] * 4 + [((2048, 128), bf16)],
        (own, *halo_in, far_in, mslot, mtarget, middle, update_own, mesh_cotangent, edge_cotangent),
        weights, (6, 8, 9),
        scratch=(
            vm((768, latent), bf16), vm(big, f32), vm(big, f32), vm((edges, 128), f32), vm(big, bf16),
            vm(small, f32), vm((2048, 128), f32), vm((8, 128), jnp.int32),
        ),
        flops=8 * 10**9, name="process",
    )
    far_back = lax.all_to_all(far_out.reshape(peers, 16, 128), AXES, 0, 0, tiled=True).reshape(2048, 128)
    halo_back = returned_rows(halos)
    edge_grad, middle_part, process_grads = call(
        scaled(process_grads_body, [edge_scale] * 3 + [node_scale] * 3),
        [(big, bf16), (small, f32), ((6, latent, latent), bf16)],
        (edge_latent, cround, phidden, plinear, middle, receive, cot_update, rounded, uhidden, cot_linear,
         edge_cotangent, mesh_cotangent),
        weights, (3, 5, 7), flops=3 * 10**9, name="process_grads",
    )
    process_grads = lax.psum(process_grads, AXES)
    cot_sender, cot_middle, elinear, upper, lower, *partials = call(
        encode_back_body,
        [(small, bf16), (small, f32), (big, bf16), (big, bf16), (big, bf16)] + [((256, latent), bf16)] * 4,
        (*halo_back, far_back, halo_table, far_table, sender_own, middle_part, pre, linear, gslot, gtarget),
        weights, (2, 4), scratch=(vm((768, latent), bf16), vm((2048, 128), f32)), flops=4 * 10**9, name="encode_back",
    )
    partials = returned_rows(partials)
    grid_own, mesh_grad, encode_grads = call(
        scaled(encode_grads_body, [grid_scale, grid_scale, edge_scale]),
        [((512, latent), f32), (small, bf16), ((3, latent, latent), bf16)],
        (upper, lower, gslot, gtarget, cot_middle, mesh_latent, middle, cot_sender, hidden, elinear),
        weights, (1,), flops=2 * 10**9, name="encode_grads",
    )
    grid_grad, grid_wgrad = call(
        scaled(grid_back_body, [grid_scale]), [((512, latent), bf16), ((latent, latent), bf16)],
        (grid_own, *partials, grid_table, grid_latent), weights, (0,),
        scratch=(vm((512, latent), bf16),), name="grid_back",
    )
    late, process_grads = lax.optimization_barrier(
        (jnp.concatenate([grid_wgrad[None], encode_grads], axis=0), process_grads)
    )
    late = lax.psum(late, AXES)
    weight_grads = jnp.stack(
        [late[0], late[3], late[1], process_grads[0], late[2], process_grads[1], process_grads[2],
         process_grads[3], process_grads[4], process_grads[5]]
    )
    return (mesh_update, grid_grad, mesh_grad, edge_grad, weight_grads)


def solution(mesh):
    row = P(AXES, None)
    return jax.shard_map(
        on_device,
        mesh=mesh,
        in_specs=(row, row, row, row, row, P(AXES, None, None), P(AXES), P(AXES), P(AXES, None, None),
                  P(AXES, None, None), P(AXES), P(AXES), P()),
        out_specs=(row, row, row, row, P()),
        check_vma=False,
    )
```

```python
import functools

import jax
import jax.numpy as jnp
from jax import lax
from jax.experimental import pallas as pl
from jax.experimental.pallas import tpu as pltpu
from jax.sharding import PartitionSpec as P

norm_eps = 1e-05
f32 = jnp.float32
bf16 = jnp.bfloat16
AXES = ("x", "core", "y", "z")
CHIPS = ("x", "y", "z")
FACE = ("x", "core")
SUB = ("y", "z")
CHUNK = 256


def shifted(value, axis, steps):
    count = lax.axis_size(axis)
    pairs = [(source, (source + steps) % count) for source in range(count)]
    return lax.ppermute(value, axis, pairs)


def outgoing_rows(blocks):
    routes = ((SUB, 1), (SUB, -1), (FACE, 1), (FACE, -1))
    return [shifted(block, axis, step) for block, (axis, step) in zip(blocks, routes)]


def returned_rows(blocks):
    routes = ((SUB, -1), (SUB, 1), (FACE, -1), (FACE, 1))
    return [shifted(block, axis, step) for block, (axis, step) in zip(blocks, routes)]


def dot(a, b):
    return jnp.dot(a, b, preferred_element_type=f32)


def dot_nt(a, b):
    return lax.dot_general(a, b, (((1,), (1,)), ((), ())), preferred_element_type=f32)


def dot_tn(a, b):
    return lax.dot_general(a, b, (((0,), (0,)), ((), ())), preferred_element_type=f32)


def halves(values):
    upper = values.astype(bf16)
    return upper, (values - upper.astype(f32)).astype(bf16)


def mean(values):
    return jnp.sum(values, axis=-1, keepdims=True) * (1.0 / values.shape[-1])


def norm_parts(values):
    centre = values - mean(values)
    inverse = lax.rsqrt(mean(centre * centre) + norm_eps)
    return centre * inverse, inverse


def norm_back(normed, inverse, upstream):
    return inverse * (upstream - mean(upstream) - normed * mean(upstream * normed))


def sigmoid(values):
    return 1.0 / (1.0 + jnp.exp(-values))


def silu(values):
    return values * sigmoid(values)


def slope(values):
    s = sigmoid(values)
    return s * (1.0 + values * (1.0 - s))


def pick_rows(row, offset, count):
    column = jnp.transpose(jnp.broadcast_to(row, (128, 128))) - offset
    lane = lax.broadcasted_iota(jnp.int32, (128, 128), 1)
    return jnp.concatenate(
        [jnp.where(column == lane + 128 * b, 1.0, 0.0).astype(bf16) for b in range(count // 128)],
        axis=1,
    )


def pick(ref, first, rows, offset, count):
    return jnp.concatenate(
        [pick_rows(ref[pl.ds(first + r, 1), :], offset, count) for r in range(rows)], axis=0
    )


def put(ref, first, rows, offset, count):
    place = lax.broadcasted_iota(jnp.int32, (count, 128), 0) + offset
    return jnp.concatenate(
        [
            jnp.where(place == jnp.broadcast_to(ref[pl.ds(first + r, 1), :], (count, 128)), 1.0, 0.0).astype(bf16)
            for r in range(rows)
        ],
        axis=1,
    )


def chunks(count, body):
    def step(i, carry):
        body(i, pl.ds(pl.multiple_of(i * CHUNK, CHUNK), CHUNK))
        return carry

    lax.fori_loop(0, count, step, 0)


def call(body, outs, args, weights=None, picks=(), scratch=(), flops=10**9, vmem=67000000, name=None):
    def whole(shape):
        return pl.BlockSpec(shape, lambda i: (0,) * len(shape))

    in_specs = [whole(a.shape) for a in args]
    for k in picks:
        in_specs.append(
            pl.BlockSpec((None, weights.shape[1], weights.shape[2]), functools.partial(lambda k, i: (k, 0, 0), k))
        )
    shapes = [jax.ShapeDtypeStruct(s, d) for s, d in outs]
    total = sum(a.size * a.dtype.itemsize for a in args) + sum(s.size * s.dtype.itemsize for s in shapes)
    total += len(picks) * 512 * 1024
    return pl.pallas_call(
        body,
        grid=(1,),
        out_shape=shapes,
        in_specs=in_specs,
        out_specs=[whole(s.shape) for s in shapes],
        scratch_shapes=list(scratch),
        compiler_params=pltpu.CompilerParams(vmem_limit_bytes=vmem),
        cost_estimate=pl.CostEstimate(flops=flops, bytes_accessed=total, transcendentals=0),
        name=name,
    )(*args, *([weights] * len(picks)))


def project_body(grid, table, w0, project, out0, out1, out2, out3):
    chunks(2, lambda i, s: project.__setitem__((s, slice(None)), dot(grid[s, :], w0[...]).astype(bf16)))
    for k, out in enumerate((out0, out1, out2, out3)):
        out[...] = dot(pick(table, 2 * k, 2, 0, 512), project[...]).astype(bf16)


def encode_own_body(project, slot, target, mesh, w1, own):
    upper, lower = halves(dot(mesh[...], w1[...]))

    def step(i, s):
        receiver = pick(target, 2 * i, 2, 0, 128)
        own[s, :] = (
            dot(pick(slot, 2 * i, 2, 0, 512), project[...]) + dot(receiver, upper) + dot(receiver, lower)
        )

    chunks(4, step)


def far_slots(slot):
    far = slot - 384
    return jnp.where(slot < 384, slot, 384 + (far & 3) * 128 + (far >> 2))


def encode_body(
    own, in0, in1, in2, in3, slot, target, mesh, halo, far, w2, w4,
    pre_out, linear_out, hidden_out, middle_out, sender_out, h0, h1, h2, h3, far_out,
    total, wide,
):
    total[...] = jnp.zeros_like(total)

    def step(i, s):
        pre = own[s, :]
        for k, block in enumerate((in0, in1, in2, in3)):
            pre = pre + dot(pick(slot, 2 * i, 2, 512 + 256 * k, 256), block[...])
        pre_out[s, :] = pre
        hidden = silu(pre).astype(bf16)
        hidden_out[s, :] = hidden
        linear = dot(hidden, w2[...])
        linear_out[s, :] = linear
        message = norm_parts(linear)[0].astype(bf16)
        total[...] += dot(put(target, 2 * i, 2, 0, 128), message)

    chunks(4, step)
    middle = (mesh[...].astype(f32) + total[...]).astype(bf16)
    middle_out[...] = middle
    sender = dot(middle, w4[...]).astype(bf16)
    sender_out[...] = sender
    rows = dot(pick(halo, 0, 2, 0, 128), sender).astype(bf16)
    for k, out in enumerate((h0, h1, h2, h3)):
        out[...] = rows[64 * k : 64 * k + 64, :]
    for r in range(4):
        picked = dot(pick(far, r, 1, 0, 128), sender)
        for c in range(4):
            wide[pl.ds(4 * c + r, 128, stride=16), :] = picked[:, 128 * c : 128 * c + 128]
    far_out[...] = wide[...].astype(bf16)


def process_own_body(middle, sender, edge, slot, target, w3, w5, w7, own, update_own):
    upper, lower = halves(dot(middle[...], w5[...]))
    update_own[...] = dot(middle[...], w7[...])

    def step(i, s):
        receiver = pick(target, 2 * i, 2, 0, 128)
        own[s, :] = (
            dot(edge[s, :], w3[...]) + dot(pick(slot, 2 * i, 2, 0, 128), sender[...]) + dot(receiver, upper) + dot(receiver, lower)
        )

    chunks(4, step)


def gather_far(wide, source, first):
    for r in range(4):
        for c in range(4):
            source[first + 128 * r : first + 128 * r + 128, 128 * c : 128 * c + 128] = wide[
                pl.ds(4 * c + r, 128, stride=16), :
            ].astype(bf16)


def process_body(
    own, in0, in1, in2, in3, far_in, slot, target, middle, update_own, mesh_cot, edge_cot, w6, w8, w9,
    mesh_update, hidden_out, round_out, uhidden_out, cot_linear_out, cot_update_out, plinear_out, cround_out,
    receive_out, sender_own, h0, h1, h2, h3, far_out,
    source, pre_s, normed_s, inverse_s, lower_s, total, wide, slots,
):
    slots[...] = far_slots(slot[...])
    for k, block in enumerate((in0, in1, in2, in3)):
        source[64 * k : 64 * k + 64, :] = block[...]
    wide[...] = far_in[...].astype(f32)
    gather_far(wide, source, 256)
    total[...] = jnp.zeros_like(total)

    def forward(i, s):
        pre = own[s, :] + dot(pick(slots, 2 * i, 2, 128, 768), source[...])
        pre_s[s, :] = pre
        hidden = silu(pre).astype(bf16)
        hidden_out[s, :] = hidden
        normed, inverse = norm_parts(dot(hidden, w6[...]))
        normed_s[s, :] = normed
        inverse_s[s, :] = jnp.broadcast_to(inverse, (CHUNK, 128))
        total[...] += dot(put(target, 2 * i, 2, 0, 128), normed.astype(bf16))

    chunks(4, forward)
    rounded = total[...].astype(bf16)
    round_out[...] = rounded
    pre = update_own[...] + dot(rounded, w8[...])
    uhidden = silu(pre).astype(bf16)
    uhidden_out[...] = uhidden
    normed, inverse = norm_parts(dot(uhidden, w9[...]))
    mesh_update[...] = (middle[...].astype(f32) + normed).astype(bf16)
    cot_linear = norm_back(normed, inverse, mesh_cot[...].astype(f32)).astype(bf16)
    cot_linear_out[...] = cot_linear
    cot_update = (dot_nt(cot_linear, w9[...]) * slope(pre)).astype(bf16)
    cot_update_out[...] = cot_update
    upper, lower = halves(dot_nt(cot_update, w8[...]))

    def backward(i, s):
        receiver = pick(target, 2 * i, 2, 0, 128)
        upstream = dot(receiver, upper) + dot(receiver, lower) + edge_cot[s, :].astype(f32)
        cot = norm_back(normed_s[s, :], inverse_s[s, 0:1], upstream).astype(bf16)
        plinear_out[s, :] = cot
        high, low = halves(dot_nt(cot, w6[...]) * slope(pre_s[s, :]))
        cround_out[s, :] = high
        lower_s[s, :] = low

    chunks(4, backward)
    kept = jnp.concatenate([put(target, 0, 8, 0, 128), put(slots, 0, 8, 0, 128)], axis=0)
    kept = dot(kept, cround_out[...]) + dot(kept, lower_s[...])
    receive_out[...] = kept[0:128, :].astype(bf16)
    sender_own[...] = kept[128:256, :]
    spread = put(slots, 0, 8, 128, 256)
    spread = (dot(spread, cround_out[...]) + dot(spread, lower_s[...])).astype(bf16)
    for k, out in enumerate((h0, h1, h2, h3)):
        out[...] = spread[64 * k : 64 * k + 64, :]
    for half in range(2):
        spread = put(slots, 0, 8, 384 + 256 * half, 256)
        spread = dot(spread, cround_out[...]) + dot(spread, lower_s[...])
        for q in range(2):
            for c in range(4):
                wide[pl.ds(4 * c + 2 * half + q, 128, stride=16), :] = spread[
                    128 * q : 128 * q + 128, 128 * c : 128 * c + 128
                ]
    far_out[...] = wide[...].astype(bf16)


def store_blocks(out, k, term):
    rows = term.astype(bf16).reshape(4, 8, 16, 512)
    for c in range(2):
        for q in range(2):
            first = 128 * (2 * c + q)
            out[:, c, :, q, k, :, :] = rows[:, :, :, first : first + 128]


def process_grads_body(
    scales, edge, cround, hidden, plinear, middle, receive, cot_update, rounded, uhidden, cot_linear, edge_cot, mesh_cot,
    w3, w5, w7, edge_grad, middle_part, grads,
):
    pairs = ((edge, cround), (middle, receive), (hidden, plinear), (middle, cot_update), (rounded, cot_update), (uhidden, cot_linear))
    for k, (x, y) in enumerate(pairs):
        store_blocks(grads, k, dot_tn(x[...], y[...]) * scales[k])
    middle_part[...] = mesh_cot[...].astype(f32) + dot_nt(cot_update[...], w7[...]) + dot_nt(receive[...], w5[...])

    def step(i, s):
        edge_grad[s, :] = (edge_cot[s, :].astype(f32) + dot_nt(cround[s, :], w3[...])).astype(bf16)

    chunks(4, step)


def encode_back_body(
    in0, in1, in2, in3, far_in, halo, far, sender_own, middle_part, pre, linear, slot, target, w2, w4,
    cot_sender_out, cot_middle_out, elinear_out, upper_out, lower_out, g0, g1, g2, g3,
    source, wide,
):
    for k, block in enumerate((in0, in1, in2, in3)):
        source[64 * k : 64 * k + 64, :] = block[...]
    wide[...] = far_in[...].astype(f32)
    gather_far(wide, source, 256)
    owners = jnp.concatenate([put(halo, 0, 2, 0, 128), put(far, 0, 4, 0, 128)], axis=1)
    cot_sender = (sender_own[...] + dot(owners, source[...])).astype(bf16)
    cot_sender_out[...] = cot_sender
    cot_middle = middle_part[...] + dot_nt(cot_sender, w4[...])
    cot_middle_out[...] = cot_middle
    upper, lower = halves(cot_middle)

    def step(i, s):
        receiver = pick(target, 2 * i, 2, 0, 128)
        normed, inverse = norm_parts(linear[s, :])
        cot = norm_back(normed, inverse, dot(receiver, upper) + dot(receiver, lower)).astype(bf16)
        elinear_out[s, :] = cot
        high, low = halves(dot_nt(cot, w2[...]) * slope(pre[s, :]))
        upper_out[s, :] = high
        lower_out[s, :] = low

    chunks(4, step)
    for k, out in enumerate((g0, g1, g2, g3)):
        spread = put(slot, 0, 8, 512 + 256 * k, 256)
        out[...] = (dot(spread, upper_out[...]) + dot(spread, lower_out[...])).astype(bf16)


def encode_grads_body(
    scales, upper, lower, slot, target, cot_middle, mesh, middle, cot_sender, hidden, elinear, w1,
    grid_own, mesh_grad, grads,
):
    grads[1] = (dot_tn(hidden[...], elinear[...]) * scales[1]).astype(bf16)
    grads[2] = (dot_tn(middle[...], cot_sender[...]) * scales[2]).astype(bf16)
    kept = put(target, 0, 8, 0, 128)
    receive = (dot(kept, upper[...]) + dot(kept, lower[...])).astype(bf16)
    grads[0] = (dot_tn(mesh[...], receive) * scales[0]).astype(bf16)
    mesh_grad[...] = (cot_middle[...] + dot_nt(receive, w1[...])).astype(bf16)
    for k in range(2):
        kept = put(slot, 0, 8, 256 * k, 256)
        grid_own[256 * k : 256 * k + 256, :] = dot(kept, upper[...]) + dot(kept, lower[...])


def grid_back_body(scales, grid_own, in0, in1, in2, in3, table, grid, others, w0, grid_grad, grads, cot):
    def step(i, s):
        total = grid_own[s, :]
        for k, block in enumerate((in0, in1, in2, in3)):
            total = total + dot(put(table, 2 * k, 2, i * CHUNK, 256), block[...])
        total = total.astype(bf16)
        cot[s, :] = total
        grid_grad[s, :] = dot_nt(total, w0[...]).astype(bf16)

    chunks(2, step)
    store_blocks(grads, 0, dot_tn(grid[...], cot[...]) * scales[0])
    for k in range(3):
        store_blocks(grads, k + 1, others[k])


def sum_body(terms, shard):
    total = terms[0].astype(f32)
    for d in range(1, terms.shape[0]):
        total = total + terms[d].astype(f32)
    total = total.astype(bf16)
    for p in range(shard.shape[0]):
        shard[p] = total


def assemble_body(order, core, *refs):
    out = refs[-1]
    first = core[0] == 0
    place = 0
    for own, other in (refs[0:2], refs[2:4]):
        for k in range(own.shape[2]):
            for q in range(2):
                a, b = own[:, q, k].reshape(512, 128), other[:, q, k].reshape(512, 128)
                out[order[place], :, 128 * q : 128 * q + 128] = jnp.where(first, a, b)
                out[order[place], :, 256 + 128 * q : 384 + 128 * q] = jnp.where(first, b, a)
            place += 1


def summed_blocks(terms, name):
    count = terms.shape[4]
    with jax.named_scope(name):
        terms = lax.all_to_all(terms.reshape(128, count * 16, 128), AXES, 0, 0, tiled=True)
    (shard,) = call(
        sum_body, [((64, count * 16, 128), bf16)], (terms,), flops=10**7, name=name + "_sum",
    )
    with jax.named_scope(name + "_spread"):
        own = lax.all_to_all(shard, CHIPS, 0, 0, tiled=True)
    with jax.named_scope(name + "_pair"):
        other = lax.ppermute(own, "core", [(0, 1), (1, 0)])
    shape = (32, 2, count, 16, 128)
    return own.reshape(shape), other.reshape(shape)


def scaled(body, scales):
    return functools.partial(body, scales)


def on_device(
    grid_latent, mesh_latent, edge_latent, mesh_cotangent, edge_cotangent, grid_send, grid_slot, grid_target,
    mesh_halo, mesh_send, mesh_slot, mesh_target, weights,
):
    peers = lax.axis_size(AXES)
    mesh_rows, latent = mesh_latent.shape
    edges = grid_slot.shape[0]
    grid_scale = 1.0 / (edges * peers) ** 0.5
    edge_scale = 1.0 / (mesh_slot.shape[0] * peers) ** 0.5
    node_scale = 1.0 / (mesh_rows * peers) ** 0.5
    grid_table = grid_send.reshape(8, 128)
    halo_table = mesh_halo.reshape(2, 128)
    far_table = mesh_send[0].T
    gslot, gtarget = grid_slot.reshape(8, 128), grid_target.reshape(8, 128)
    mslot, mtarget = mesh_slot.reshape(8, 128), mesh_target.reshape(8, 128)
    big, small, halo = (edges, latent), (mesh_rows, latent), (64, latent)
    block = (4, 2, 8, 2)
    vm = pltpu.VMEM

    project, *outgoing = call(
        project_body, [((512, latent), bf16)] + [((256, latent), bf16)] * 4,
        (grid_latent, grid_table), weights, (0,), name="project",
    )
    arrived = outgoing_rows(outgoing)
    (own,) = call(
        encode_own_body, [(big, f32)], (project, gslot, gtarget, mesh_latent),
        weights, (1,), flops=10**9, name="encode_own",
    )
    pre, linear, hidden, middle, sender, *halos, far_out = call(
        encode_body,
        [(big, f32), (big, f32), (big, bf16), (small, bf16), (small, bf16)] + [(halo, bf16)] * 4 + [((2048, 128), bf16)],
        (own, *arrived, gslot, gtarget, mesh_latent, halo_table, far_table), weights, (2, 4),
        scratch=(vm(small, f32), vm((2048, 128), f32)), flops=2 * 10**9, name="encode",
    )
    far_in = lax.all_to_all(far_out.reshape(peers, 16, 128), AXES, 0, 0, tiled=True).reshape(2048, 128)
    halo_in = outgoing_rows(halos)
    own, update_own = call(
        process_own_body, [(big, f32), (small, f32)], (middle, sender, edge_latent, mslot, mtarget),
        weights, (3, 5, 7), name="process_own",
    )
    (
        mesh_update, phidden, rounded, uhidden, cot_linear, cot_update, plinear, cround, receive, sender_own,
        *halos, far_out,
    ) = call(
        process_body,
        [(small, bf16), (big, bf16)] + [(small, bf16)] * 4 + [(big, bf16)] * 2
        + [(small, bf16), (small, f32)] + [(halo, bf16)] * 4 + [((2048, 128), bf16)],
        (own, *halo_in, far_in, mslot, mtarget, middle, update_own, mesh_cotangent, edge_cotangent),
        weights, (6, 8, 9),
        scratch=(
            vm((768, latent), bf16), vm(big, f32), vm(big, f32), vm((edges, 128), f32), vm(big, bf16),
            vm(small, f32), vm((2048, 128), f32), vm((8, 128), jnp.int32),
        ),
        flops=8 * 10**9, name="process",
    )
    far_back = lax.all_to_all(far_out.reshape(peers, 16, 128), AXES, 0, 0, tiled=True).reshape(2048, 128)
    halo_back = returned_rows(halos)
    edge_grad, middle_part, process_grads = call(
        scaled(process_grads_body, [edge_scale] * 3 + [node_scale] * 3),
        [(big, bf16), (small, f32), (block + (6, 16, 128), bf16)],
        (edge_latent, cround, phidden, plinear, middle, receive, cot_update, rounded, uhidden, cot_linear,
         edge_cotangent, mesh_cotangent),
        weights, (3, 5, 7), flops=3 * 10**9, name="process_grads",
    )
    early = summed_blocks(process_grads, "early")
    cot_sender, cot_middle, elinear, upper, lower, *partials = call(
        encode_back_body,
        [(small, bf16), (small, f32), (big, bf16), (big, bf16), (big, bf16)] + [((256, latent), bf16)] * 4,
        (*halo_back, far_back, halo_table, far_table, sender_own, middle_part, pre, linear, gslot, gtarget),
        weights, (2, 4), scratch=(vm((768, latent), bf16), vm((2048, 128), f32)), flops=4 * 10**9, name="encode_back",
    )
    partials = returned_rows(partials)
    grid_own, mesh_grad, encode_grads = call(
        scaled(encode_grads_body, [grid_scale, grid_scale, edge_scale]),
        [((512, latent), f32), (small, bf16), ((3, latent, latent), bf16)],
        (upper, lower, gslot, gtarget, cot_middle, mesh_latent, middle, cot_sender, hidden, elinear),
        weights, (1,), flops=2 * 10**9, name="encode_grads",
    )
    grid_grad, grid_wgrad = call(
        scaled(grid_back_body, [grid_scale]), [((512, latent), bf16), (block + (4, 16, 128), bf16)],
        (grid_own, *partials, grid_table, grid_latent, encode_grads), weights, (0,),
        scratch=(vm((512, latent), bf16),), name="grid_back",
    )
    late = summed_blocks(grid_wgrad, "late")
    core = lax.axis_index("core").reshape(1)
    order = (3, 5, 6, 7, 8, 9, 0, 1, 2, 4)
    weight_grads = pl.pallas_call(
        functools.partial(assemble_body, order),
        grid_spec=pltpu.PrefetchScalarGridSpec(
            num_scalar_prefetch=1,
            grid=(1,),
            in_specs=[pl.BlockSpec(a.shape, lambda i, c: (0,) * 5) for a in (*early, *late)],
            out_specs=pl.BlockSpec(weights.shape, lambda i, c: (0, 0, 0)),
        ),
        out_shape=jax.ShapeDtypeStruct(weights.shape, bf16),
        compiler_params=pltpu.CompilerParams(vmem_limit_bytes=67000000),
        name="assemble",
    )(core, *early, *late)
    return (mesh_update, grid_grad, mesh_grad, edge_grad, weight_grads)


def solution(mesh):
    row = P(AXES, None)
    wide = jax.sharding.Mesh(mesh.devices.reshape(4, 2, 4, 4), AXES)
    return jax.shard_map(
        on_device,
        mesh=wide,
        in_specs=(row, row, row, row, row, P(AXES, None, None), P(AXES), P(AXES), P(AXES, None, None),
                  P(AXES, None, None), P(AXES), P(AXES), P()),
        out_specs=(row, row, row, row, P()),
        check_vma=False,
    )
```

```python
import functools

import jax
import jax.numpy as jnp
from jax import lax
from jax.experimental import pallas as pl
from jax.experimental.pallas import tpu as pltpu
from jax.sharding import PartitionSpec as P


norm_eps = 1e-05
f32 = jnp.float32
bf16 = jnp.bfloat16
AXES = ("x", "core", "y", "z")
CHIPS = ("x", "y", "z")
FACE = ("x", "core")
SUB = ("y", "z")
CHUNK = 256


def shifted(value, axis, steps):
    count = lax.axis_size(axis)
    pairs = [(source, (source + steps) % count) for source in range(count)]
    return lax.ppermute(value, axis, pairs)


def outgoing_rows(blocks):
    routes = ((SUB, 1), (SUB, -1), (FACE, 1), (FACE, -1))
    return [shifted(block, axis, step) for block, (axis, step) in zip(blocks, routes)]


def returned_rows(blocks):
    routes = ((SUB, -1), (SUB, 1), (FACE, -1), (FACE, 1))
    return [shifted(block, axis, step) for block, (axis, step) in zip(blocks, routes)]


def dot(a, b):
    return jnp.dot(a, b, preferred_element_type=f32)


def dot_nt(a, b):
    return lax.dot_general(a, b, (((1,), (1,)), ((), ())), preferred_element_type=f32)


def dot_tn(a, b):
    return lax.dot_general(a, b, (((0,), (0,)), ((), ())), preferred_element_type=f32)


def halves(values):
    upper = values.astype(bf16)
    return upper, (values - upper.astype(f32)).astype(bf16)


def mean(values):
    return jnp.sum(values, axis=-1, keepdims=True) * (1.0 / values.shape[-1])


def norm_parts(values):
    centre = values - mean(values)
    inverse = lax.rsqrt(mean(centre * centre) + norm_eps)
    return centre * inverse, inverse


def norm_back(normed, inverse, upstream):
    return inverse * (upstream - mean(upstream) - normed * mean(upstream * normed))


def sigmoid(values):
    return 1.0 / (1.0 + jnp.exp(-values))


def silu(values):
    return values * sigmoid(values)


def slope(values):
    s = sigmoid(values)
    return s * (1.0 + values * (1.0 - s))


def pick_rows(row, offset, count):
    column = jnp.transpose(jnp.broadcast_to(row, (128, 128))) - offset
    lane = lax.broadcasted_iota(jnp.int32, (128, 128), 1)
    return jnp.concatenate(
        [jnp.where(column == lane + 128 * b, 1.0, 0.0).astype(bf16) for b in range(count // 128)],
        axis=1,
    )


def pick(ref, first, rows, offset, count):
    return jnp.concatenate(
        [pick_rows(ref[pl.ds(first + r, 1), :], offset, count) for r in range(rows)], axis=0
    )


def put(ref, first, rows, offset, count):
    return put_rows([ref[pl.ds(first + r, 1), :] for r in range(rows)], offset, count)


def table_rows(table, k):
    return [table[0, k : k + 1, 128 * h : 128 * h + 128] for h in range(2)]


def put_rows(rows, offset, count):
    place = lax.broadcasted_iota(jnp.int32, (count, 128), 0) + offset
    return jnp.concatenate(
        [jnp.where(place == jnp.broadcast_to(row, (count, 128)), 1.0, 0.0).astype(bf16) for row in rows], axis=1
    )


def stack_halves(values):
    return jnp.concatenate(halves(values), axis=0)


def twice(values):
    return jnp.concatenate([values, values], axis=1)


def chunks(count, body):
    def step(i, carry):
        body(i, pl.ds(pl.multiple_of(i * CHUNK, CHUNK), CHUNK))
        return carry

    lax.fori_loop(0, count, step, 0)


def call(body, outs, args, weights=None, picks=(), scratch=(), flops=10**9, vmem=67000000):
    def whole(shape):
        return pl.BlockSpec(shape, lambda i: (0,) * len(shape))

    in_specs = [pl.BlockSpec(memory_space=pltpu.SMEM) if a.shape == (1,) else whole(a.shape) for a in args]
    for k in picks:
        in_specs.append(
            pl.BlockSpec((None, weights.shape[1], weights.shape[2]), functools.partial(lambda k, i: (k, 0, 0), k))
        )
    shapes = [jax.ShapeDtypeStruct(s, d) for s, d in outs]
    total = sum(a.size * a.dtype.itemsize for a in args) + sum(s.size * s.dtype.itemsize for s in shapes)
    total += len(picks) * 512 * 1024
    return pl.pallas_call(
        body,
        grid=(1,),
        out_shape=shapes,
        in_specs=in_specs,
        out_specs=[whole(s.shape) for s in shapes],
        scratch_shapes=list(scratch),
        compiler_params=pltpu.CompilerParams(vmem_limit_bytes=vmem),
        cost_estimate=pl.CostEstimate(flops=flops, bytes_accessed=total, transcendentals=0),
    )(*args, *([weights] * len(picks)))


def project_body(grid, table, w0, project, out0, out1, out2, out3):
    chunks(2, lambda i, s: project.__setitem__((s, slice(None)), dot(grid[s, :], w0[...]).astype(bf16)))
    for k, out in enumerate((out0, out1, out2, out3)):
        picked = jnp.concatenate([pick_rows(row, 0, 512) for row in table_rows(table, k)], axis=0)
        out[...] = dot(picked, project[...]).astype(bf16)


def encode_own_body(project, slot, target, mesh, w1, own, source):
    source[0:512, :] = project[...]
    source[512:768, :] = stack_halves(dot(mesh[...], w1[...]))

    def step(i, s):
        receiver = pick(target, 2 * i, 2, 0, 128)
        own[s, :] = dot(jnp.concatenate([pick(slot, 2 * i, 2, 0, 512), twice(receiver)], axis=1), source[...])

    chunks(4, step)


def far_slots(slot):
    far = slot - 384
    return jnp.where(slot < 384, slot, 384 + (far & 3) * 128 + (far >> 2))


def encode_body(
    own, in0, in1, in2, in3, slot, target, mesh, halo, far, w2, w4,
    pre_out, linear_out, hidden_out, middle_out, sender_out, h0, h1, h2, h3, far_out,
    total, wide,
):
    total[...] = jnp.zeros_like(total)

    def step(i, s):
        pre = own[s, :]
        for k, block in enumerate((in0, in1, in2, in3)):
            pre = pre + dot(pick(slot, 2 * i, 2, 512 + 256 * k, 256), block[...])
        pre_out[s, :] = pre
        hidden = silu(pre).astype(bf16)
        hidden_out[s, :] = hidden
        linear = dot(hidden, w2[...])
        linear_out[s, :] = linear
        message = norm_parts(linear)[0].astype(bf16)
        total[...] += dot(put(target, 2 * i, 2, 0, 128), message)

    chunks(4, step)
    middle = (mesh[...].astype(f32) + total[...]).astype(bf16)
    middle_out[...] = middle
    sender = dot(middle, w4[...]).astype(bf16)
    sender_out[...] = sender
    rows = dot(pick(halo, 0, 2, 0, 128), sender).astype(bf16)
    for k, out in enumerate((h0, h1, h2, h3)):
        out[...] = rows[64 * k : 64 * k + 64, :]
    for r in range(4):
        picked = dot(pick(far, r, 1, 0, 128), sender)
        for c in range(4):
            wide[pl.ds(4 * c + r, 128, stride=16), :] = picked[:, 128 * c : 128 * c + 128]
    far_out[...] = wide[...].astype(bf16)


def process_own_body(middle, sender, edge, slot, target, w3, w5, w7, own, update_own, source):
    source[0:128, :] = sender[...]
    source[128:384, :] = stack_halves(dot(middle[...], w5[...]))
    update_own[...] = dot(middle[...], w7[...])

    def step(i, s):
        receiver = pick(target, 2 * i, 2, 0, 128)
        picked = jnp.concatenate([pick(slot, 2 * i, 2, 0, 128), twice(receiver)], axis=1)
        own[s, :] = dot(edge[s, :], w3[...]) + dot(picked, source[...])

    chunks(4, step)


def gather_far(wide, source, first):
    for r in range(4):
        for c in range(4):
            source[first + 128 * r : first + 128 * r + 128, 128 * c : 128 * c + 128] = wide[
                pl.ds(4 * c + r, 128, stride=16), :
            ].astype(bf16)


def process_body(
    own, in0, in1, in2, in3, far_in, slot, target, middle, update_own, mesh_cot, edge_cot, w6, w8, w9,
    mesh_update, hidden_out, round_out, uhidden_out, cot_linear_out, cot_update_out, plinear_out, cround_out,
    receive_out, sender_own, h0, h1, h2, h3, far_out,
    source, pre_s, normed_s, inverse_s, total, wide, slots,
):
    slots[...] = far_slots(slot[...])
    for k, block in enumerate((in0, in1, in2, in3)):
        source[64 * k : 64 * k + 64, :] = block[...]
    wide[...] = far_in[...].astype(f32)
    gather_far(wide, source, 256)
    total[...] = jnp.zeros_like(total)

    def forward(i, s):
        pre = own[s, :] + dot(pick(slots, 2 * i, 2, 128, 768), source[...])
        pre_s[s, :] = pre
        hidden = silu(pre).astype(bf16)
        hidden_out[s, :] = hidden
        normed, inverse = norm_parts(dot(hidden, w6[...]))
        normed_s[s, :] = normed
        inverse_s[s, :] = jnp.broadcast_to(inverse, (CHUNK, 128))
        total[...] += dot(put(target, 2 * i, 2, 0, 128), normed.astype(bf16))

    chunks(4, forward)
    rounded = total[...].astype(bf16)
    round_out[...] = rounded
    pre = update_own[...] + dot(rounded, w8[...])
    uhidden = silu(pre).astype(bf16)
    uhidden_out[...] = uhidden
    normed, inverse = norm_parts(dot(uhidden, w9[...]))
    mesh_update[...] = (middle[...].astype(f32) + normed).astype(bf16)
    cot_linear = norm_back(normed, inverse, mesh_cot[...].astype(f32)).astype(bf16)
    cot_linear_out[...] = cot_linear
    cot_update = (dot_nt(cot_linear, w9[...]) * slope(pre)).astype(bf16)
    cot_update_out[...] = cot_update
    cot_total = stack_halves(dot_nt(cot_update, w8[...]))

    def backward(i, s):
        receiver = pick(target, 2 * i, 2, 0, 128)
        upstream = dot(twice(receiver), cot_total) + edge_cot[s, :].astype(f32)
        cot = norm_back(normed_s[s, :], inverse_s[s, 0:1], upstream).astype(bf16)
        plinear_out[s, :] = cot
        cround_out[s, :] = (dot_nt(cot, w6[...]) * slope(pre_s[s, :])).astype(bf16)

    chunks(4, backward)
    kept = jnp.concatenate([put(target, 0, 8, 0, 128), put(slots, 0, 8, 0, 128)], axis=0)
    kept = dot(kept, cround_out[...])
    receive_out[...] = kept[0:128, :].astype(bf16)
    sender_own[...] = kept[128:256, :]
    spread = put(slots, 0, 8, 128, 256)
    spread = dot(spread, cround_out[...]).astype(bf16)
    for k, out in enumerate((h0, h1, h2, h3)):
        out[...] = spread[64 * k : 64 * k + 64, :]
    for half in range(2):
        spread = put(slots, 0, 8, 384 + 256 * half, 256)
        spread = dot(spread, cround_out[...])
        for q in range(2):
            for c in range(4):
                wide[pl.ds(4 * c + 2 * half + q, 128, stride=16), :] = spread[
                    128 * q : 128 * q + 128, 128 * c : 128 * c + 128
                ]
    far_out[...] = wide[...].astype(bf16)


def store_blocks(own, other, k, term, held, core):
    held[...] = term.astype(bf16)
    for q in range(2):
        for out, c in ((own, core[0]), (other, 1 - core[0])):
            columns = pl.ds(pl.multiple_of(256 * c + 128 * q, 128), 128)
            out[:, q, k, :, :] = held[:, columns].reshape(32, 16, 128)


def process_grads_body(
    scales, core, edge, cround, hidden, plinear, middle, receive, cot_update, rounded, uhidden, cot_linear, edge_cot, mesh_cot,
    w3, w5, w7, edge_grad, middle_part, grads_own, grads_other, held,
):
    pairs = ((edge, cround), (middle, receive), (hidden, plinear), (middle, cot_update), (rounded, cot_update), (uhidden, cot_linear))
    for k, (x, y) in enumerate(pairs):
        store_blocks(grads_own, grads_other, k, dot_tn(x[...], y[...]) * scales[k], held, core)
    middle_part[...] = mesh_cot[...].astype(f32) + dot_nt(cot_update[...], w7[...]) + dot_nt(receive[...], w5[...])

    def step(i, s):
        edge_grad[s, :] = (edge_cot[s, :].astype(f32) + dot_nt(cround[s, :], w3[...])).astype(bf16)

    chunks(4, step)


def encode_back_body(
    in0, in1, in2, in3, far_in, halo, far, sender_own, middle_part, pre, linear, slot, target, w2, w4,
    cot_sender_out, cot_middle_out, elinear_out, upper_out, g0, g1, g2, g3,
    source, wide,
):
    for k, block in enumerate((in0, in1, in2, in3)):
        source[64 * k : 64 * k + 64, :] = block[...]
    wide[...] = far_in[...].astype(f32)
    gather_far(wide, source, 256)
    owners = jnp.concatenate([put(halo, 0, 2, 0, 128), put(far, 0, 4, 0, 128)], axis=1)
    cot_sender = (sender_own[...] + dot(owners, source[...])).astype(bf16)
    cot_sender_out[...] = cot_sender
    cot_middle = middle_part[...] + dot_nt(cot_sender, w4[...])
    cot_middle_out[...] = cot_middle
    cot_middle = stack_halves(cot_middle)

    def step(i, s):
        receiver = pick(target, 2 * i, 2, 0, 128)
        normed, inverse = norm_parts(linear[s, :])
        cot = norm_back(normed, inverse, dot(twice(receiver), cot_middle)).astype(bf16)
        elinear_out[s, :] = cot
        upper_out[s, :] = (dot_nt(cot, w2[...]) * slope(pre[s, :])).astype(bf16)

    chunks(4, step)
    for k, out in enumerate((g0, g1, g2, g3)):
        spread = put(slot, 0, 8, 512 + 256 * k, 256)
        out[...] = dot(spread, upper_out[...]).astype(bf16)


def encode_grads_body(
    scales, core, upper, slot, target, cot_middle, mesh, middle, cot_sender, hidden, elinear, w1,
    grid_own, mesh_grad, grads_own, grads_other, held,
):
    def store(k, x, y, scale):
        store_blocks(grads_own, grads_other, k, dot_tn(x, y) * scale, held, core)

    store(1, hidden[...], elinear[...], scales[1])
    store(2, middle[...], cot_sender[...], scales[2])
    receive = dot(put(target, 0, 8, 0, 128), upper[...]).astype(bf16)
    store(0, mesh[...], receive, scales[0])
    mesh_grad[...] = (cot_middle[...] + dot_nt(receive, w1[...])).astype(bf16)
    for k in range(2):
        grid_own[256 * k : 256 * k + 256, :] = dot(put(slot, 0, 8, 256 * k, 256), upper[...])


def grid_back_body(scales, core, grid_own, in0, in1, in2, in3, table, grid, w0, grid_grad, grads_own, grads_other, cot, held):
    for i in range(2):
        s = slice(CHUNK * i, CHUNK * i + CHUNK)
        total = grid_own[s, :]
        for k, block in enumerate((in0, in1, in2, in3)):
            total = total + dot(put_rows(table_rows(table, k), i * CHUNK, CHUNK), block[...])
        total = total.astype(bf16)
        cot[s, :] = total
        grid_grad[s, :] = dot_nt(total, w0[...]).astype(bf16)
    store_blocks(grads_own, grads_other, 0, dot_tn(grid[...], cot[...]) * scales[0], held, core)


def pair_body(*refs):
    out = refs[-1]
    place = 0
    for own, got in zip(refs[0:-1:2], refs[1:-1:2]):
        for k in range(own.shape[2]):
            out[:, :, place] = (own[:, :, k].astype(f32) + got[:, :, k].astype(f32)).astype(bf16)
            place += 1


def sum_body(terms, *shard):
    total = terms[0].astype(f32)
    for d in range(1, terms.shape[0]):
        total = total + terms[d].astype(f32)
    total = total.astype(bf16)
    if len(shard[0].shape) == 2:
        shard[0][...] = total
    else:
        for p in range(shard[0].shape[0]):
            shard[0][p] = total


def place_early_body(order, blocks, out):
    for place, k in enumerate(order):
        for c in range(2):
            for q in range(2):
                first = 256 * c + 128 * q
                out[k, :, first : first + 128] = blocks[:, c, :, q, place].reshape(512, 128)


def place_late_body(core, own, other, kept, out):
    del kept
    first = core[0] == 0
    for q in range(2):
        a, b = own[:, q].reshape(512, 128), other[:, q].reshape(512, 128)
        out[:, 128 * q : 128 * q + 128] = jnp.where(first, a, b)
        out[:, 256 + 128 * q : 384 + 128 * q] = jnp.where(first, b, a)


def swapped(value):
    return lax.ppermute(value, "core", [(0, 1), (1, 0)])


def scaled(body, scales):
    return functools.partial(body, scales)


def on_device(
    grid_latent, mesh_latent, edge_latent, mesh_cotangent, edge_cotangent, grid_send, grid_slot, grid_target,
    mesh_halo, mesh_send, mesh_slot, mesh_target, weights,
):
    peers = lax.axis_size(AXES)
    mesh_rows, latent = mesh_latent.shape
    edges = grid_slot.shape[0]
    grid_scale = 1.0 / (edges * peers) ** 0.5
    edge_scale = 1.0 / (mesh_slot.shape[0] * peers) ** 0.5
    node_scale = 1.0 / (mesh_rows * peers) ** 0.5
    grid_table = grid_send
    core = lax.axis_index("core").reshape(1)
    halo_table = mesh_halo.reshape(2, 128)
    far_table = mesh_send[0].T
    gslot, gtarget = grid_slot.reshape(8, 128), grid_target.reshape(8, 128)
    mslot, mtarget = mesh_slot.reshape(8, 128), mesh_target.reshape(8, 128)
    big, small, halo = (edges, latent), (mesh_rows, latent), (64, latent)
    vm = pltpu.VMEM

    project, *outgoing = call(
        project_body, [((512, latent), bf16)] + [((256, latent), bf16)] * 4,
        (grid_latent, grid_table), weights, (0,),
    )
    arrived = outgoing_rows(outgoing)
    (own,) = call(
        encode_own_body, [(big, f32)], (project, gslot, gtarget, mesh_latent),
        weights, (1,), scratch=(vm((768, latent), bf16),), flops=10**9,
    )
    pre, linear, hidden, middle, sender, *halos, far_out = call(
        encode_body,
        [(big, f32), (big, f32), (big, bf16), (small, bf16), (small, bf16)] + [(halo, bf16)] * 4 + [((2048, 128), bf16)],
        (own, *arrived, gslot, gtarget, mesh_latent, halo_table, far_table), weights, (2, 4),
        scratch=(vm(small, f32), vm((2048, 128), f32)), flops=2 * 10**9,
    )
    far_in = lax.all_to_all(far_out.reshape(peers, 16, 128), AXES, 0, 0, tiled=True).reshape(2048, 128)
    halo_in = outgoing_rows(halos)
    own, update_own = call(
        process_own_body, [(big, f32), (small, f32)], (middle, sender, edge_latent, mslot, mtarget),
        weights, (3, 5, 7), scratch=(vm((384, latent), bf16),), flops=2 * 10**9,
    )
    (
        mesh_update, phidden, rounded, uhidden, cot_linear, cot_update, plinear, cround, receive, sender_own,
        *halos, far_out,
    ) = call(
        process_body,
        [(small, bf16), (big, bf16)] + [(small, bf16)] * 4 + [(big, bf16)] * 2
        + [(small, bf16), (small, f32)] + [(halo, bf16)] * 4 + [((2048, 128), bf16)],
        (own, *halo_in, far_in, mslot, mtarget, middle, update_own, mesh_cotangent, edge_cotangent),
        weights, (6, 8, 9),
        scratch=(
            vm((768, latent), bf16), vm(big, f32), vm(big, f32), vm((edges, 128), f32),
            vm(small, f32), vm((2048, 128), f32), vm((8, 128), jnp.int32),
        ),
        flops=8 * 10**9,
    )
    far_back = lax.all_to_all(far_out.reshape(peers, 16, 128), AXES, 0, 0, tiled=True).reshape(2048, 128)
    halo_back = returned_rows(halos)

    def blocks(count):
        return ((32, 2, count, 16, 128), bf16)

    held = vm((latent, latent), bf16)
    edge_grad, middle_part, early_own, early_other = call(
        scaled(process_grads_body, [edge_scale] * 3 + [node_scale] * 3),
        [(big, bf16), (small, f32), blocks(6), blocks(6)],
        (core, edge_latent, cround, phidden, plinear, middle, receive, cot_update, rounded, uhidden, cot_linear,
         edge_cotangent, mesh_cotangent),
        weights, (3, 5, 7), scratch=(held,), flops=3 * 10**9,
    )
    (early,) = call(pair_body, [blocks(6)], (early_own, swapped(early_other)), flops=10**6)
    early, _ = lax.optimization_barrier((early, (halo_back, far_back)))
    early = lax.all_to_all(early.reshape(64, 96, 128), CHIPS, 0, 0, tiled=True)
    (early,) = call(sum_body, [((96, 128), bf16)], (early,), flops=10**7)
    early = lax.all_gather(early, AXES, axis=0, tiled=True).reshape(4, 2, 8, 2, 6, 16, 128)
    (placed,) = call(
        functools.partial(place_early_body, (3, 5, 6, 7, 8, 9)), [(weights.shape, bf16)], (early,),
        flops=10**6,
    )
    cot_sender, cot_middle, elinear, upper, *partials = call(
        encode_back_body,
        [(small, bf16), (small, f32), (big, bf16), (big, bf16)] + [((256, latent), bf16)] * 4,
        (*halo_back, far_back, halo_table, far_table, sender_own, middle_part, pre, linear, gslot, gtarget),
        weights, (2, 4), scratch=(vm((768, latent), bf16), vm((2048, 128), f32)), flops=4 * 10**9,
    )
    partials = returned_rows(partials)
    grid_own, mesh_grad, late_own, late_other = call(
        scaled(encode_grads_body, [grid_scale, grid_scale, edge_scale]),
        [((512, latent), f32), (small, bf16), blocks(3), blocks(3)],
        (core, upper, gslot, gtarget, cot_middle, mesh_latent, middle, cot_sender, hidden, elinear),
        weights, (1,), scratch=(held,), flops=2 * 10**9,
    )
    grid_grad, last_own, last_other = call(
        scaled(grid_back_body, [grid_scale]), [((512, latent), bf16), blocks(1), blocks(1)],
        (core, grid_own, *partials, grid_table, grid_latent), weights, (0,),
        scratch=(vm((512, latent), bf16), held),
    )
    (late,) = call(
        pair_body, [blocks(4)], (last_own, swapped(last_other), late_own, swapped(late_other)),
        flops=10**6,
    )
    late = lax.all_to_all(late.reshape(64, 64, 128), CHIPS, 0, 0, tiled=True)
    (late,) = call(sum_body, [((64, 64, 128), bf16)], (late,), flops=10**7)
    late = lax.all_to_all(late, CHIPS, 0, 0, tiled=True)
    other = swapped(late).reshape(blocks(4)[0])
    late = late.reshape(blocks(4)[0])
    weight_grads = pl.pallas_call(
        place_late_body,
        grid_spec=pltpu.PrefetchScalarGridSpec(
            num_scalar_prefetch=1,
            grid=(4,),
            in_specs=[pl.BlockSpec((32, 2, None, 16, 128), lambda i, c: (0, 0, i, 0, 0))] * 2
            + [pl.BlockSpec(memory_space=pl.ANY)],
            out_specs=pl.BlockSpec((None, latent, latent), lambda i, c: (i + i // 3, 0, 0)),
        ),
        out_shape=jax.ShapeDtypeStruct(weights.shape, bf16),
        input_output_aliases={3: 0},
        compiler_params=pltpu.CompilerParams(vmem_limit_bytes=67000000),
        name="place_late",
    )(core, late, other, placed)
    return (mesh_update, grid_grad, mesh_grad, edge_grad, weight_grads)


def solution(mesh):
    row = P(AXES, None)
    wide = jax.sharding.Mesh(mesh.devices.reshape(4, 2, 4, 4), AXES)

    return jax.shard_map(
        on_device,
        mesh=wide,
        in_specs=(row, row, row, row, row, P(AXES, None, None), P(AXES), P(AXES), P(AXES, None, None),
                  P(AXES, None, None), P(AXES), P(AXES), P()),
        out_specs=(row, row, row, row, P()),
        check_vma=False,
    )
```

```python
import functools

import jax
import jax.numpy as jnp
from jax import lax
from jax.experimental import pallas as pl
from jax.experimental.pallas import tpu as pltpu
from jax.sharding import PartitionSpec as P


norm_eps = 1e-05
f32 = jnp.float32
bf16 = jnp.bfloat16
AXES = ("x", "core", "y", "z")
CHIPS = ("x", "y", "z")
FACE = ("x", "core")
SUB = ("y", "z")
CHUNK = 512
ROWS = CHUNK // 128


def shifted(value, axis, steps):
    count = lax.axis_size(axis)
    pairs = [(source, (source + steps) % count) for source in range(count)]
    return lax.ppermute(value, axis, pairs)


def outgoing_rows(blocks):
    routes = ((SUB, 1), (SUB, -1), (FACE, 1), (FACE, -1))
    return [shifted(block, axis, step) for block, (axis, step) in zip(blocks, routes)]


def returned_rows(blocks):
    routes = ((SUB, -1), (SUB, 1), (FACE, -1), (FACE, 1))
    return [shifted(block, axis, step) for block, (axis, step) in zip(blocks, routes)]


def dot(a, b):
    return jnp.dot(a, b, preferred_element_type=f32)


def dot_nt(a, b):
    return lax.dot_general(a, b, (((1,), (1,)), ((), ())), preferred_element_type=f32)


def dot_tn(a, b):
    return lax.dot_general(a, b, (((0,), (0,)), ((), ())), preferred_element_type=f32)


def halves(values):
    upper = values.astype(bf16)
    return upper, (values - upper.astype(f32)).astype(bf16)


def mean(values):
    return jnp.sum(values, axis=-1, keepdims=True) * (1.0 / values.shape[-1])


def norm_parts(values):
    centre = values - mean(values)
    inverse = lax.rsqrt(mean(centre * centre) + norm_eps)
    return centre * inverse, inverse


def norm_back(normed, inverse, upstream):
    return inverse * (upstream - mean(upstream) - normed * mean(upstream * normed))


def sigmoid(values):
    return 1.0 / (1.0 + jnp.exp(-values))


def silu(values):
    return values * sigmoid(values)


def slope(values):
    s = sigmoid(values)
    return s * (1.0 + values * (1.0 - s))


def pick_rows(row, offset, count):
    column = jnp.transpose(jnp.broadcast_to(row, (128, 128))) - offset
    lane = lax.broadcasted_iota(jnp.int32, (128, 128), 1)
    return jnp.concatenate(
        [jnp.where(column == lane + 128 * b, 1.0, 0.0).astype(bf16) for b in range(count // 128)],
        axis=1,
    )


def pick(ref, first, rows, offset, count):
    return jnp.concatenate(
        [pick_rows(ref[pl.ds(first + r, 1), :], offset, count) for r in range(rows)], axis=0
    )


def put(ref, first, rows, offset, count):
    return put_rows([ref[pl.ds(first + r, 1), :] for r in range(rows)], offset, count)


def table_rows(table, k):
    return [table[0, k : k + 1, 128 * h : 128 * h + 128] for h in range(2)]


def put_rows(rows, offset, count):
    place = lax.broadcasted_iota(jnp.int32, (count, 128), 0) + offset
    return jnp.concatenate(
        [jnp.where(place == jnp.broadcast_to(row, (count, 128)), 1.0, 0.0).astype(bf16) for row in rows], axis=1
    )


def stack_halves(values):
    return jnp.concatenate(halves(values), axis=0)


def twice(values):
    return jnp.concatenate([values, values], axis=1)


def chunks(count, body):
    def step(i, carry):
        body(i, pl.ds(pl.multiple_of(i * CHUNK, CHUNK), CHUNK))
        return carry

    lax.fori_loop(0, count, step, 0)


def call(body, outs, args, weights=None, picks=(), scratch=(), flops=10**9, vmem=67000000):
    def whole(shape):
        return pl.BlockSpec(shape, lambda i: (0,) * len(shape))

    in_specs = [pl.BlockSpec(memory_space=pltpu.SMEM) if a.shape == (1,) else whole(a.shape) for a in args]
    for k in picks:
        in_specs.append(
            pl.BlockSpec((None, weights.shape[1], weights.shape[2]), functools.partial(lambda k, i: (k, 0, 0), k))
        )
    shapes = [jax.ShapeDtypeStruct(s, d) for s, d in outs]
    total = sum(a.size * a.dtype.itemsize for a in args) + sum(s.size * s.dtype.itemsize for s in shapes)
    total += len(picks) * 512 * 1024
    return pl.pallas_call(
        body,
        grid=(1,),
        out_shape=shapes,
        in_specs=in_specs,
        out_specs=[whole(s.shape) for s in shapes],
        scratch_shapes=list(scratch),
        compiler_params=pltpu.CompilerParams(vmem_limit_bytes=vmem),
        cost_estimate=pl.CostEstimate(flops=flops, bytes_accessed=total, transcendentals=0),
    )(*args, *([weights] * len(picks)))


def project_body(grid, table, w0, project, out0, out1, out2, out3):
    chunks(512 // CHUNK, lambda i, s: project.__setitem__((s, slice(None)), dot(grid[s, :], w0[...]).astype(bf16)))
    for k, out in enumerate((out0, out1, out2, out3)):
        picked = jnp.concatenate([pick_rows(row, 0, 512) for row in table_rows(table, k)], axis=0)
        out[...] = dot(picked, project[...]).astype(bf16)


def encode_own_body(project, slot, target, mesh, w1, own, source):
    source[0:512, :] = project[...]
    source[512:768, :] = stack_halves(dot(mesh[...], w1[...]))

    def step(i, s):
        receiver = pick(target, ROWS * i, ROWS, 0, 128)
        own[s, :] = dot(jnp.concatenate([pick(slot, ROWS * i, ROWS, 0, 512), twice(receiver)], axis=1), source[...])

    chunks(1024 // CHUNK, step)


def far_slots(slot):
    far = slot - 384
    return jnp.where(slot < 384, slot, 384 + (far & 3) * 128 + (far >> 2))


def encode_body(
    own, in0, in1, in2, in3, slot, target, mesh, halo, far, w2, w4,
    pre_out, linear_out, hidden_out, middle_out, sender_out, h0, h1, h2, h3, far_out,
    total, wide,
):
    total[...] = jnp.zeros_like(total)

    def step(i, s):
        pre = own[s, :]
        for k, block in enumerate((in0, in1, in2, in3)):
            pre = pre + dot(pick(slot, ROWS * i, ROWS, 512 + 256 * k, 256), block[...])
        pre_out[s, :] = pre
        hidden = silu(pre).astype(bf16)
        hidden_out[s, :] = hidden
        linear = dot(hidden, w2[...])
        linear_out[s, :] = linear
        message = norm_parts(linear)[0].astype(bf16)
        total[...] += dot(put(target, ROWS * i, ROWS, 0, 128), message)

    chunks(1024 // CHUNK, step)
    middle = (mesh[...].astype(f32) + total[...]).astype(bf16)
    middle_out[...] = middle
    sender = dot(middle, w4[...]).astype(bf16)
    sender_out[...] = sender
    rows = dot(pick(halo, 0, 2, 0, 128), sender).astype(bf16)
    for k, out in enumerate((h0, h1, h2, h3)):
        out[...] = rows[64 * k : 64 * k + 64, :]
    for r in range(4):
        picked = dot(pick(far, r, 1, 0, 128), sender)
        for c in range(4):
            wide[pl.ds(4 * c + r, 128, stride=16), :] = picked[:, 128 * c : 128 * c + 128]
    far_out[...] = wide[...].astype(bf16)


def process_own_body(middle, sender, edge, slot, target, w3, w5, w7, own, update_own, source):
    source[0:128, :] = sender[...]
    source[128:384, :] = stack_halves(dot(middle[...], w5[...]))
    update_own[...] = dot(middle[...], w7[...])

    def step(i, s):
        receiver = pick(target, ROWS * i, ROWS, 0, 128)
        picked = jnp.concatenate([pick(slot, ROWS * i, ROWS, 0, 128), twice(receiver)], axis=1)
        own[s, :] = dot(edge[s, :], w3[...]) + dot(picked, source[...])

    chunks(1024 // CHUNK, step)


def gather_far(wide, source, first):
    for r in range(4):
        for c in range(4):
            source[first + 128 * r : first + 128 * r + 128, 128 * c : 128 * c + 128] = wide[
                pl.ds(4 * c + r, 128, stride=16), :
            ].astype(bf16)


def process_body(
    own, in0, in1, in2, in3, far_in, slot, target, middle, update_own, mesh_cot, edge_cot, w6, w8, w9,
    mesh_update, hidden_out, round_out, uhidden_out, cot_linear_out, cot_update_out, plinear_out, cround_out,
    receive_out, sender_own, h0, h1, h2, h3, far_out,
    source, pre_s, normed_s, inverse_s, total, wide, slots,
):
    slots[...] = far_slots(slot[...])
    for k, block in enumerate((in0, in1, in2, in3)):
        source[64 * k : 64 * k + 64, :] = block[...]
    wide[...] = far_in[...].astype(f32)
    gather_far(wide, source, 256)
    total[...] = jnp.zeros_like(total)

    def forward(i, s):
        pre = own[s, :] + dot(pick(slots, ROWS * i, ROWS, 128, 768), source[...])
        pre_s[s, :] = pre
        hidden = silu(pre).astype(bf16)
        hidden_out[s, :] = hidden
        normed, inverse = norm_parts(dot(hidden, w6[...]))
        normed_s[s, :] = normed
        inverse_s[s, :] = jnp.broadcast_to(inverse, (CHUNK, 128))
        total[...] += dot(put(target, ROWS * i, ROWS, 0, 128), normed.astype(bf16))

    chunks(1024 // CHUNK, forward)
    rounded = total[...].astype(bf16)
    round_out[...] = rounded
    pre = update_own[...] + dot(rounded, w8[...])
    uhidden = silu(pre).astype(bf16)
    uhidden_out[...] = uhidden
    normed, inverse = norm_parts(dot(uhidden, w9[...]))
    mesh_update[...] = (middle[...].astype(f32) + normed).astype(bf16)
    cot_linear = norm_back(normed, inverse, mesh_cot[...].astype(f32)).astype(bf16)
    cot_linear_out[...] = cot_linear
    cot_update = (dot_nt(cot_linear, w9[...]) * slope(pre)).astype(bf16)
    cot_update_out[...] = cot_update
    cot_total = stack_halves(dot_nt(cot_update, w8[...]))

    def backward(i, s):
        receiver = pick(target, ROWS * i, ROWS, 0, 128)
        upstream = dot(twice(receiver), cot_total) + edge_cot[s, :].astype(f32)
        cot = norm_back(normed_s[s, :], inverse_s[s, 0:1], upstream).astype(bf16)
        plinear_out[s, :] = cot
        cround_out[s, :] = (dot_nt(cot, w6[...]) * slope(pre_s[s, :])).astype(bf16)

    chunks(1024 // CHUNK, backward)
    kept = jnp.concatenate([put(target, 0, 8, 0, 128), put(slots, 0, 8, 0, 128)], axis=0)
    kept = dot(kept, cround_out[...])
    receive_out[...] = kept[0:128, :].astype(bf16)
    sender_own[...] = kept[128:256, :]
    spread = put(slots, 0, 8, 128, 256)
    spread = dot(spread, cround_out[...]).astype(bf16)
    for k, out in enumerate((h0, h1, h2, h3)):
        out[...] = spread[64 * k : 64 * k + 64, :]
    for half in range(2):
        spread = put(slots, 0, 8, 384 + 256 * half, 256)
        spread = dot(spread, cround_out[...])
        for q in range(2):
            for c in range(4):
                wide[pl.ds(4 * c + 2 * half + q, 128, stride=16), :] = spread[
                    128 * q : 128 * q + 128, 128 * c : 128 * c + 128
                ]
    far_out[...] = wide[...].astype(bf16)


def store_blocks(own, other, k, term, held, core):
    held[...] = term.astype(bf16)
    for q in range(2):
        for out, c in ((own, core[0]), (other, 1 - core[0])):
            columns = pl.ds(pl.multiple_of(256 * c + 128 * q, 128), 128)
            out[:, q, k, :, :] = held[:, columns].reshape(32, 16, 128)


def process_grads_body(
    scales, core, edge, cround, hidden, plinear, middle, receive, cot_update, rounded, uhidden, cot_linear, edge_cot, mesh_cot,
    w3, w5, w7, edge_grad, middle_part, grads_own, grads_other, held,
):
    pairs = ((edge, cround), (middle, receive), (hidden, plinear), (middle, cot_update), (rounded, cot_update), (uhidden, cot_linear))
    for k, (x, y) in enumerate(pairs):
        store_blocks(grads_own, grads_other, k, dot_tn(x[...], y[...]) * scales[k], held, core)
    middle_part[...] = mesh_cot[...].astype(f32) + dot_nt(cot_update[...], w7[...]) + dot_nt(receive[...], w5[...])

    def step(i, s):
        edge_grad[s, :] = (edge_cot[s, :].astype(f32) + dot_nt(cround[s, :], w3[...])).astype(bf16)

    chunks(1024 // CHUNK, step)


def encode_back_body(
    in0, in1, in2, in3, far_in, halo, far, sender_own, middle_part, pre, linear, slot, target, w2, w4,
    cot_sender_out, cot_middle_out, elinear_out, upper_out, g0, g1, g2, g3,
    source, wide,
):
    for k, block in enumerate((in0, in1, in2, in3)):
        source[64 * k : 64 * k + 64, :] = block[...]
    wide[...] = far_in[...].astype(f32)
    gather_far(wide, source, 256)
    owners = jnp.concatenate([put(halo, 0, 2, 0, 128), put(far, 0, 4, 0, 128)], axis=1)
    cot_sender = (sender_own[...] + dot(owners, source[...])).astype(bf16)
    cot_sender_out[...] = cot_sender
    cot_middle = middle_part[...] + dot_nt(cot_sender, w4[...])
    cot_middle_out[...] = cot_middle
    cot_middle = stack_halves(cot_middle)

    def step(i, s):
        receiver = pick(target, ROWS * i, ROWS, 0, 128)
        normed, inverse = norm_parts(linear[s, :])
        cot = norm_back(normed, inverse, dot(twice(receiver), cot_middle)).astype(bf16)
        elinear_out[s, :] = cot
        upper_out[s, :] = (dot_nt(cot, w2[...]) * slope(pre[s, :])).astype(bf16)

    chunks(1024 // CHUNK, step)
    for k, out in enumerate((g0, g1, g2, g3)):
        spread = put(slot, 0, 8, 512 + 256 * k, 256)
        out[...] = dot(spread, upper_out[...]).astype(bf16)


def encode_grads_body(
    scales, core, upper, slot, target, cot_middle, mesh, middle, cot_sender, hidden, elinear, w1,
    grid_own, mesh_grad, grads_own, grads_other, held,
):
    def store(k, x, y, scale):
        store_blocks(grads_own, grads_other, k, dot_tn(x, y) * scale, held, core)

    store(1, hidden[...], elinear[...], scales[1])
    store(2, middle[...], cot_sender[...], scales[2])
    receive = dot(put(target, 0, 8, 0, 128), upper[...]).astype(bf16)
    store(0, mesh[...], receive, scales[0])
    mesh_grad[...] = (cot_middle[...] + dot_nt(receive, w1[...])).astype(bf16)
    for k in range(2):
        grid_own[256 * k : 256 * k + 256, :] = dot(put(slot, 0, 8, 256 * k, 256), upper[...])


def grid_back_body(scales, core, grid_own, in0, in1, in2, in3, table, grid, w0, grid_grad, grads_own, grads_other, cot, held):
    for i in range(2):
        s = slice(256 * i, 256 * i + 256)
        total = grid_own[s, :]
        for k, block in enumerate((in0, in1, in2, in3)):
            total = total + dot(put_rows(table_rows(table, k), i * 256, 256), block[...])
        total = total.astype(bf16)
        cot[s, :] = total
        grid_grad[s, :] = dot_nt(total, w0[...]).astype(bf16)
    store_blocks(grads_own, grads_other, 0, dot_tn(grid[...], cot[...]) * scales[0], held, core)


def pair_body(*refs):
    out = refs[-1]
    place = 0
    for own, got in zip(refs[0:-1:2], refs[1:-1:2]):
        for k in range(own.shape[2]):
            out[:, :, place] = (own[:, :, k].astype(f32) + got[:, :, k].astype(f32)).astype(bf16)
            place += 1


def sum_body(terms, *shard):
    total = terms[0].astype(f32)
    for d in range(1, terms.shape[0]):
        total = total + terms[d].astype(f32)
    total = total.astype(bf16)
    if len(shard[0].shape) == 2:
        shard[0][...] = total
    else:
        for p in range(shard[0].shape[0]):
            shard[0][p] = total


def place_early_body(core, own, other, out):
    first = core[0] == 0
    for q in range(2):
        a, b = own[:, q].reshape(512, 128), other[:, q].reshape(512, 128)
        out[:, 128 * q : 128 * q + 128] = jnp.where(first, a, b)
        out[:, 256 + 128 * q : 384 + 128 * q] = jnp.where(first, b, a)


def place_late_body(core, own, other, kept, out):
    del kept
    place_early_body(core, own, other, out)


def swapped(value):
    return lax.ppermute(value, "core", [(0, 1), (1, 0)])


def scaled(body, scales):
    return functools.partial(body, scales)


def on_device(
    grid_latent, mesh_latent, edge_latent, mesh_cotangent, edge_cotangent, grid_send, grid_slot, grid_target,
    mesh_halo, mesh_send, mesh_slot, mesh_target, weights,
):
    peers = lax.axis_size(AXES)
    mesh_rows, latent = mesh_latent.shape
    edges = grid_slot.shape[0]
    grid_scale = 1.0 / (edges * peers) ** 0.5
    edge_scale = 1.0 / (mesh_slot.shape[0] * peers) ** 0.5
    node_scale = 1.0 / (mesh_rows * peers) ** 0.5
    grid_table = grid_send
    core = lax.axis_index("core").reshape(1)
    halo_table = mesh_halo.reshape(2, 128)
    far_table = mesh_send[0].T
    gslot, gtarget = grid_slot.reshape(8, 128), grid_target.reshape(8, 128)
    mslot, mtarget = mesh_slot.reshape(8, 128), mesh_target.reshape(8, 128)
    big, small, halo = (edges, latent), (mesh_rows, latent), (64, latent)
    vm = pltpu.VMEM

    project, *outgoing = call(
        project_body, [((512, latent), bf16)] + [((256, latent), bf16)] * 4,
        (grid_latent, grid_table), weights, (0,),
    )
    arrived = outgoing_rows(outgoing)
    (own,) = call(
        encode_own_body, [(big, f32)], (project, gslot, gtarget, mesh_latent),
        weights, (1,), scratch=(vm((768, latent), bf16),), flops=10**9,
    )
    pre, linear, hidden, middle, sender, *halos, far_out = call(
        encode_body,
        [(big, f32), (big, f32), (big, bf16), (small, bf16), (small, bf16)] + [(halo, bf16)] * 4 + [((2048, 128), bf16)],
        (own, *arrived, gslot, gtarget, mesh_latent, halo_table, far_table), weights, (2, 4),
        scratch=(vm(small, f32), vm((2048, 128), f32)), flops=2 * 10**9,
    )
    far_in = lax.all_to_all(far_out.reshape(peers, 16, 128), AXES, 0, 0, tiled=True).reshape(2048, 128)
    halo_in = outgoing_rows(halos)
    own, update_own = call(
        process_own_body, [(big, f32), (small, f32)], (middle, sender, edge_latent, mslot, mtarget),
        weights, (3, 5, 7), scratch=(vm((384, latent), bf16),), flops=2 * 10**9,
    )
    (
        mesh_update, phidden, rounded, uhidden, cot_linear, cot_update, plinear, cround, receive, sender_own,
        *halos, far_out,
    ) = call(
        process_body,
        [(small, bf16), (big, bf16)] + [(small, bf16)] * 4 + [(big, bf16)] * 2
        + [(small, bf16), (small, f32)] + [(halo, bf16)] * 4 + [((2048, 128), bf16)],
        (own, *halo_in, far_in, mslot, mtarget, middle, update_own, mesh_cotangent, edge_cotangent),
        weights, (6, 8, 9),
        scratch=(
            vm((768, latent), bf16), vm(big, f32), vm(big, f32), vm((edges, 128), f32),
            vm(small, f32), vm((2048, 128), f32), vm((8, 128), jnp.int32),
        ),
        flops=8 * 10**9,
    )
    far_back = lax.all_to_all(far_out.reshape(peers, 16, 128), AXES, 0, 0, tiled=True).reshape(2048, 128)
    halo_back = returned_rows(halos)

    def blocks(count):
        return ((32, 2, count, 16, 128), bf16)

    held = vm((latent, latent), bf16)
    edge_grad, middle_part, early_own, early_other = call(
        scaled(process_grads_body, [edge_scale] * 3 + [node_scale] * 3),
        [(big, bf16), (small, f32), blocks(6), blocks(6)],
        (core, edge_latent, cround, phidden, plinear, middle, receive, cot_update, rounded, uhidden, cot_linear,
         edge_cotangent, mesh_cotangent),
        weights, (3, 5, 7), scratch=(held,), flops=3 * 10**9,
    )
    early = (early_own.astype(f32) + swapped(early_other).astype(f32)).astype(bf16)
    early, _ = lax.optimization_barrier((early, (halo_back, far_back)))
    early = lax.all_to_all(early.reshape(64, 96, 128), CHIPS, 0, 0, tiled=True)
    cot_sender, cot_middle, elinear, upper, *partials = call(
        encode_back_body,
        [(small, bf16), (small, f32), (big, bf16), (big, bf16)] + [((256, latent), bf16)] * 4,
        (*halo_back, far_back, halo_table, far_table, sender_own, middle_part, pre, linear, gslot, gtarget),
        weights, (2, 4), scratch=(vm((768, latent), bf16), vm((2048, 128), f32)), flops=4 * 10**9,
    )
    partials = returned_rows(partials)
    grid_own, mesh_grad, late_own, late_other = call(
        scaled(encode_grads_body, [grid_scale, grid_scale, edge_scale]),
        [((512, latent), f32), (small, bf16), blocks(3), blocks(3)],
        (core, upper, gslot, gtarget, cot_middle, mesh_latent, middle, cot_sender, hidden, elinear),
        weights, (1,), scratch=(held,), flops=2 * 10**9,
    )
    (early,) = call(sum_body, [((64, 96, 128), bf16)], (early,), flops=10**7)
    early = lax.all_to_all(early, CHIPS, 0, 0, tiled=True)
    grid_grad, last_own, last_other = call(
        scaled(grid_back_body, [grid_scale]), [((512, latent), bf16), blocks(1), blocks(1)],
        (core, grid_own, *partials, grid_table, grid_latent), weights, (0,),
        scratch=(vm((512, latent), bf16), held),
    )
    (late,) = call(
        pair_body, [blocks(4)], (last_own, swapped(last_other), late_own, swapped(late_other)),
        flops=10**6,
    )
    late, early = lax.optimization_barrier((late, early))
    late = lax.all_to_all(late.reshape(64, 64, 128), CHIPS, 0, 0, tiled=True)
    early_swapped = swapped(early).reshape(blocks(6)[0])
    early = early.reshape(blocks(6)[0])
    placed = pl.pallas_call(
        place_early_body,
        grid_spec=pltpu.PrefetchScalarGridSpec(
            num_scalar_prefetch=1,
            grid=(6,),
            in_specs=[pl.BlockSpec((32, 2, None, 16, 128), lambda i, c: (0, 0, i, 0, 0))] * 2,
            out_specs=pl.BlockSpec((None, latent, latent), lambda i, c: (i + 3 + (i + 5) // 6, 0, 0)),
        ),
        out_shape=jax.ShapeDtypeStruct(weights.shape, bf16),
        compiler_params=pltpu.CompilerParams(vmem_limit_bytes=67000000),
        name="place_early",
    )(core, early, early_swapped)
    (late,) = call(sum_body, [((64, 64, 128), bf16)], (late,), flops=10**7)
    late = lax.all_to_all(late, CHIPS, 0, 0, tiled=True)
    other = swapped(late).reshape(blocks(4)[0])
    late = late.reshape(blocks(4)[0])
    weight_grads = pl.pallas_call(
        place_late_body,
        grid_spec=pltpu.PrefetchScalarGridSpec(
            num_scalar_prefetch=1,
            grid=(4,),
            in_specs=[pl.BlockSpec((32, 2, None, 16, 128), lambda i, c: (0, 0, i, 0, 0))] * 2
            + [pl.BlockSpec(memory_space=pl.ANY)],
            out_specs=pl.BlockSpec((None, latent, latent), lambda i, c: (i + i // 3, 0, 0)),
        ),
        out_shape=jax.ShapeDtypeStruct(weights.shape, bf16),
        input_output_aliases={3: 0},
        compiler_params=pltpu.CompilerParams(vmem_limit_bytes=67000000),
        name="place_late",
    )(core, late, other, placed)
    return (mesh_update, grid_grad, mesh_grad, edge_grad, weight_grads)


def solution(mesh):
    row = P(AXES, None)
    wide = jax.sharding.Mesh(mesh.devices.reshape(4, 2, 4, 4), AXES)

    return jax.shard_map(
        on_device,
        mesh=wide,
        in_specs=(row, row, row, row, row, P(AXES, None, None), P(AXES), P(AXES), P(AXES, None, None),
                  P(AXES, None, None), P(AXES), P(AXES), P()),
        out_specs=(row, row, row, row, P()),
        check_vma=False,
    )
```

```python
import functools

import jax
import jax.numpy as jnp
from jax import lax
from jax.experimental import pallas as pl
from jax.experimental.pallas import tpu as pltpu
from jax.sharding import PartitionSpec as P


norm_eps = 1e-05
f32 = jnp.float32
bf16 = jnp.bfloat16
AXES = ("x", "core", "y", "z")
CHIPS = ("x", "y", "z")
FACE = ("x", "core")
SUB = ("y", "z")
CHUNK = 512
ROWS = CHUNK // 128


def shifted(value, axis, steps):
    count = lax.axis_size(axis)
    pairs = [(source, (source + steps) % count) for source in range(count)]
    return lax.ppermute(value, axis, pairs)


def outgoing_rows(blocks):
    routes = ((SUB, 1), (SUB, -1), (FACE, 1), (FACE, -1))
    return [shifted(block, axis, step) for block, (axis, step) in zip(blocks, routes)]


def returned_rows(blocks):
    routes = ((SUB, -1), (SUB, 1), (FACE, -1), (FACE, 1))
    return [shifted(block, axis, step) for block, (axis, step) in zip(blocks, routes)]


def dot(a, b):
    return jnp.dot(a, b, preferred_element_type=f32)


def dot_nt(a, b):
    return lax.dot_general(a, b, (((1,), (1,)), ((), ())), preferred_element_type=f32)


def dot_tn(a, b):
    return lax.dot_general(a, b, (((0,), (0,)), ((), ())), preferred_element_type=f32)


def halves(values):
    upper = values.astype(bf16)
    return upper, (values - upper.astype(f32)).astype(bf16)


def mean(values):
    return jnp.sum(values, axis=-1, keepdims=True) * (1.0 / values.shape[-1])


def norm_parts(values):
    centre = values - mean(values)
    inverse = lax.rsqrt(mean(centre * centre) + norm_eps)
    return centre * inverse, inverse


def norm_back(normed, inverse, upstream):
    return inverse * (upstream - mean(upstream) - normed * mean(upstream * normed))


def sigmoid(values):
    return 1.0 / (1.0 + jnp.exp(-values))


def silu(values):
    return values * sigmoid(values)


def slope(values):
    s = sigmoid(values)
    return s * (1.0 + values * (1.0 - s))


def pick_rows(row, offset, count):
    column = jnp.transpose(jnp.broadcast_to(row, (128, 128))) - offset
    lane = lax.broadcasted_iota(jnp.int32, (128, 128), 1)
    return jnp.concatenate(
        [jnp.where(column == lane + 128 * b, 1.0, 0.0).astype(bf16) for b in range(count // 128)],
        axis=1,
    )


def pick(ref, first, rows, offset, count):
    return jnp.concatenate(
        [pick_rows(ref[pl.ds(first + r, 1), :], offset, count) for r in range(rows)], axis=0
    )


def put(ref, first, rows, offset, count):
    return put_rows([ref[pl.ds(first + r, 1), :] for r in range(rows)], offset, count)


def table_rows(table, k):
    return [table[0, k : k + 1, 128 * h : 128 * h + 128] for h in range(2)]


def put_rows(rows, offset, count):
    place = lax.broadcasted_iota(jnp.int32, (count, 128), 0) + offset
    return jnp.concatenate(
        [jnp.where(place == jnp.broadcast_to(row, (count, 128)), 1.0, 0.0).astype(bf16) for row in rows], axis=1
    )


def stack_halves(values):
    return jnp.concatenate(halves(values), axis=0)


def twice(values):
    return jnp.concatenate([values, values], axis=1)


def chunks(count, body):
    for i in range(count):
        body(i, slice(i * CHUNK, i * CHUNK + CHUNK))


class Arriving:
    def __init__(self, source, held, sems):
        self.held, self.shape = held, held.shape
        parts = sems.shape[0]
        rows = held.shape[0] // parts
        pieces = [slice(None)] if parts == 1 else [slice(rows * i, rows * i + rows) for i in range(parts)]
        self.rows, self.waited = rows, [False] * parts
        self.copies = [
            pltpu.make_async_copy(source if parts == 1 else source.at[piece], held if parts == 1 else held.at[piece], sems.at[i])
            for i, piece in enumerate(pieces)
        ]

    def start(self):
        for copy in self.copies:
            copy.start()

    def wait(self, first=0, last=None):
        for i in range(first, len(self.copies) if last is None else last):
            if not self.waited[i]:
                self.copies[i].wait()
                self.waited[i] = True

    def __getitem__(self, index):
        rows = index[0] if isinstance(index, tuple) else index
        if len(self.copies) > 1 and isinstance(rows, slice) and rows.stop is not None:
            self.wait(rows.start // self.rows, -(-rows.stop // self.rows))
        else:
            self.wait()
        return self.held[index]


class Leaving:
    def __init__(self, held, target, sems):
        self.held, self.target, self.sems, self.shape = held, target, sems, held.shape
        self.copies = []

    def send(self, rows=None):
        if rows is None:
            copy = pltpu.make_async_copy(self.held, self.target, self.sems.at[0])
        else:
            copy = pltpu.make_async_copy(self.held.at[rows], self.target.at[rows], self.sems.at[len(self.copies)])
        copy.start()
        self.copies.append(copy)

    def finish(self):
        if not self.copies:
            self.send()

    def __getitem__(self, index):
        return self.held[index]

    def __setitem__(self, index, value):
        self.held[index] = value


def call(body, outs, args, weights=None, picks=(), scratch=(), flops=10**9, late=()):
    args = list(args)
    moved = [k for k, a in enumerate(args) if a.shape != (1,) and a.size * a.dtype.itemsize >= 4096 and a.shape[0] != 1]
    shapes = [jax.ShapeDtypeStruct(s, d) for s, d in outs]
    square = () if weights is None else weights.shape[1:]

    def parts(shape):
        return 2 if shape[0] == 1024 else 1

    def kernel(*refs):
        refs = list(refs)
        take = lambda count: [refs.pop(0) for _ in range(count)]
        given, bank, results = take(len(args)), take(1 if picks else 0), take(len(outs))
        held, held_w, held_out = take(len(moved)), take(len(picks)), take(len(outs))
        sems, sems_w, sems_out = take(len(moved)), take(len(picks)), take(len(outs))
        arriving = {k: Arriving(given[k], v, m) for k, v, m in zip(moved, held, sems)}
        chosen = [Arriving(bank[0].at[k], v, m) for k, v, m in zip(picks, held_w, sems_w)]
        for k in moved:
            if k not in late:
                arriving[k].start()
        for one in chosen:
            one.start()
        for k in late:
            arriving[k].start()
        leaving = [Leaving(v, t, m) for v, t, m in zip(held_out, results, sems_out)]
        body(*[arriving.get(k, given[k]) for k in range(len(args))], *chosen, *leaving, *refs)
        for one in leaving:
            one.finish()
        for one in list(arriving.values()) + chosen:
            one.wait()
        for one in leaving:
            for copy in one.copies:
                copy.wait()

    def spec(k):
        if k in moved:
            return pl.BlockSpec(memory_space=pl.ANY)
        return pl.BlockSpec(memory_space=pltpu.SMEM if args[k].shape == (1,) else pltpu.VMEM)

    any_space = pl.BlockSpec(memory_space=pl.ANY)
    total = sum(a.size * a.dtype.itemsize for a in args) + sum(s.size * s.dtype.itemsize for s in shapes)
    total += len(picks) * 512 * 1024
    dma = pltpu.SemaphoreType.DMA
    return pl.pallas_call(
        kernel,
        out_shape=shapes,
        in_specs=[spec(k) for k in range(len(args))] + [any_space] * (1 if picks else 0),
        out_specs=[any_space] * len(shapes),
        scratch_shapes=[pltpu.VMEM(args[k].shape, args[k].dtype) for k in moved]
        + [pltpu.VMEM(square, weights.dtype) for _ in picks]
        + [pltpu.VMEM(s.shape, s.dtype) for s in shapes]
        + [dma((parts(args[k].shape),)) for k in moved]
        + [dma((1,)) for _ in picks]
        + [dma((2,)) for _ in shapes]
        + list(scratch),
        compiler_params=pltpu.CompilerParams(vmem_limit_bytes=67000000),
        cost_estimate=pl.CostEstimate(flops=flops, bytes_accessed=total, transcendentals=0),
    )(*args, *([weights] if picks else []))


def project_body(grid, table, w0, project, out0, out1, out2, out3):
    project[...] = dot(grid[...], w0[...]).astype(bf16)
    project.send()
    for k, out in enumerate((out0, out1, out2, out3)):
        picked = jnp.concatenate([pick_rows(row, 0, 512) for row in table_rows(table, k)], axis=0)
        out[...] = dot(picked, project[...]).astype(bf16)
        out.send()


def encode_own_body(project, slot, target, mesh, w1, own, source):
    source[0:512, :] = project[...]
    source[512:768, :] = stack_halves(dot(mesh[...], w1[...]))

    def step(i, s):
        receiver = pick(target, ROWS * i, ROWS, 0, 128)
        own[s, :] = dot(jnp.concatenate([pick(slot, ROWS * i, ROWS, 0, 512), twice(receiver)], axis=1), source[...])
        own.send(s)

    chunks(1024 // CHUNK, step)


def far_slots(slot):
    far = slot - 384
    return jnp.where(slot < 384, slot, 384 + (far & 3) * 128 + (far >> 2))


def encode_body(
    own, in0, in1, in2, in3, slot, target, mesh, halo, far, w2, w4,
    pre_out, linear_out, hidden_out, middle_out, sender_out, h0, h1, h2, h3, far_out,
    total, wide,
):
    total[...] = jnp.zeros_like(total)

    def step(i, s):
        pre = own[s, :]
        for k, block in enumerate((in0, in1, in2, in3)):
            pre = pre + dot(pick(slot, ROWS * i, ROWS, 512 + 256 * k, 256), block[...])
        pre_out[s, :] = pre
        hidden = silu(pre).astype(bf16)
        hidden_out[s, :] = hidden
        linear = dot(hidden, w2[...])
        linear_out[s, :] = linear
        message = norm_parts(linear)[0].astype(bf16)
        total[...] += dot(put(target, ROWS * i, ROWS, 0, 128), message)
        for one in (pre_out, linear_out, hidden_out):
            one.send(s)

    chunks(1024 // CHUNK, step)
    middle = (mesh[...].astype(f32) + total[...]).astype(bf16)
    middle_out[...] = middle
    sender = dot(middle, w4[...]).astype(bf16)
    sender_out[...] = sender
    rows = dot(pick(halo, 0, 2, 0, 128), sender).astype(bf16)
    for k, out in enumerate((h0, h1, h2, h3)):
        out[...] = rows[64 * k : 64 * k + 64, :]
    for r in range(4):
        picked = dot(pick(far, r, 1, 0, 128), sender)
        for c in range(4):
            wide[pl.ds(4 * c + r, 128, stride=16), :] = picked[:, 128 * c : 128 * c + 128]
    far_out[...] = wide[...].astype(bf16)


def process_own_body(middle, sender, edge, slot, target, w3, w5, w7, own, update_own, source):
    source[0:128, :] = sender[...]
    source[128:384, :] = stack_halves(dot(middle[...], w5[...]))
    update_own[...] = dot(middle[...], w7[...])

    def step(i, s):
        receiver = pick(target, ROWS * i, ROWS, 0, 128)
        picked = jnp.concatenate([pick(slot, ROWS * i, ROWS, 0, 128), twice(receiver)], axis=1)
        own[s, :] = dot(edge[s, :], w3[...]) + dot(picked, source[...])
        own.send(s)

    chunks(1024 // CHUNK, step)


def gather_far(wide, source, first):
    for r in range(4):
        for c in range(4):
            source[first + 128 * r : first + 128 * r + 128, 128 * c : 128 * c + 128] = wide[
                pl.ds(4 * c + r, 128, stride=16), :
            ].astype(bf16)


def process_body(
    own, in0, in1, in2, in3, far_in, slot, target, middle, update_own, mesh_cot, edge_cot, w6, w8, w9,
    mesh_update, hidden_out, round_out, uhidden_out, cot_linear_out, cot_update_out, plinear_out, cround_out,
    receive_out, sender_own, h0, h1, h2, h3, far_out,
    source, pre_s, normed_s, inverse_s, total, wide, slots,
):
    slots[...] = far_slots(slot[...])
    for k, block in enumerate((in0, in1, in2, in3)):
        source[64 * k : 64 * k + 64, :] = block[...]
    wide[...] = far_in[...].astype(f32)
    gather_far(wide, source, 256)
    total[...] = jnp.zeros_like(total)

    def forward(i, s):
        pre = own[s, :] + dot(pick(slots, ROWS * i, ROWS, 128, 768), source[...])
        pre_s[s, :] = pre
        hidden = silu(pre).astype(bf16)
        hidden_out[s, :] = hidden
        normed, inverse = norm_parts(dot(hidden, w6[...]))
        normed_s[s, :] = normed
        inverse_s[s, :] = jnp.broadcast_to(inverse, (CHUNK, 128))
        total[...] += dot(put(target, ROWS * i, ROWS, 0, 128), normed.astype(bf16))
        hidden_out.send(s)

    chunks(1024 // CHUNK, forward)
    rounded = total[...].astype(bf16)
    round_out[...] = rounded
    pre = update_own[...] + dot(rounded, w8[...])
    uhidden = silu(pre).astype(bf16)
    uhidden_out[...] = uhidden
    normed, inverse = norm_parts(dot(uhidden, w9[...]))
    mesh_update[...] = (middle[...].astype(f32) + normed).astype(bf16)
    cot_linear = norm_back(normed, inverse, mesh_cot[...].astype(f32)).astype(bf16)
    cot_linear_out[...] = cot_linear
    cot_update = (dot_nt(cot_linear, w9[...]) * slope(pre)).astype(bf16)
    cot_update_out[...] = cot_update
    cot_total = stack_halves(dot_nt(cot_update, w8[...]))

    def backward(i, s):
        receiver = pick(target, ROWS * i, ROWS, 0, 128)
        upstream = dot(twice(receiver), cot_total) + edge_cot[s, :].astype(f32)
        cot = norm_back(normed_s[s, :], inverse_s[s, 0:1], upstream).astype(bf16)
        plinear_out[s, :] = cot
        cround_out[s, :] = (dot_nt(cot, w6[...]) * slope(pre_s[s, :])).astype(bf16)
        plinear_out.send(s)
        cround_out.send(s)

    chunks(1024 // CHUNK, backward)
    kept = jnp.concatenate([put(target, 0, 8, 0, 128), put(slots, 0, 8, 0, 128)], axis=0)
    kept = dot(kept, cround_out[...])
    receive_out[...] = kept[0:128, :].astype(bf16)
    sender_own[...] = kept[128:256, :]
    spread = put(slots, 0, 8, 128, 256)
    spread = dot(spread, cround_out[...]).astype(bf16)
    for k, out in enumerate((h0, h1, h2, h3)):
        out[...] = spread[64 * k : 64 * k + 64, :]
    for half in range(2):
        spread = put(slots, 0, 8, 384 + 256 * half, 256)
        spread = dot(spread, cround_out[...])
        for q in range(2):
            for c in range(4):
                wide[pl.ds(4 * c + 2 * half + q, 128, stride=16), :] = spread[
                    128 * q : 128 * q + 128, 128 * c : 128 * c + 128
                ]
    far_out[...] = wide[...].astype(bf16)


def store_blocks(own, other, k, term, held, core):
    held[...] = term.astype(bf16)
    for q in range(2):
        for out, c in ((own, core[0]), (other, 1 - core[0])):
            columns = pl.ds(pl.multiple_of(256 * c + 128 * q, 128), 128)
            out[:, q, k, :, :] = held[:, columns].reshape(32, 16, 128)


def process_grads_body(
    scales, core, edge, cround, hidden, plinear, middle, receive, cot_update, rounded, uhidden, cot_linear, edge_cot, mesh_cot,
    w3, w5, w7, edge_grad, middle_part, grads_own, grads_other, held,
):
    pairs = ((edge, cround), (middle, receive), (hidden, plinear), (middle, cot_update), (rounded, cot_update), (uhidden, cot_linear))
    for k, (x, y) in enumerate(pairs):
        store_blocks(grads_own, grads_other, k, dot_tn(x[...], y[...]) * scales[k], held, core)
    middle_part[...] = mesh_cot[...].astype(f32) + dot_nt(cot_update[...], w7[...]) + dot_nt(receive[...], w5[...])

    def step(i, s):
        edge_grad[s, :] = (edge_cot[s, :].astype(f32) + dot_nt(cround[s, :], w3[...])).astype(bf16)
        edge_grad.send(s)

    chunks(1024 // CHUNK, step)


def encode_back_body(
    in0, in1, in2, in3, far_in, halo, far, sender_own, middle_part, pre, linear, slot, target, w2, w4,
    cot_sender_out, cot_middle_out, elinear_out, upper_out, g0, g1, g2, g3,
    source, wide,
):
    for k, block in enumerate((in0, in1, in2, in3)):
        source[64 * k : 64 * k + 64, :] = block[...]
    wide[...] = far_in[...].astype(f32)
    gather_far(wide, source, 256)
    owners = jnp.concatenate([put(halo, 0, 2, 0, 128), put(far, 0, 4, 0, 128)], axis=1)
    cot_sender = (sender_own[...] + dot(owners, source[...])).astype(bf16)
    cot_sender_out[...] = cot_sender
    cot_middle = middle_part[...] + dot_nt(cot_sender, w4[...])
    cot_middle_out[...] = cot_middle
    cot_middle = stack_halves(cot_middle)

    def step(i, s):
        receiver = pick(target, ROWS * i, ROWS, 0, 128)
        normed, inverse = norm_parts(linear[s, :])
        cot = norm_back(normed, inverse, dot(twice(receiver), cot_middle)).astype(bf16)
        elinear_out[s, :] = cot
        upper_out[s, :] = (dot_nt(cot, w2[...]) * slope(pre[s, :])).astype(bf16)
        elinear_out.send(s)
        upper_out.send(s)

    chunks(1024 // CHUNK, step)
    for k, out in enumerate((g0, g1, g2, g3)):
        spread = put(slot, 0, 8, 512 + 256 * k, 256)
        out[...] = dot(spread, upper_out[...]).astype(bf16)
        out.send()


def encode_grads_body(
    scales, core, upper, slot, target, cot_middle, mesh, middle, cot_sender, hidden, elinear, w1,
    grid_own, mesh_grad, grads_own, grads_other, held,
):
    def store(k, x, y, scale):
        store_blocks(grads_own, grads_other, k, dot_tn(x, y) * scale, held, core)

    store(1, hidden[...], elinear[...], scales[1])
    store(2, middle[...], cot_sender[...], scales[2])
    receive = dot(put(target, 0, 8, 0, 128), upper[...]).astype(bf16)
    store(0, mesh[...], receive, scales[0])
    mesh_grad[...] = (cot_middle[...] + dot_nt(receive, w1[...])).astype(bf16)
    for k in range(2):
        grid_own[256 * k : 256 * k + 256, :] = dot(put(slot, 0, 8, 256 * k, 256), upper[...])


def grid_back_body(scales, core, grid_own, in0, in1, in2, in3, table, grid, w0, grid_grad, grads_own, grads_other, cot, held):
    for i in range(2):
        s = slice(256 * i, 256 * i + 256)
        total = grid_own[s, :]
        for k, block in enumerate((in0, in1, in2, in3)):
            total = total + dot(put_rows(table_rows(table, k), i * 256, 256), block[...])
        total = total.astype(bf16)
        cot[s, :] = total
        grid_grad[s, :] = dot_nt(total, w0[...]).astype(bf16)
    store_blocks(grads_own, grads_other, 0, dot_tn(grid[...], cot[...]) * scales[0], held, core)


def pair_body(*refs):
    out = refs[-1]
    place = 0
    for own, got in zip(refs[0:-1:2], refs[1:-1:2]):
        for k in range(own.shape[2]):
            out[:, :, place] = (own[:, :, k].astype(f32) + got[:, :, k].astype(f32)).astype(bf16)
            place += 1


def sum_body(terms, *shard):
    total = terms[0].astype(f32)
    for d in range(1, terms.shape[0]):
        total = total + terms[d].astype(f32)
    total = total.astype(bf16)
    if len(shard[0].shape) == 2:
        shard[0][...] = total
    else:
        for p in range(shard[0].shape[0]):
            shard[0][p] = total


def place_early_body(core, own, other, out):
    first = core[0] == 0
    for q in range(2):
        a, b = own[:, q].reshape(512, 128), other[:, q].reshape(512, 128)
        out[:, 128 * q : 128 * q + 128] = jnp.where(first, a, b)
        out[:, 256 + 128 * q : 384 + 128 * q] = jnp.where(first, b, a)


def place_late_body(core, own, other, kept, out):
    del kept
    place_early_body(core, own, other, out)


def swapped(value):
    return lax.ppermute(value, "core", [(0, 1), (1, 0)])


def scaled(body, scales):
    return functools.partial(body, scales)


def on_device(
    grid_latent, mesh_latent, edge_latent, mesh_cotangent, edge_cotangent, grid_send, grid_slot, grid_target,
    mesh_halo, mesh_send, mesh_slot, mesh_target, weights,
):
    peers = lax.axis_size(AXES)
    mesh_rows, latent = mesh_latent.shape
    edges = grid_slot.shape[0]
    grid_scale = 1.0 / (edges * peers) ** 0.5
    edge_scale = 1.0 / (mesh_slot.shape[0] * peers) ** 0.5
    node_scale = 1.0 / (mesh_rows * peers) ** 0.5
    grid_table = grid_send
    core = lax.axis_index("core").reshape(1)
    halo_table = mesh_halo.reshape(2, 128)
    far_table = mesh_send[0].T
    gslot, gtarget = grid_slot.reshape(8, 128), grid_target.reshape(8, 128)
    mslot, mtarget = mesh_slot.reshape(8, 128), mesh_target.reshape(8, 128)
    big, small, halo = (edges, latent), (mesh_rows, latent), (64, latent)
    vm = pltpu.VMEM

    project, *outgoing = call(
        project_body, [((512, latent), bf16)] + [((256, latent), bf16)] * 4,
        (grid_latent, grid_table), weights, (0,),
    )
    arrived = outgoing_rows(outgoing)
    (own,) = call(
        encode_own_body, [(big, f32)], (project, gslot, gtarget, mesh_latent),
        weights, (1,), scratch=(vm((768, latent), bf16),), flops=10**9,
    )
    pre, linear, hidden, middle, sender, *halos, far_out = call(
        encode_body,
        [(big, f32), (big, f32), (big, bf16), (small, bf16), (small, bf16)] + [(halo, bf16)] * 4 + [((2048, 128), bf16)],
        (own, *arrived, gslot, gtarget, mesh_latent, halo_table, far_table), weights, (2, 4),
        scratch=(vm(small, f32), vm((2048, 128), f32)), flops=2 * 10**9,
    )
    far_in = lax.all_to_all(far_out.reshape(peers, 16, 128), AXES, 0, 0, tiled=True).reshape(2048, 128)
    halo_in = outgoing_rows(halos)
    own, update_own = call(
        process_own_body, [(big, f32), (small, f32)], (middle, sender, edge_latent, mslot, mtarget),
        weights, (3, 5, 7), scratch=(vm((384, latent), bf16),), flops=2 * 10**9,
    )
    (
        mesh_update, phidden, rounded, uhidden, cot_linear, cot_update, plinear, cround, receive, sender_own,
        *halos, far_out,
    ) = call(
        process_body,
        [(small, bf16), (big, bf16)] + [(small, bf16)] * 4 + [(big, bf16)] * 2
        + [(small, bf16), (small, f32)] + [(halo, bf16)] * 4 + [((2048, 128), bf16)],
        (own, *halo_in, far_in, mslot, mtarget, middle, update_own, mesh_cotangent, edge_cotangent),
        weights, (6, 8, 9),
        scratch=(
            vm((768, latent), bf16), vm(big, f32), vm(big, f32), vm((edges, 128), f32),
            vm(small, f32), vm((2048, 128), f32), vm((8, 128), jnp.int32),
        ),
        flops=8 * 10**9, late=(8, 9, 10, 11),
    )
    far_back = lax.all_to_all(far_out.reshape(peers, 16, 128), AXES, 0, 0, tiled=True).reshape(2048, 128)
    halo_back = returned_rows(halos)

    def blocks(count):
        return ((32, 2, count, 16, 128), bf16)

    held = vm((latent, latent), bf16)
    edge_grad, middle_part, early_own, early_other = call(
        scaled(process_grads_body, [edge_scale] * 3 + [node_scale] * 3),
        [(big, bf16), (small, f32), blocks(6), blocks(6)],
        (core, edge_latent, cround, phidden, plinear, middle, receive, cot_update, rounded, uhidden, cot_linear,
         edge_cotangent, mesh_cotangent),
        weights, (3, 5, 7), scratch=(held,), flops=3 * 10**9, late=(11, 12),
    )
    early = (early_own.astype(f32) + swapped(early_other).astype(f32)).astype(bf16)
    early, _ = lax.optimization_barrier((early, (halo_back, far_back)))
    early = lax.all_to_all(early.reshape(64, 96, 128), CHIPS, 0, 0, tiled=True)
    cot_sender, cot_middle, elinear, upper, *partials = call(
        encode_back_body,
        [(small, bf16), (small, f32), (big, bf16), (big, bf16)] + [((256, latent), bf16)] * 4,
        (*halo_back, far_back, halo_table, far_table, sender_own, middle_part, pre, linear, gslot, gtarget),
        weights, (2, 4), scratch=(vm((768, latent), bf16), vm((2048, 128), f32)), flops=4 * 10**9,
    )
    partials = returned_rows(partials)
    grid_own, mesh_grad, late_own, late_other = call(
        scaled(encode_grads_body, [grid_scale, grid_scale, edge_scale]),
        [((512, latent), f32), (small, bf16), blocks(3), blocks(3)],
        (core, upper, gslot, gtarget, cot_middle, mesh_latent, middle, cot_sender, hidden, elinear),
        weights, (1,), scratch=(held,), flops=2 * 10**9,
    )
    (early,) = call(sum_body, [((64, 96, 128), bf16)], (early,), flops=10**7)
    early = lax.all_to_all(early, CHIPS, 0, 0, tiled=True)
    grid_grad, last_own, last_other = call(
        scaled(grid_back_body, [grid_scale]), [((512, latent), bf16), blocks(1), blocks(1)],
        (core, grid_own, *partials, grid_table, grid_latent), weights, (0,),
        scratch=(vm((512, latent), bf16), held),
    )
    (late,) = call(
        pair_body, [blocks(4)], (last_own, swapped(last_other), late_own, swapped(late_other)),
        flops=10**6,
    )
    late, early = lax.optimization_barrier((late, early))
    late = lax.all_to_all(late.reshape(64, 64, 128), CHIPS, 0, 0, tiled=True)
    early_swapped = swapped(early).reshape(blocks(6)[0])
    early = early.reshape(blocks(6)[0])
    placed = pl.pallas_call(
        place_early_body,
        grid_spec=pltpu.PrefetchScalarGridSpec(
            num_scalar_prefetch=1,
            grid=(6,),
            in_specs=[pl.BlockSpec((32, 2, None, 16, 128), lambda i, c: (0, 0, i, 0, 0))] * 2,
            out_specs=pl.BlockSpec((None, latent, latent), lambda i, c: (i + 3 + (i + 5) // 6, 0, 0)),
        ),
        out_shape=jax.ShapeDtypeStruct(weights.shape, bf16),
        compiler_params=pltpu.CompilerParams(vmem_limit_bytes=67000000),
        name="place_early",
    )(core, early, early_swapped)
    (late,) = call(sum_body, [((64, 64, 128), bf16)], (late,), flops=10**7)
    late = lax.all_to_all(late, CHIPS, 0, 0, tiled=True)
    other = swapped(late).reshape(blocks(4)[0])
    late = late.reshape(blocks(4)[0])
    weight_grads = pl.pallas_call(
        place_late_body,
        grid_spec=pltpu.PrefetchScalarGridSpec(
            num_scalar_prefetch=1,
            grid=(4,),
            in_specs=[pl.BlockSpec((32, 2, None, 16, 128), lambda i, c: (0, 0, i, 0, 0))] * 2
            + [pl.BlockSpec(memory_space=pl.ANY)],
            out_specs=pl.BlockSpec((None, latent, latent), lambda i, c: (i + i // 3, 0, 0)),
        ),
        out_shape=jax.ShapeDtypeStruct(weights.shape, bf16),
        input_output_aliases={3: 0},
        compiler_params=pltpu.CompilerParams(vmem_limit_bytes=67000000),
        name="place_late",
    )(core, late, other, placed)
    return (mesh_update, grid_grad, mesh_grad, edge_grad, weight_grads)


def solution(mesh):
    row = P(AXES, None)
    wide = jax.sharding.Mesh(mesh.devices.reshape(4, 2, 4, 4), AXES)

    return jax.shard_map(
        on_device,
        mesh=wide,
        in_specs=(row, row, row, row, row, P(AXES, None, None), P(AXES), P(AXES), P(AXES, None, None),
                  P(AXES, None, None), P(AXES), P(AXES), P()),
        out_specs=(row, row, row, row, P()),
        check_vma=False,
    )
```

```python
import functools

import jax
import jax.numpy as jnp
from jax import lax
from jax.experimental import pallas as pl
from jax.experimental.pallas import tpu as pltpu
from jax.sharding import PartitionSpec as P


norm_eps = 1e-05
f32 = jnp.float32
bf16 = jnp.bfloat16
AXES = ("x", "core", "y", "z")
CHIPS = ("x", "y", "z")
FACE = ("x", "core")
SUB = ("y", "z")
CHUNK = 512
ROWS = CHUNK // 128


def shifted(value, axis, steps):
    count = lax.axis_size(axis)
    pairs = [(source, (source + steps) % count) for source in range(count)]
    return lax.ppermute(value, axis, pairs)


def outgoing_rows(blocks):
    routes = ((SUB, 1), (SUB, -1), (FACE, 1), (FACE, -1))
    return [shifted(block, axis, step) for block, (axis, step) in zip(blocks, routes)]


def returned_rows(blocks):
    routes = ((SUB, -1), (SUB, 1), (FACE, -1), (FACE, 1))
    return [shifted(block, axis, step) for block, (axis, step) in zip(blocks, routes)]


def dot(a, b):
    return jnp.dot(a, b, preferred_element_type=f32)


def dot_nt(a, b):
    return lax.dot_general(a, b, (((1,), (1,)), ((), ())), preferred_element_type=f32)


def dot_tn(a, b):
    return lax.dot_general(a, b, (((0,), (0,)), ((), ())), preferred_element_type=f32)


def halves(values):
    upper = values.astype(bf16)
    return upper, (values - upper.astype(f32)).astype(bf16)


def mean(values):
    return jnp.sum(values, axis=-1, keepdims=True) * (1.0 / values.shape[-1])


def norm_parts(values):
    centre = values - mean(values)
    inverse = lax.rsqrt(mean(centre * centre) + norm_eps)
    return centre * inverse, inverse


def norm_back(normed, inverse, upstream):
    return inverse * (upstream - mean(upstream) - normed * mean(upstream * normed))


def sigmoid(values):
    return 1.0 / (1.0 + jnp.exp(-values))


def silu(values):
    return values * sigmoid(values)


def slope(values):
    s = sigmoid(values)
    return s * (1.0 + values * (1.0 - s))


def pick_rows(row, offset, count):
    column = jnp.transpose(jnp.broadcast_to(row, (128, 128))) - offset
    lane = lax.broadcasted_iota(jnp.int32, (128, 128), 1)
    return jnp.concatenate(
        [jnp.where(column == lane + 128 * b, 1.0, 0.0).astype(bf16) for b in range(count // 128)],
        axis=1,
    )


def pick(ref, first, rows, offset, count):
    return jnp.concatenate(
        [pick_rows(ref[pl.ds(first + r, 1), :], offset, count) for r in range(rows)], axis=0
    )


def put(ref, first, rows, offset, count):
    return put_rows([ref[pl.ds(first + r, 1), :] for r in range(rows)], offset, count)


def table_rows(table, k):
    return [table[0, k : k + 1, 128 * h : 128 * h + 128] for h in range(2)]


def put_rows(rows, offset, count):
    place = lax.broadcasted_iota(jnp.int32, (count, 128), 0) + offset
    return jnp.concatenate(
        [jnp.where(place == jnp.broadcast_to(row, (count, 128)), 1.0, 0.0).astype(bf16) for row in rows], axis=1
    )


def stack_halves(values):
    return jnp.concatenate(halves(values), axis=0)


def twice(values):
    return jnp.concatenate([values, values], axis=1)


def chunks(count, body):
    def step(i, carry):
        body(i, pl.ds(pl.multiple_of(i * CHUNK, CHUNK), CHUNK))
        return carry

    lax.fori_loop(0, count, step, 0)


def call(body, outs, args, weights=None, picks=(), scratch=(), flops=10**9, vmem=67000000):
    def whole(shape):
        return pl.BlockSpec(shape, lambda i: (0,) * len(shape))

    in_specs = [pl.BlockSpec(memory_space=pltpu.SMEM) if a.shape == (1,) else whole(a.shape) for a in args]
    for k in picks:
        in_specs.append(
            pl.BlockSpec((None, weights.shape[1], weights.shape[2]), functools.partial(lambda k, i: (k, 0, 0), k))
        )
    shapes = [jax.ShapeDtypeStruct(s, d) for s, d in outs]
    total = sum(a.size * a.dtype.itemsize for a in args) + sum(s.size * s.dtype.itemsize for s in shapes)
    total += len(picks) * 512 * 1024
    return pl.pallas_call(
        body,
        grid=(1,),
        out_shape=shapes,
        in_specs=in_specs,
        out_specs=[whole(s.shape) for s in shapes],
        scratch_shapes=list(scratch),
        compiler_params=pltpu.CompilerParams(vmem_limit_bytes=vmem),
        cost_estimate=pl.CostEstimate(flops=flops, bytes_accessed=total, transcendentals=0),
    )(*args, *([weights] * len(picks)))


def project_body(grid, table, w0, project, out0, out1, out2, out3):
    chunks(512 // CHUNK, lambda i, s: project.__setitem__((s, slice(None)), dot(grid[s, :], w0[...]).astype(bf16)))
    for k, out in enumerate((out0, out1, out2, out3)):
        picked = jnp.concatenate([pick_rows(row, 0, 512) for row in table_rows(table, k)], axis=0)
        out[...] = dot(picked, project[...]).astype(bf16)


def encode_own_body(project, slot, target, mesh, w1, own, source):
    source[0:512, :] = project[...]
    source[512:768, :] = stack_halves(dot(mesh[...], w1[...]))

    def step(i, s):
        receiver = pick(target, ROWS * i, ROWS, 0, 128)
        own[s, :] = dot(jnp.concatenate([pick(slot, ROWS * i, ROWS, 0, 512), twice(receiver)], axis=1), source[...])

    chunks(1024 // CHUNK, step)


def far_slots(slot):
    far = slot - 384
    return jnp.where(slot < 384, slot, 384 + (far & 3) * 128 + (far >> 2))


def encode_body(
    own, in0, in1, in2, in3, slot, target, mesh, halo, far, w2, w4,
    pre_out, linear_out, hidden_out, middle_out, sender_out, h0, h1, h2, h3, far_out,
    total, wide,
):
    total[...] = jnp.zeros_like(total)

    def step(i, s):
        pre = own[s, :]
        for k, block in enumerate((in0, in1, in2, in3)):
            pre = pre + dot(pick(slot, ROWS * i, ROWS, 512 + 256 * k, 256), block[...])
        pre_out[s, :] = pre
        hidden = silu(pre).astype(bf16)
        hidden_out[s, :] = hidden
        linear = dot(hidden, w2[...])
        linear_out[s, :] = linear
        message = norm_parts(linear)[0].astype(bf16)
        total[...] += dot(put(target, ROWS * i, ROWS, 0, 128), message)

    chunks(1024 // CHUNK, step)
    middle = (mesh[...].astype(f32) + total[...]).astype(bf16)
    middle_out[...] = middle
    sender = dot(middle, w4[...]).astype(bf16)
    sender_out[...] = sender
    rows = dot(pick(halo, 0, 2, 0, 128), sender).astype(bf16)
    for k, out in enumerate((h0, h1, h2, h3)):
        out[...] = rows[64 * k : 64 * k + 64, :]
    for r in range(4):
        picked = dot(pick(far, r, 1, 0, 128), sender)
        for c in range(4):
            wide[pl.ds(4 * c + r, 128, stride=16), :] = picked[:, 128 * c : 128 * c + 128]
    far_out[...] = wide[...].astype(bf16)


def process_own_body(middle, sender, edge, slot, target, w3, w5, w7, own, update_own, source):
    source[0:128, :] = sender[...]
    source[128:384, :] = stack_halves(dot(middle[...], w5[...]))
    update_own[...] = dot(middle[...], w7[...])

    def step(i, s):
        receiver = pick(target, ROWS * i, ROWS, 0, 128)
        picked = jnp.concatenate([pick(slot, ROWS * i, ROWS, 0, 128), twice(receiver)], axis=1)
        own[s, :] = dot(edge[s, :], w3[...]) + dot(picked, source[...])

    chunks(1024 // CHUNK, step)


def gather_far(wide, source, first):
    for r in range(4):
        for c in range(4):
            source[first + 128 * r : first + 128 * r + 128, 128 * c : 128 * c + 128] = wide[
                pl.ds(4 * c + r, 128, stride=16), :
            ].astype(bf16)


def process_body(
    own, in0, in1, in2, in3, far_in, slot, target, middle, update_own, mesh_cot, edge_cot, w6, w8, w9,
    mesh_update, hidden_out, round_out, uhidden_out, cot_linear_out, cot_update_out, plinear_out, cround_out,
    receive_out, sender_own, h0, h1, h2, h3, far_out,
    source, pre_s, normed_s, inverse_s, total, wide, slots,
):
    slots[...] = far_slots(slot[...])
    for k, block in enumerate((in0, in1, in2, in3)):
        source[64 * k : 64 * k + 64, :] = block[...]
    wide[...] = far_in[...].astype(f32)
    gather_far(wide, source, 256)
    total[...] = jnp.zeros_like(total)

    def forward(i, s):
        pre = own[s, :] + dot(pick(slots, ROWS * i, ROWS, 128, 768), source[...])
        pre_s[s, :] = pre
        hidden = silu(pre).astype(bf16)
        hidden_out[s, :] = hidden
        normed, inverse = norm_parts(dot(hidden, w6[...]))
        normed_s[s, :] = normed
        inverse_s[s, :] = jnp.broadcast_to(inverse, (CHUNK, 128))
        total[...] += dot(put(target, ROWS * i, ROWS, 0, 128), normed.astype(bf16))

    chunks(1024 // CHUNK, forward)
    rounded = total[...].astype(bf16)
    round_out[...] = rounded
    pre = update_own[...] + dot(rounded, w8[...])
    uhidden = silu(pre).astype(bf16)
    uhidden_out[...] = uhidden
    normed, inverse = norm_parts(dot(uhidden, w9[...]))
    mesh_update[...] = (middle[...].astype(f32) + normed).astype(bf16)
    cot_linear = norm_back(normed, inverse, mesh_cot[...].astype(f32)).astype(bf16)
    cot_linear_out[...] = cot_linear
    cot_update = (dot_nt(cot_linear, w9[...]) * slope(pre)).astype(bf16)
    cot_update_out[...] = cot_update
    cot_total = stack_halves(dot_nt(cot_update, w8[...]))

    def backward(i, s):
        receiver = pick(target, ROWS * i, ROWS, 0, 128)
        upstream = dot(twice(receiver), cot_total) + edge_cot[s, :].astype(f32)
        cot = norm_back(normed_s[s, :], inverse_s[s, 0:1], upstream).astype(bf16)
        plinear_out[s, :] = cot
        cround_out[s, :] = (dot_nt(cot, w6[...]) * slope(pre_s[s, :])).astype(bf16)

    chunks(1024 // CHUNK, backward)
    kept = jnp.concatenate([put(target, 0, 8, 0, 128), put(slots, 0, 8, 0, 128)], axis=0)
    kept = dot(kept, cround_out[...])
    receive_out[...] = kept[0:128, :].astype(bf16)
    sender_own[...] = kept[128:256, :]
    spread = put(slots, 0, 8, 128, 256)
    spread = dot(spread, cround_out[...]).astype(bf16)
    for k, out in enumerate((h0, h1, h2, h3)):
        out[...] = spread[64 * k : 64 * k + 64, :]
    for half in range(2):
        spread = put(slots, 0, 8, 384 + 256 * half, 256)
        spread = dot(spread, cround_out[...])
        for q in range(2):
            for c in range(4):
                wide[pl.ds(4 * c + 2 * half + q, 128, stride=16), :] = spread[
                    128 * q : 128 * q + 128, 128 * c : 128 * c + 128
                ]
    far_out[...] = wide[...].astype(bf16)


def store_blocks(own, other, k, term, held, core):
    held[...] = term.astype(bf16)
    for q in range(2):
        for out, c in ((own, core[0]), (other, 1 - core[0])):
            columns = pl.ds(pl.multiple_of(256 * c + 128 * q, 128), 128)
            out[:, q, k, :, :] = held[:, columns].reshape(32, 16, 128)


def process_grads_body(
    scales, core, edge, cround, hidden, plinear, middle, receive, cot_update, rounded, uhidden, cot_linear,
    grads_own, grads_other, held,
):
    pairs = ((edge, cround), (middle, receive), (hidden, plinear), (middle, cot_update), (rounded, cot_update), (uhidden, cot_linear))
    for k, (x, y) in enumerate(pairs):
        store_blocks(grads_own, grads_other, k, dot_tn(x[...], y[...]) * scales[k], held, core)


def edge_back_body(cround, edge_cot, receive, cot_update, mesh_cot, w3, w5, w7, edge_grad, middle_part):
    middle_part[...] = mesh_cot[...].astype(f32) + dot_nt(cot_update[...], w7[...]) + dot_nt(receive[...], w5[...])

    def step(i, s):
        edge_grad[s, :] = (edge_cot[s, :].astype(f32) + dot_nt(cround[s, :], w3[...])).astype(bf16)

    chunks(1024 // CHUNK, step)


def encode_back_body(
    in0, in1, in2, in3, far_in, halo, far, sender_own, middle_part, pre, linear, slot, target, w2, w4,
    cot_sender_out, cot_middle_out, elinear_out, upper_out, g0, g1, g2, g3,
    source, wide,
):
    for k, block in enumerate((in0, in1, in2, in3)):
        source[64 * k : 64 * k + 64, :] = block[...]
    wide[...] = far_in[...].astype(f32)
    gather_far(wide, source, 256)
    owners = jnp.concatenate([put(halo, 0, 2, 0, 128), put(far, 0, 4, 0, 128)], axis=1)
    cot_sender = (sender_own[...] + dot(owners, source[...])).astype(bf16)
    cot_sender_out[...] = cot_sender
    cot_middle = middle_part[...] + dot_nt(cot_sender, w4[...])
    cot_middle_out[...] = cot_middle
    cot_middle = stack_halves(cot_middle)

    def step(i, s):
        receiver = pick(target, ROWS * i, ROWS, 0, 128)
        normed, inverse = norm_parts(linear[s, :])
        cot = norm_back(normed, inverse, dot(twice(receiver), cot_middle)).astype(bf16)
        elinear_out[s, :] = cot
        upper_out[s, :] = (dot_nt(cot, w2[...]) * slope(pre[s, :])).astype(bf16)

    chunks(1024 // CHUNK, step)
    for k, out in enumerate((g0, g1, g2, g3)):
        spread = put(slot, 0, 8, 512 + 256 * k, 256)
        out[...] = dot(spread, upper_out[...]).astype(bf16)


def encode_grads_body(
    scales, core, upper, slot, target, cot_middle, mesh, middle, cot_sender, hidden, elinear, w1,
    grid_own, mesh_grad, grads_own, grads_other, held,
):
    def store(k, x, y, scale):
        store_blocks(grads_own, grads_other, k, dot_tn(x, y) * scale, held, core)

    store(1, hidden[...], elinear[...], scales[1])
    store(2, middle[...], cot_sender[...], scales[2])
    receive = dot(put(target, 0, 8, 0, 128), upper[...]).astype(bf16)
    store(0, mesh[...], receive, scales[0])
    mesh_grad[...] = (cot_middle[...] + dot_nt(receive, w1[...])).astype(bf16)
    for k in range(2):
        grid_own[256 * k : 256 * k + 256, :] = dot(put(slot, 0, 8, 256 * k, 256), upper[...])


def grid_back_body(scales, core, grid_own, in0, in1, in2, in3, table, grid, w0, grid_grad, grads_own, grads_other, cot, held):
    for i in range(2):
        s = slice(256 * i, 256 * i + 256)
        total = grid_own[s, :]
        for k, block in enumerate((in0, in1, in2, in3)):
            total = total + dot(put_rows(table_rows(table, k), i * 256, 256), block[...])
        total = total.astype(bf16)
        cot[s, :] = total
        grid_grad[s, :] = dot_nt(total, w0[...]).astype(bf16)
    store_blocks(grads_own, grads_other, 0, dot_tn(grid[...], cot[...]) * scales[0], held, core)


def pair_body(*refs):
    out = refs[-1]
    place = 0
    for own, got in zip(refs[0:-1:2], refs[1:-1:2]):
        for k in range(own.shape[2]):
            out[:, :, place] = (own[:, :, k].astype(f32) + got[:, :, k].astype(f32)).astype(bf16)
            place += 1


def sum_body(terms, *shard):
    total = terms[0].astype(f32)
    for d in range(1, terms.shape[0]):
        total = total + terms[d].astype(f32)
    total = total.astype(bf16)
    if len(shard[0].shape) == 2:
        shard[0][...] = total
    else:
        for p in range(shard[0].shape[0]):
            shard[0][p] = total


def place_early_body(core, own, other, out):
    first = core[0] == 0
    for q in range(2):
        a, b = own[:, q].reshape(512, 128), other[:, q].reshape(512, 128)
        out[:, 128 * q : 128 * q + 128] = jnp.where(first, a, b)
        out[:, 256 + 128 * q : 384 + 128 * q] = jnp.where(first, b, a)


def place_late_body(core, own, other, kept, out):
    del kept
    place_early_body(core, own, other, out)


def swapped(value):
    return lax.ppermute(value, "core", [(0, 1), (1, 0)])


def scaled(body, scales):
    return functools.partial(body, scales)


def on_device(
    grid_latent, mesh_latent, edge_latent, mesh_cotangent, edge_cotangent, grid_send, grid_slot, grid_target,
    mesh_halo, mesh_send, mesh_slot, mesh_target, weights,
):
    peers = lax.axis_size(AXES)
    mesh_rows, latent = mesh_latent.shape
    edges = grid_slot.shape[0]
    grid_scale = 1.0 / (edges * peers) ** 0.5
    edge_scale = 1.0 / (mesh_slot.shape[0] * peers) ** 0.5
    node_scale = 1.0 / (mesh_rows * peers) ** 0.5
    grid_table = grid_send
    core = lax.axis_index("core").reshape(1)
    halo_table = mesh_halo.reshape(2, 128)
    far_table = mesh_send[0].T
    gslot, gtarget = grid_slot.reshape(8, 128), grid_target.reshape(8, 128)
    mslot, mtarget = mesh_slot.reshape(8, 128), mesh_target.reshape(8, 128)
    big, small, halo = (edges, latent), (mesh_rows, latent), (64, latent)
    vm = pltpu.VMEM

    project, *outgoing = call(
        project_body, [((512, latent), bf16)] + [((256, latent), bf16)] * 4,
        (grid_latent, grid_table), weights, (0,),
    )
    arrived = outgoing_rows(outgoing)
    (own,) = call(
        encode_own_body, [(big, f32)], (project, gslot, gtarget, mesh_latent),
        weights, (1,), scratch=(vm((768, latent), bf16),), flops=10**9,
    )
    pre, linear, hidden, middle, sender, *halos, far_out = call(
        encode_body,
        [(big, f32), (big, f32), (big, bf16), (small, bf16), (small, bf16)] + [(halo, bf16)] * 4 + [((2048, 128), bf16)],
        (own, *arrived, gslot, gtarget, mesh_latent, halo_table, far_table), weights, (2, 4),
        scratch=(vm(small, f32), vm((2048, 128), f32)), flops=2 * 10**9,
    )
    far_in = lax.all_to_all(far_out.reshape(peers, 16, 128), AXES, 0, 0, tiled=True).reshape(2048, 128)
    halo_in = outgoing_rows(halos)
    own, update_own = call(
        process_own_body, [(big, f32), (small, f32)], (middle, sender, edge_latent, mslot, mtarget),
        weights, (3, 5, 7), scratch=(vm((384, latent), bf16),), flops=2 * 10**9,
    )
    (
        mesh_update, phidden, rounded, uhidden, cot_linear, cot_update, plinear, cround, receive, sender_own,
        *halos, far_out,
    ) = call(
        process_body,
        [(small, bf16), (big, bf16)] + [(small, bf16)] * 4 + [(big, bf16)] * 2
        + [(small, bf16), (small, f32)] + [(halo, bf16)] * 4 + [((2048, 128), bf16)],
        (own, *halo_in, far_in, mslot, mtarget, middle, update_own, mesh_cotangent, edge_cotangent),
        weights, (6, 8, 9),
        scratch=(
            vm((768, latent), bf16), vm(big, f32), vm(big, f32), vm((edges, 128), f32),
            vm(small, f32), vm((2048, 128), f32), vm((8, 128), jnp.int32),
        ),
        flops=8 * 10**9,
    )
    far_back = lax.all_to_all(far_out.reshape(peers, 16, 128), AXES, 0, 0, tiled=True).reshape(2048, 128)
    halo_back = returned_rows(halos)

    def blocks(count):
        return ((32, 2, count, 16, 128), bf16)

    held = vm((latent, latent), bf16)
    early_own, early_other = call(
        scaled(process_grads_body, [edge_scale] * 3 + [node_scale] * 3),
        [blocks(6), blocks(6)],
        (core, edge_latent, cround, phidden, plinear, middle, receive, cot_update, rounded, uhidden, cot_linear),
        scratch=(held,), flops=2 * 10**9,
    )
    early_other = swapped(early_other)
    edge_grad, middle_part = call(
        edge_back_body, [(big, bf16), (small, f32)], (cround, edge_cotangent, receive, cot_update, mesh_cotangent),
        weights, (3, 5, 7),
    )
    early = (early_own.astype(f32) + early_other.astype(f32)).astype(bf16)
    early, _ = lax.optimization_barrier((early, (halo_back, far_back)))
    early = lax.all_to_all(early.reshape(64, 96, 128), CHIPS, 0, 0, tiled=True)
    cot_sender, cot_middle, elinear, upper, *partials = call(
        encode_back_body,
        [(small, bf16), (small, f32), (big, bf16), (big, bf16)] + [((256, latent), bf16)] * 4,
        (*halo_back, far_back, halo_table, far_table, sender_own, middle_part, pre, linear, gslot, gtarget),
        weights, (2, 4), scratch=(vm((768, latent), bf16), vm((2048, 128), f32)), flops=4 * 10**9,
    )
    partials = returned_rows(partials)
    grid_own, mesh_grad, late_own, late_other = call(
        scaled(encode_grads_body, [grid_scale, grid_scale, edge_scale]),
        [((512, latent), f32), (small, bf16), blocks(3), blocks(3)],
        (core, upper, gslot, gtarget, cot_middle, mesh_latent, middle, cot_sender, hidden, elinear),
        weights, (1,), scratch=(held,), flops=2 * 10**9,
    )
    (early,) = call(sum_body, [((64, 96, 128), bf16)], (early,), flops=10**7)
    early = lax.all_to_all(early, CHIPS, 0, 0, tiled=True)
    grid_grad, last_own, last_other = call(
        scaled(grid_back_body, [grid_scale]), [((512, latent), bf16), blocks(1), blocks(1)],
        (core, grid_own, *partials, grid_table, grid_latent), weights, (0,),
        scratch=(vm((512, latent), bf16), held),
    )
    (late,) = call(
        pair_body, [blocks(4)], (last_own, swapped(last_other), late_own, swapped(late_other)),
        flops=10**6,
    )
    late, early = lax.optimization_barrier((late, early))
    late = lax.all_to_all(late.reshape(64, 64, 128), CHIPS, 0, 0, tiled=True)
    early_swapped = swapped(early).reshape(blocks(6)[0])
    early = early.reshape(blocks(6)[0])
    placed = pl.pallas_call(
        place_early_body,
        grid_spec=pltpu.PrefetchScalarGridSpec(
            num_scalar_prefetch=1,
            grid=(6,),
            in_specs=[pl.BlockSpec((32, 2, None, 16, 128), lambda i, c: (0, 0, i, 0, 0))] * 2,
            out_specs=pl.BlockSpec((None, latent, latent), lambda i, c: (i + 3 + (i + 5) // 6, 0, 0)),
        ),
        out_shape=jax.ShapeDtypeStruct(weights.shape, bf16),
        compiler_params=pltpu.CompilerParams(vmem_limit_bytes=67000000),
        name="place_early",
    )(core, early, early_swapped)
    (late,) = call(sum_body, [((64, 64, 128), bf16)], (late,), flops=10**7)
    late = lax.all_to_all(late, CHIPS, 0, 0, tiled=True)
    other = swapped(late).reshape(blocks(4)[0])
    late = late.reshape(blocks(4)[0])
    weight_grads = pl.pallas_call(
        place_late_body,
        grid_spec=pltpu.PrefetchScalarGridSpec(
            num_scalar_prefetch=1,
            grid=(4,),
            in_specs=[pl.BlockSpec((32, 2, None, 16, 128), lambda i, c: (0, 0, i, 0, 0))] * 2
            + [pl.BlockSpec(memory_space=pl.ANY)],
            out_specs=pl.BlockSpec((None, latent, latent), lambda i, c: (i + i // 3, 0, 0)),
        ),
        out_shape=jax.ShapeDtypeStruct(weights.shape, bf16),
        input_output_aliases={3: 0},
        compiler_params=pltpu.CompilerParams(vmem_limit_bytes=12 << 20),
        name="place_late",
    )(core, late, other, placed)
    return (mesh_update, grid_grad, mesh_grad, edge_grad, weight_grads)


def solution(mesh):
    row = P(AXES, None)
    wide = jax.sharding.Mesh(mesh.devices.reshape(4, 2, 4, 4), AXES)

    return jax.shard_map(
        on_device,
        mesh=wide,
        in_specs=(row, row, row, row, row, P(AXES, None, None), P(AXES), P(AXES), P(AXES, None, None),
                  P(AXES, None, None), P(AXES), P(AXES), P()),
        out_specs=(row, row, row, row, P()),
        check_vma=False,
    )
```

```python
import functools

import jax
import jax.numpy as jnp
from jax import lax
from jax.experimental import pallas as pl
from jax.experimental.pallas import tpu as pltpu
from jax.sharding import PartitionSpec as P


norm_eps = 1e-05
f32 = jnp.float32
bf16 = jnp.bfloat16
AXES = ("x", "core", "y", "z")
CHIPS = ("x", "y", "z")
FACE = ("x", "core")
SUB = ("y", "z")
CHUNK = 512
ROWS = CHUNK // 128


def shifted(value, axis, steps):
    count = lax.axis_size(axis)
    pairs = [(source, (source + steps) % count) for source in range(count)]
    return lax.ppermute(value, axis, pairs)


def moved_rows(blocks, routes):
    arrived = {}
    for k in (2, 3, 0, 1) if routes[2][1] < 0 else (3, 2, 1, 0):
        axis, step = routes[k]
        arrived[k] = shifted(blocks[k], axis, step)
    return [arrived[k] for k in range(4)]


def outgoing_rows(blocks):
    return moved_rows(blocks, ((SUB, 1), (SUB, -1), (FACE, 1), (FACE, -1)))


def returned_rows(blocks):
    return moved_rows(blocks, ((SUB, -1), (SUB, 1), (FACE, -1), (FACE, 1)))


def dot(a, b):
    return jnp.dot(a, b, preferred_element_type=f32)


def dot_nt(a, b):
    return lax.dot_general(a, b, (((1,), (1,)), ((), ())), preferred_element_type=f32)


def dot_tn(a, b):
    return lax.dot_general(a, b, (((0,), (0,)), ((), ())), preferred_element_type=f32)


def halves(values):
    upper = values.astype(bf16)
    return upper, (values - upper.astype(f32)).astype(bf16)


def mean(values):
    return jnp.sum(values, axis=-1, keepdims=True) * (1.0 / values.shape[-1])


def norm_parts(values):
    centre = values - mean(values)
    inverse = lax.rsqrt(mean(centre * centre) + norm_eps)
    return centre * inverse, inverse


def norm_back(normed, inverse, upstream):
    return inverse * (upstream - mean(upstream) - normed * mean(upstream * normed))


def sigmoid(values):
    return 1.0 / (1.0 + jnp.exp(-values))


def silu(values):
    return values * sigmoid(values)


def slope(values):
    s = sigmoid(values)
    return s * (1.0 + values * (1.0 - s))


def pick_rows(row, offset, count):
    column = jnp.transpose(jnp.broadcast_to(row, (128, 128))) - offset
    lane = lax.broadcasted_iota(jnp.int32, (128, 128), 1)
    return jnp.concatenate(
        [jnp.where(column == lane + 128 * b, 1.0, 0.0).astype(bf16) for b in range(count // 128)],
        axis=1,
    )


def pick(ref, first, rows, offset, count):
    return jnp.concatenate(
        [pick_rows(ref[pl.ds(first + r, 1), :], offset, count) for r in range(rows)], axis=0
    )


def put(ref, first, rows, offset, count):
    return put_rows([ref[pl.ds(first + r, 1), :] for r in range(rows)], offset, count)


def table_rows(table, k):
    return [table[0, k : k + 1, 128 * h : 128 * h + 128] for h in range(2)]


def put_rows(rows, offset, count):
    place = lax.broadcasted_iota(jnp.int32, (count, 128), 0) + offset
    return jnp.concatenate(
        [jnp.where(place == jnp.broadcast_to(row, (count, 128)), 1.0, 0.0).astype(bf16) for row in rows], axis=1
    )


def stack_halves(values):
    return jnp.concatenate(halves(values), axis=0)


def twice(values):
    return jnp.concatenate([values, values], axis=1)


def chunks(count, body):
    def step(i, carry):
        body(i, pl.ds(pl.multiple_of(i * CHUNK, CHUNK), CHUNK))
        return carry

    lax.fori_loop(0, count, step, 0)


def call(body, outs, args, weights=None, picks=(), scratch=(), flops=10**9, vmem=67000000):
    def whole(shape):
        return pl.BlockSpec(shape, lambda i: (0,) * len(shape))

    in_specs = [pl.BlockSpec(memory_space=pltpu.SMEM) if a.shape == (1,) else whole(a.shape) for a in args]
    for k in picks:
        in_specs.append(
            pl.BlockSpec((None, weights.shape[1], weights.shape[2]), functools.partial(lambda k, i: (k, 0, 0), k))
        )
    shapes = [jax.ShapeDtypeStruct(s, d) for s, d in outs]
    total = sum(a.size * a.dtype.itemsize for a in args) + sum(s.size * s.dtype.itemsize for s in shapes)
    total += len(picks) * 512 * 1024
    return pl.pallas_call(
        body,
        grid=(1,),
        out_shape=shapes,
        in_specs=in_specs,
        out_specs=[whole(s.shape) for s in shapes],
        scratch_shapes=list(scratch),
        compiler_params=pltpu.CompilerParams(vmem_limit_bytes=vmem),
        cost_estimate=pl.CostEstimate(flops=flops, bytes_accessed=total, transcendentals=0),
    )(*args, *([weights] * len(picks)))


def project_body(grid, table, w0, project, out0, out1, out2, out3):
    chunks(512 // CHUNK, lambda i, s: project.__setitem__((s, slice(None)), dot(grid[s, :], w0[...]).astype(bf16)))
    for k, out in enumerate((out0, out1, out2, out3)):
        picked = jnp.concatenate([pick_rows(row, 0, 512) for row in table_rows(table, k)], axis=0)
        out[...] = dot(picked, project[...]).astype(bf16)


def encode_own_body(project, slot, target, mesh, w1, own, source):
    source[0:512, :] = project[...]
    source[512:768, :] = stack_halves(dot(mesh[...], w1[...]))

    def step(i, s):
        receiver = pick(target, ROWS * i, ROWS, 0, 128)
        own[s, :] = dot(jnp.concatenate([pick(slot, ROWS * i, ROWS, 0, 512), twice(receiver)], axis=1), source[...])

    chunks(1024 // CHUNK, step)


def far_slots(slot):
    far = slot - 384
    return jnp.where(slot < 384, slot, 384 + (far & 3) * 128 + (far >> 2))


def encode_body(
    own, in0, in1, in2, in3, slot, target, mesh, halo, far, w2, w4,
    pre_out, linear_out, hidden_out, middle_out, sender_out, h0, h1, h2, h3, far_out,
    total, wide,
):
    total[...] = jnp.zeros_like(total)

    def step(i, s):
        pre = own[s, :]
        for k, block in enumerate((in0, in1, in2, in3)):
            pre = pre + dot(pick(slot, ROWS * i, ROWS, 512 + 256 * k, 256), block[...])
        pre_out[s, :] = pre
        hidden = silu(pre).astype(bf16)
        hidden_out[s, :] = hidden
        linear = dot(hidden, w2[...])
        linear_out[s, :] = linear
        message = norm_parts(linear)[0].astype(bf16)
        total[...] += dot(put(target, ROWS * i, ROWS, 0, 128), message)

    chunks(1024 // CHUNK, step)
    middle = (mesh[...].astype(f32) + total[...]).astype(bf16)
    middle_out[...] = middle
    sender = dot(middle, w4[...]).astype(bf16)
    sender_out[...] = sender
    rows = dot(pick(halo, 0, 2, 0, 128), sender).astype(bf16)
    for k, out in enumerate((h0, h1, h2, h3)):
        out[...] = rows[64 * k : 64 * k + 64, :]
    for r in range(4):
        picked = dot(pick(far, r, 1, 0, 128), sender)
        for c in range(4):
            wide[pl.ds(4 * c + r, 128, stride=16), :] = picked[:, 128 * c : 128 * c + 128]
    far_out[...] = wide[...].astype(bf16)


def process_own_body(middle, sender, edge, slot, target, w3, w5, w7, own, update_own, source):
    source[0:128, :] = sender[...]
    source[128:384, :] = stack_halves(dot(middle[...], w5[...]))
    update_own[...] = dot(middle[...], w7[...])

    def step(i, s):
        receiver = pick(target, ROWS * i, ROWS, 0, 128)
        picked = jnp.concatenate([pick(slot, ROWS * i, ROWS, 0, 128), twice(receiver)], axis=1)
        own[s, :] = dot(edge[s, :], w3[...]) + dot(picked, source[...])

    chunks(1024 // CHUNK, step)


def gather_far(wide, source, first):
    for r in range(4):
        for c in range(4):
            source[first + 128 * r : first + 128 * r + 128, 128 * c : 128 * c + 128] = wide[
                pl.ds(4 * c + r, 128, stride=16), :
            ].astype(bf16)


def process_body(
    own, in0, in1, in2, in3, far_in, slot, target, middle, update_own, mesh_cot, edge_cot, w6, w8, w9,
    mesh_update, hidden_out, round_out, uhidden_out, cot_linear_out, cot_update_out, plinear_out, cround_out,
    receive_out, sender_own, h0, h1, h2, h3, far_out,
    source, pre_s, normed_s, inverse_s, total, wide, slots,
):
    slots[...] = far_slots(slot[...])
    for k, block in enumerate((in0, in1, in2, in3)):
        source[64 * k : 64 * k + 64, :] = block[...]
    wide[...] = far_in[...].astype(f32)
    gather_far(wide, source, 256)
    total[...] = jnp.zeros_like(total)

    def forward(i, s):
        pre = own[s, :] + dot(pick(slots, ROWS * i, ROWS, 128, 768), source[...])
        pre_s[s, :] = pre
        hidden = silu(pre).astype(bf16)
        hidden_out[s, :] = hidden
        normed, inverse = norm_parts(dot(hidden, w6[...]))
        normed_s[s, :] = normed
        inverse_s[s, :] = jnp.broadcast_to(inverse, (CHUNK, 128))
        total[...] += dot(put(target, ROWS * i, ROWS, 0, 128), normed.astype(bf16))

    chunks(1024 // CHUNK, forward)
    rounded = total[...].astype(bf16)
    round_out[...] = rounded
    pre = update_own[...] + dot(rounded, w8[...])
    uhidden = silu(pre).astype(bf16)
    uhidden_out[...] = uhidden
    normed, inverse = norm_parts(dot(uhidden, w9[...]))
    mesh_update[...] = (middle[...].astype(f32) + normed).astype(bf16)
    cot_linear = norm_back(normed, inverse, mesh_cot[...].astype(f32)).astype(bf16)
    cot_linear_out[...] = cot_linear
    cot_update = (dot_nt(cot_linear, w9[...]) * slope(pre)).astype(bf16)
    cot_update_out[...] = cot_update
    cot_total = stack_halves(dot_nt(cot_update, w8[...]))

    def backward(i, s):
        receiver = pick(target, ROWS * i, ROWS, 0, 128)
        upstream = dot(twice(receiver), cot_total) + edge_cot[s, :].astype(f32)
        cot = norm_back(normed_s[s, :], inverse_s[s, 0:1], upstream).astype(bf16)
        plinear_out[s, :] = cot
        cround_out[s, :] = (dot_nt(cot, w6[...]) * slope(pre_s[s, :])).astype(bf16)

    chunks(1024 // CHUNK, backward)
    kept = jnp.concatenate([put(target, 0, 8, 0, 128), put(slots, 0, 8, 0, 128)], axis=0)
    kept = dot(kept, cround_out[...])
    receive_out[...] = kept[0:128, :].astype(bf16)
    sender_own[...] = kept[128:256, :]
    spread = put(slots, 0, 8, 128, 256)
    spread = dot(spread, cround_out[...]).astype(bf16)
    for k, out in enumerate((h0, h1, h2, h3)):
        out[...] = spread[64 * k : 64 * k + 64, :]
    for half in range(2):
        spread = put(slots, 0, 8, 384 + 256 * half, 256)
        spread = dot(spread, cround_out[...])
        for q in range(2):
            for c in range(4):
                wide[pl.ds(4 * c + 2 * half + q, 128, stride=16), :] = spread[
                    128 * q : 128 * q + 128, 128 * c : 128 * c + 128
                ]
    far_out[...] = wide[...].astype(bf16)


def store_blocks(own, other, k, term, held, core):
    held[...] = term.astype(bf16)
    for q in range(2):
        for out, c in ((own, core[0]), (other, 1 - core[0])):
            columns = pl.ds(pl.multiple_of(256 * c + 128 * q, 128), 128)
            out[:, q, k, :, :] = held[:, columns].reshape(32, 16, 128)


def process_grads_body(
    scales, core, edge, cround, hidden, plinear, middle, receive, cot_update, rounded, uhidden, cot_linear,
    grads_own, grads_other, held,
):
    pairs = ((edge, cround), (middle, receive), (hidden, plinear), (middle, cot_update), (rounded, cot_update), (uhidden, cot_linear))
    for k, (x, y) in enumerate(pairs):
        store_blocks(grads_own, grads_other, k, dot_tn(x[...], y[...]) * scales[k], held, core)


def edge_back_body(cround, edge_cot, receive, cot_update, mesh_cot, w3, w5, w7, edge_grad, middle_part):
    middle_part[...] = mesh_cot[...].astype(f32) + dot_nt(cot_update[...], w7[...]) + dot_nt(receive[...], w5[...])

    def step(i, s):
        edge_grad[s, :] = (edge_cot[s, :].astype(f32) + dot_nt(cround[s, :], w3[...])).astype(bf16)

    chunks(1024 // CHUNK, step)


def encode_back_body(
    in0, in1, in2, in3, far_in, halo, far, sender_own, middle_part, pre, linear, slot, target, w2, w4,
    cot_sender_out, cot_middle_out, elinear_out, upper_out, g0, g1, g2, g3,
    source, wide,
):
    for k, block in enumerate((in0, in1, in2, in3)):
        source[64 * k : 64 * k + 64, :] = block[...]
    wide[...] = far_in[...].astype(f32)
    gather_far(wide, source, 256)
    owners = jnp.concatenate([put(halo, 0, 2, 0, 128), put(far, 0, 4, 0, 128)], axis=1)
    cot_sender = (sender_own[...] + dot(owners, source[...])).astype(bf16)
    cot_sender_out[...] = cot_sender
    cot_middle = middle_part[...] + dot_nt(cot_sender, w4[...])
    cot_middle_out[...] = cot_middle
    cot_middle = stack_halves(cot_middle)

    def step(i, s):
        receiver = pick(target, ROWS * i, ROWS, 0, 128)
        normed, inverse = norm_parts(linear[s, :])
        cot = norm_back(normed, inverse, dot(twice(receiver), cot_middle)).astype(bf16)
        elinear_out[s, :] = cot
        upper_out[s, :] = (dot_nt(cot, w2[...]) * slope(pre[s, :])).astype(bf16)

    chunks(1024 // CHUNK, step)
    for k, out in enumerate((g0, g1, g2, g3)):
        spread = put(slot, 0, 8, 512 + 256 * k, 256)
        out[...] = dot(spread, upper_out[...]).astype(bf16)


def encode_grads_body(
    scales, core, upper, slot, target, cot_middle, mesh, middle, cot_sender, hidden, elinear, w1,
    grid_own, mesh_grad, grads_own, grads_other, held,
):
    def store(k, x, y, scale):
        store_blocks(grads_own, grads_other, k, dot_tn(x, y) * scale, held, core)

    store(1, hidden[...], elinear[...], scales[1])
    store(2, middle[...], cot_sender[...], scales[2])
    receive = dot(put(target, 0, 8, 0, 128), upper[...]).astype(bf16)
    store(0, mesh[...], receive, scales[0])
    mesh_grad[...] = (cot_middle[...] + dot_nt(receive, w1[...])).astype(bf16)
    for k in range(2):
        grid_own[256 * k : 256 * k + 256, :] = dot(put(slot, 0, 8, 256 * k, 256), upper[...])


def grid_back_body(scales, core, grid_own, in0, in1, in2, in3, table, grid, w0, grid_grad, grads_own, grads_other, cot, held):
    for i in range(2):
        s = slice(256 * i, 256 * i + 256)
        total = grid_own[s, :]
        for k, block in enumerate((in0, in1, in2, in3)):
            total = total + dot(put_rows(table_rows(table, k), i * 256, 256), block[...])
        total = total.astype(bf16)
        cot[s, :] = total
        grid_grad[s, :] = dot_nt(total, w0[...]).astype(bf16)
    store_blocks(grads_own, grads_other, 0, dot_tn(grid[...], cot[...]) * scales[0], held, core)


def pair_body(*refs):
    out = refs[-1]
    place = 0
    for own, got in zip(refs[0:-1:2], refs[1:-1:2]):
        for k in range(own.shape[2]):
            out[:, :, place] = (own[:, :, k].astype(f32) + got[:, :, k].astype(f32)).astype(bf16)
            place += 1


def sum_body(terms, *shard):
    total = terms[0].astype(f32)
    for d in range(1, terms.shape[0]):
        total = total + terms[d].astype(f32)
    total = total.astype(bf16)
    if len(shard[0].shape) == 2:
        shard[0][...] = total
    else:
        for p in range(shard[0].shape[0]):
            shard[0][p] = total


def place_early_body(core, own, other, out):
    first = core[0] == 0
    for q in range(2):
        a, b = own[:, q].reshape(512, 128), other[:, q].reshape(512, 128)
        out[:, 128 * q : 128 * q + 128] = jnp.where(first, a, b)
        out[:, 256 + 128 * q : 384 + 128 * q] = jnp.where(first, b, a)


def place_late_body(core, own, other, kept, out):
    del kept
    place_early_body(core, own, other, out)


def swapped(value):
    return lax.ppermute(value, "core", [(0, 1), (1, 0)])


def scaled(body, scales):
    return functools.partial(body, scales)


def on_device(
    grid_latent, mesh_latent, edge_latent, mesh_cotangent, edge_cotangent, grid_send, grid_slot, grid_target,
    mesh_halo, mesh_send, mesh_slot, mesh_target, weights,
):
    peers = lax.axis_size(AXES)
    mesh_rows, latent = mesh_latent.shape
    edges = grid_slot.shape[0]
    grid_scale = 1.0 / (edges * peers) ** 0.5
    edge_scale = 1.0 / (mesh_slot.shape[0] * peers) ** 0.5
    node_scale = 1.0 / (mesh_rows * peers) ** 0.5
    grid_table = grid_send
    core = lax.axis_index("core").reshape(1)
    halo_table = mesh_halo.reshape(2, 128)
    far_table = mesh_send[0].T
    gslot, gtarget = grid_slot.reshape(8, 128), grid_target.reshape(8, 128)
    mslot, mtarget = mesh_slot.reshape(8, 128), mesh_target.reshape(8, 128)
    big, small, halo = (edges, latent), (mesh_rows, latent), (64, latent)
    vm = pltpu.VMEM

    project, *outgoing = call(
        project_body, [((512, latent), bf16)] + [((256, latent), bf16)] * 4,
        (grid_latent, grid_table), weights, (0,),
    )
    arrived = outgoing_rows(outgoing)
    (own,) = call(
        encode_own_body, [(big, f32)], (project, gslot, gtarget, mesh_latent),
        weights, (1,), scratch=(vm((768, latent), bf16),), flops=10**9,
    )
    pre, linear, hidden, middle, sender, *halos, far_out = call(
        encode_body,
        [(big, f32), (big, f32), (big, bf16), (small, bf16), (small, bf16)] + [(halo, bf16)] * 4 + [((2048, 128), bf16)],
        (own, *arrived, gslot, gtarget, mesh_latent, halo_table, far_table), weights, (2, 4),
        scratch=(vm(small, f32), vm((2048, 128), f32)), flops=2 * 10**9,
    )
    far_in = lax.all_to_all(far_out.reshape(peers, 16, 128), AXES, 0, 0, tiled=True).reshape(2048, 128)
    halo_in = outgoing_rows(halos)
    own, update_own = call(
        process_own_body, [(big, f32), (small, f32)], (middle, sender, edge_latent, mslot, mtarget),
        weights, (3, 5, 7), scratch=(vm((384, latent), bf16),), flops=2 * 10**9,
    )
    (
        mesh_update, phidden, rounded, uhidden, cot_linear, cot_update, plinear, cround, receive, sender_own,
        *halos, far_out,
    ) = call(
        process_body,
        [(small, bf16), (big, bf16)] + [(small, bf16)] * 4 + [(big, bf16)] * 2
        + [(small, bf16), (small, f32)] + [(halo, bf16)] * 4 + [((2048, 128), bf16)],
        (own, *halo_in, far_in, mslot, mtarget, middle, update_own, mesh_cotangent, edge_cotangent),
        weights, (6, 8, 9),
        scratch=(
            vm((768, latent), bf16), vm(big, f32), vm(big, f32), vm((edges, 128), f32),
            vm(small, f32), vm((2048, 128), f32), vm((8, 128), jnp.int32),
        ),
        flops=8 * 10**9,
    )
    far_back = lax.all_to_all(far_out.reshape(peers, 16, 128), AXES, 0, 0, tiled=True).reshape(2048, 128)
    halo_back = returned_rows(halos)

    def blocks(count):
        return ((32, 2, count, 16, 128), bf16)

    held = vm((latent, latent), bf16)
    early_own, early_other = call(
        scaled(process_grads_body, [edge_scale] * 3 + [node_scale] * 3),
        [blocks(6), blocks(6)],
        (core, edge_latent, cround, phidden, plinear, middle, receive, cot_update, rounded, uhidden, cot_linear),
        scratch=(held,), flops=2 * 10**9,
    )
    early_other = swapped(early_other)
    edge_grad, middle_part = call(
        edge_back_body, [(big, bf16), (small, f32)], (cround, edge_cotangent, receive, cot_update, mesh_cotangent),
        weights, (3, 5, 7),
    )
    early = (early_own.astype(f32) + early_other.astype(f32)).astype(bf16)
    early, _ = lax.optimization_barrier((early, (halo_back, far_back)))
    early = lax.all_to_all(early.reshape(64, 96, 128), CHIPS, 0, 0, tiled=True)
    cot_sender, cot_middle, elinear, upper, *partials = call(
        encode_back_body,
        [(small, bf16), (small, f32), (big, bf16), (big, bf16)] + [((256, latent), bf16)] * 4,
        (*halo_back, far_back, halo_table, far_table, sender_own, middle_part, pre, linear, gslot, gtarget),
        weights, (2, 4), scratch=(vm((768, latent), bf16), vm((2048, 128), f32)), flops=4 * 10**9,
    )
    partials = returned_rows(partials)
    grid_own, mesh_grad, late_own, late_other = call(
        scaled(encode_grads_body, [grid_scale, grid_scale, edge_scale]),
        [((512, latent), f32), (small, bf16), blocks(3), blocks(3)],
        (core, upper, gslot, gtarget, cot_middle, mesh_latent, middle, cot_sender, hidden, elinear),
        weights, (1,), scratch=(held,), flops=2 * 10**9,
    )
    (early,) = call(sum_body, [((64, 96, 128), bf16)], (early,), flops=10**7)
    early = lax.all_to_all(early, CHIPS, 0, 0, tiled=True)
    grid_grad, last_own, last_other = call(
        scaled(grid_back_body, [grid_scale]), [((512, latent), bf16), blocks(1), blocks(1)],
        (core, grid_own, *partials, grid_table, grid_latent), weights, (0,),
        scratch=(vm((512, latent), bf16), held),
    )
    (late,) = call(
        pair_body, [blocks(4)], (last_own, swapped(last_other), late_own, swapped(late_other)),
        flops=10**6,
    )
    late, early = lax.optimization_barrier((late, early))
    late = lax.all_to_all(late.reshape(64, 64, 128), CHIPS, 0, 0, tiled=True)
    early_swapped = swapped(early).reshape(blocks(6)[0])
    early = early.reshape(blocks(6)[0])
    placed = pl.pallas_call(
        place_early_body,
        grid_spec=pltpu.PrefetchScalarGridSpec(
            num_scalar_prefetch=1,
            grid=(6,),
            in_specs=[pl.BlockSpec((32, 2, None, 16, 128), lambda i, c: (0, 0, i, 0, 0))] * 2,
            out_specs=pl.BlockSpec((None, latent, latent), lambda i, c: (i + 3 + (i + 5) // 6, 0, 0)),
        ),
        out_shape=jax.ShapeDtypeStruct(weights.shape, bf16),
        compiler_params=pltpu.CompilerParams(vmem_limit_bytes=67000000),
        name="place_early",
    )(core, early, early_swapped)
    (late,) = call(sum_body, [((64, 64, 128), bf16)], (late,), flops=10**7)
    late = lax.all_to_all(late, CHIPS, 0, 0, tiled=True)
    other = swapped(late).reshape(blocks(4)[0])
    late = late.reshape(blocks(4)[0])
    weight_grads = pl.pallas_call(
        place_late_body,
        grid_spec=pltpu.PrefetchScalarGridSpec(
            num_scalar_prefetch=1,
            grid=(4,),
            in_specs=[pl.BlockSpec((32, 2, None, 16, 128), lambda i, c: (0, 0, i, 0, 0))] * 2
            + [pl.BlockSpec(memory_space=pl.ANY)],
            out_specs=pl.BlockSpec((None, latent, latent), lambda i, c: (i + i // 3, 0, 0)),
        ),
        out_shape=jax.ShapeDtypeStruct(weights.shape, bf16),
        input_output_aliases={3: 0},
        compiler_params=pltpu.CompilerParams(vmem_limit_bytes=12 << 20),
        name="place_late",
    )(core, late, other, placed)
    return (mesh_update, grid_grad, mesh_grad, edge_grad, weight_grads)


def solution(mesh):
    row = P(AXES, None)
    wide = jax.sharding.Mesh(mesh.devices.reshape(4, 2, 4, 4), AXES)

    return jax.shard_map(
        on_device,
        mesh=wide,
        in_specs=(row, row, row, row, row, P(AXES, None, None), P(AXES), P(AXES), P(AXES, None, None),
                  P(AXES, None, None), P(AXES), P(AXES), P()),
        out_specs=(row, row, row, row, P()),
        check_vma=False,
    )
```

```python
import functools

import jax
import jax.numpy as jnp
from jax import lax
from jax.experimental import pallas as pl
from jax.experimental.pallas import tpu as pltpu
from jax.sharding import PartitionSpec as P


norm_eps = 1e-05
f32 = jnp.float32
bf16 = jnp.bfloat16
AXES = ("x", "core", "y", "z")
CHIPS = ("x", "y", "z")
FACE = ("x", "core")
SUB = ("y", "z")
CHUNK = 512
ROWS = CHUNK // 128


def shifted(value, axis, steps):
    count = lax.axis_size(axis)
    pairs = [(source, (source + steps) % count) for source in range(count)]
    return lax.ppermute(value, axis, pairs)


def outgoing_rows(blocks):
    routes = ((SUB, 1), (SUB, -1), (FACE, 1), (FACE, -1))
    return [shifted(block, axis, step) for block, (axis, step) in zip(blocks, routes)]


def returned_rows(blocks):
    routes = ((SUB, -1), (SUB, 1), (FACE, -1), (FACE, 1))
    return [shifted(block, axis, step) for block, (axis, step) in zip(blocks, routes)]


def dot(a, b):
    return jnp.dot(a, b, preferred_element_type=f32)


def dot_nt(a, b):
    return lax.dot_general(a, b, (((1,), (1,)), ((), ())), preferred_element_type=f32)


def dot_tn(a, b):
    return lax.dot_general(a, b, (((0,), (0,)), ((), ())), preferred_element_type=f32)


def halves(values):
    upper = values.astype(bf16)
    return upper, (values - upper.astype(f32)).astype(bf16)


def mean(values):
    return jnp.sum(values, axis=-1, keepdims=True) * (1.0 / values.shape[-1])


def norm_parts(values):
    centre = values - mean(values)
    inverse = lax.rsqrt(mean(centre * centre) + norm_eps)
    return centre * inverse, inverse


def norm_back(normed, inverse, upstream):
    return inverse * (upstream - mean(upstream) - normed * mean(upstream * normed))


def sigmoid(values):
    return 0.5 + 0.5 * jnp.tanh(0.5 * values)


def silu(values):
    return values * sigmoid(values)


def slope(values):
    s = sigmoid(values)
    return s * (1.0 + values * (1.0 - s))


def pick_rows(row, offset, count):
    column = jnp.transpose(jnp.broadcast_to(row, (128, 128))) - offset
    lane = lax.broadcasted_iota(jnp.int32, (128, 128), 1)
    return jnp.concatenate(
        [jnp.where(column == lane + 128 * b, 1.0, 0.0).astype(bf16) for b in range(count // 128)],
        axis=1,
    )


def pick(ref, first, rows, offset, count):
    return jnp.concatenate(
        [pick_rows(ref[pl.ds(first + r, 1), :], offset, count) for r in range(rows)], axis=0
    )


def put(ref, first, rows, offset, count):
    return put_rows([ref[pl.ds(first + r, 1), :] for r in range(rows)], offset, count)


def table_rows(table, k):
    return [table[0, k : k + 1, 128 * h : 128 * h + 128] for h in range(2)]


def put_rows(rows, offset, count):
    place = lax.broadcasted_iota(jnp.int32, (count, 128), 0) + offset
    return jnp.concatenate(
        [jnp.where(place == jnp.broadcast_to(row, (count, 128)), 1.0, 0.0).astype(bf16) for row in rows], axis=1
    )


def stack_halves(values):
    return jnp.concatenate(halves(values), axis=0)


def twice(values):
    return jnp.concatenate([values, values], axis=1)


def chunks(count, body):
    def step(i, carry):
        body(i, pl.ds(pl.multiple_of(i * CHUNK, CHUNK), CHUNK))
        return carry

    lax.fori_loop(0, count, step, 0)


def call(body, outs, args, weights=None, picks=(), scratch=(), flops=10**9, vmem=67000000):
    def whole(shape):
        return pl.BlockSpec(shape, lambda i: (0,) * len(shape))

    in_specs = [pl.BlockSpec(memory_space=pltpu.SMEM) if a.shape == (1,) else whole(a.shape) for a in args]
    for k in picks:
        in_specs.append(
            pl.BlockSpec((None, weights.shape[1], weights.shape[2]), functools.partial(lambda k, i: (k, 0, 0), k))
        )
    shapes = [jax.ShapeDtypeStruct(s, d) for s, d in outs]
    total = sum(a.size * a.dtype.itemsize for a in args) + sum(s.size * s.dtype.itemsize for s in shapes)
    total += len(picks) * 512 * 1024
    return pl.pallas_call(
        body,
        grid=(1,),
        out_shape=shapes,
        in_specs=in_specs,
        out_specs=[whole(s.shape) for s in shapes],
        scratch_shapes=list(scratch),
        compiler_params=pltpu.CompilerParams(vmem_limit_bytes=vmem),
        cost_estimate=pl.CostEstimate(flops=flops, bytes_accessed=total, transcendentals=0),
    )(*args, *([weights] * len(picks)))


def project_body(grid, table, w0, project, out0, out1, out2, out3):
    chunks(512 // CHUNK, lambda i, s: project.__setitem__((s, slice(None)), dot(grid[s, :], w0[...]).astype(bf16)))
    for k, out in enumerate((out0, out1, out2, out3)):
        picked = jnp.concatenate([pick_rows(row, 0, 512) for row in table_rows(table, k)], axis=0)
        out[...] = dot(picked, project[...]).astype(bf16)


def encode_own_body(project, slot, target, mesh, w1, own, source):
    source[0:512, :] = project[...]
    source[512:768, :] = stack_halves(dot(mesh[...], w1[...]))

    def step(i, s):
        receiver = pick(target, ROWS * i, ROWS, 0, 128)
        own[s, :] = dot(jnp.concatenate([pick(slot, ROWS * i, ROWS, 0, 512), twice(receiver)], axis=1), source[...])

    chunks(1024 // CHUNK, step)


def far_slots(slot):
    far = slot - 384
    return jnp.where(slot < 384, slot, 384 + (far & 3) * 128 + (far >> 2))


def encode_body(
    own, in0, in1, in2, in3, slot, target, mesh, halo, far, w2, w4,
    pre_out, linear_out, hidden_out, middle_out, sender_out, h0, h1, h2, h3, far_out,
    total, wide,
):
    total[...] = jnp.zeros_like(total)

    def step(i, s):
        pre = own[s, :]
        for k, block in enumerate((in0, in1, in2, in3)):
            pre = pre + dot(pick(slot, ROWS * i, ROWS, 512 + 256 * k, 256), block[...])
        pre_out[s, :] = pre
        hidden = silu(pre).astype(bf16)
        hidden_out[s, :] = hidden
        linear = dot(hidden, w2[...])
        linear_out[s, :] = linear
        message = norm_parts(linear)[0].astype(bf16)
        total[...] += dot(put(target, ROWS * i, ROWS, 0, 128), message)

    chunks(1024 // CHUNK, step)
    middle = (mesh[...].astype(f32) + total[...]).astype(bf16)
    middle_out[...] = middle
    sender = dot(middle, w4[...]).astype(bf16)
    sender_out[...] = sender
    rows = dot(pick(halo, 0, 2, 0, 128), sender).astype(bf16)
    for k, out in enumerate((h0, h1, h2, h3)):
        out[...] = rows[64 * k : 64 * k + 64, :]
    for r in range(4):
        picked = dot(pick(far, r, 1, 0, 128), sender)
        for c in range(4):
            wide[pl.ds(4 * c + r, 128, stride=16), :] = picked[:, 128 * c : 128 * c + 128]
    far_out[...] = wide[...].astype(bf16)


def process_own_body(middle, sender, edge, slot, target, w3, w5, w7, own, update_own, source):
    source[0:128, :] = sender[...]
    source[128:384, :] = stack_halves(dot(middle[...], w5[...]))
    update_own[...] = dot(middle[...], w7[...])

    def step(i, s):
        receiver = pick(target, ROWS * i, ROWS, 0, 128)
        picked = jnp.concatenate([pick(slot, ROWS * i, ROWS, 0, 128), twice(receiver)], axis=1)
        own[s, :] = dot(edge[s, :], w3[...]) + dot(picked, source[...])

    chunks(1024 // CHUNK, step)


def gather_far(wide, source, first):
    for r in range(4):
        for c in range(4):
            source[first + 128 * r : first + 128 * r + 128, 128 * c : 128 * c + 128] = wide[
                pl.ds(4 * c + r, 128, stride=16), :
            ].astype(bf16)


def process_body(
    own, in0, in1, in2, in3, far_in, slot, target, middle, update_own, mesh_cot, edge_cot, w6, w8, w9,
    mesh_update, hidden_out, round_out, uhidden_out, cot_linear_out, cot_update_out, plinear_out, cround_out,
    receive_out, sender_own, h0, h1, h2, h3, far_out,
    source, pre_s, normed_s, inverse_s, total, wide, slots,
):
    slots[...] = far_slots(slot[...])
    for k, block in enumerate((in0, in1, in2, in3)):
        source[64 * k : 64 * k + 64, :] = block[...]
    wide[...] = far_in[...].astype(f32)
    gather_far(wide, source, 256)
    total[...] = jnp.zeros_like(total)

    def forward(i, s):
        pre = own[s, :] + dot(pick(slots, ROWS * i, ROWS, 128, 768), source[...])
        pre_s[s, :] = pre
        hidden = silu(pre).astype(bf16)
        hidden_out[s, :] = hidden
        normed, inverse = norm_parts(dot(hidden, w6[...]))
        normed_s[s, :] = normed
        inverse_s[s, :] = jnp.broadcast_to(inverse, (CHUNK, 128))
        total[...] += dot(put(target, ROWS * i, ROWS, 0, 128), normed.astype(bf16))

    chunks(1024 // CHUNK, forward)
    rounded = total[...].astype(bf16)
    round_out[...] = rounded
    pre = update_own[...] + dot(rounded, w8[...])
    uhidden = silu(pre).astype(bf16)
    uhidden_out[...] = uhidden
    normed, inverse = norm_parts(dot(uhidden, w9[...]))
    mesh_update[...] = (middle[...].astype(f32) + normed).astype(bf16)
    cot_linear = norm_back(normed, inverse, mesh_cot[...].astype(f32)).astype(bf16)
    cot_linear_out[...] = cot_linear
    cot_update = (dot_nt(cot_linear, w9[...]) * slope(pre)).astype(bf16)
    cot_update_out[...] = cot_update
    cot_total = stack_halves(dot_nt(cot_update, w8[...]))

    def backward(i, s):
        receiver = pick(target, ROWS * i, ROWS, 0, 128)
        upstream = dot(twice(receiver), cot_total) + edge_cot[s, :].astype(f32)
        cot = norm_back(normed_s[s, :], inverse_s[s, 0:1], upstream).astype(bf16)
        plinear_out[s, :] = cot
        cround_out[s, :] = (dot_nt(cot, w6[...]) * slope(pre_s[s, :])).astype(bf16)

    chunks(1024 // CHUNK, backward)
    kept = jnp.concatenate([put(target, 0, 8, 0, 128), put(slots, 0, 8, 0, 128)], axis=0)
    kept = dot(kept, cround_out[...])
    receive_out[...] = kept[0:128, :].astype(bf16)
    sender_own[...] = kept[128:256, :]
    spread = put(slots, 0, 8, 128, 256)
    spread = dot(spread, cround_out[...]).astype(bf16)
    for k, out in enumerate((h0, h1, h2, h3)):
        out[...] = spread[64 * k : 64 * k + 64, :]
    for half in range(2):
        spread = put(slots, 0, 8, 384 + 256 * half, 256)
        spread = dot(spread, cround_out[...])
        for q in range(2):
            for c in range(4):
                wide[pl.ds(4 * c + 2 * half + q, 128, stride=16), :] = spread[
                    128 * q : 128 * q + 128, 128 * c : 128 * c + 128
                ]
    far_out[...] = wide[...].astype(bf16)


def store_blocks(own, other, k, term, held, core):
    held[...] = term.astype(bf16)
    for q in range(2):
        for out, c in ((own, core[0]), (other, 1 - core[0])):
            columns = pl.ds(pl.multiple_of(256 * c + 128 * q, 128), 128)
            out[:, q, k, :, :] = held[:, columns].reshape(32, 16, 128)


def process_grads_body(
    scales, core, edge, cround, hidden, plinear, middle, receive, cot_update, rounded, uhidden, cot_linear,
    grads_own, grads_other, held,
):
    pairs = ((edge, cround), (middle, receive), (hidden, plinear), (middle, cot_update), (rounded, cot_update), (uhidden, cot_linear))
    for k, (x, y) in enumerate(pairs):
        store_blocks(grads_own, grads_other, k, dot_tn(x[...], y[...]) * scales[k], held, core)


def edge_back_body(cround, edge_cot, receive, cot_update, mesh_cot, w3, w5, w7, edge_grad, middle_part):
    middle_part[...] = mesh_cot[...].astype(f32) + dot_nt(cot_update[...], w7[...]) + dot_nt(receive[...], w5[...])

    def step(i, s):
        edge_grad[s, :] = (edge_cot[s, :].astype(f32) + dot_nt(cround[s, :], w3[...])).astype(bf16)

    chunks(1024 // CHUNK, step)


def encode_back_body(
    in0, in1, in2, in3, far_in, halo, far, sender_own, middle_part, pre, linear, slot, target, w2, w4,
    cot_sender_out, cot_middle_out, elinear_out, upper_out, g0, g1, g2, g3,
    source, wide,
):
    for k, block in enumerate((in0, in1, in2, in3)):
        source[64 * k : 64 * k + 64, :] = block[...]
    wide[...] = far_in[...].astype(f32)
    gather_far(wide, source, 256)
    owners = jnp.concatenate([put(halo, 0, 2, 0, 128), put(far, 0, 4, 0, 128)], axis=1)
    cot_sender = (sender_own[...] + dot(owners, source[...])).astype(bf16)
    cot_sender_out[...] = cot_sender
    cot_middle = middle_part[...] + dot_nt(cot_sender, w4[...])
    cot_middle_out[...] = cot_middle
    cot_middle = stack_halves(cot_middle)

    def step(i, s):
        receiver = pick(target, ROWS * i, ROWS, 0, 128)
        normed, inverse = norm_parts(linear[s, :])
        cot = norm_back(normed, inverse, dot(twice(receiver), cot_middle)).astype(bf16)
        elinear_out[s, :] = cot
        upper_out[s, :] = (dot_nt(cot, w2[...]) * slope(pre[s, :])).astype(bf16)

    chunks(1024 // CHUNK, step)
    for k, out in enumerate((g0, g1, g2, g3)):
        spread = put(slot, 0, 8, 512 + 256 * k, 256)
        out[...] = dot(spread, upper_out[...]).astype(bf16)


def encode_grads_body(
    scales, core, upper, slot, target, cot_middle, mesh, middle, cot_sender, hidden, elinear, w1,
    grid_own, mesh_grad, grads_own, grads_other, held,
):
    def store(k, x, y, scale):
        store_blocks(grads_own, grads_other, k, dot_tn(x, y) * scale, held, core)

    store(1, hidden[...], elinear[...], scales[1])
    store(2, middle[...], cot_sender[...], scales[2])
    receive = dot(put(target, 0, 8, 0, 128), upper[...]).astype(bf16)
    store(0, mesh[...], receive, scales[0])
    mesh_grad[...] = (cot_middle[...] + dot_nt(receive, w1[...])).astype(bf16)
    for k in range(2):
        grid_own[256 * k : 256 * k + 256, :] = dot(put(slot, 0, 8, 256 * k, 256), upper[...])


def grid_back_body(scales, core, grid_own, in0, in1, in2, in3, table, grid, w0, grid_grad, grads_own, grads_other, cot, held):
    for i in range(2):
        s = slice(256 * i, 256 * i + 256)
        total = grid_own[s, :]
        for k, block in enumerate((in0, in1, in2, in3)):
            total = total + dot(put_rows(table_rows(table, k), i * 256, 256), block[...])
        total = total.astype(bf16)
        cot[s, :] = total
        grid_grad[s, :] = dot_nt(total, w0[...]).astype(bf16)
    store_blocks(grads_own, grads_other, 0, dot_tn(grid[...], cot[...]) * scales[0], held, core)


def pair_body(*refs):
    out = refs[-1]
    place = 0
    for own, got in zip(refs[0:-1:2], refs[1:-1:2]):
        for k in range(own.shape[2]):
            out[:, :, place] = (own[:, :, k].astype(f32) + got[:, :, k].astype(f32)).astype(bf16)
            place += 1


def sum_body(terms, shard):
    total = terms[0].astype(f32)
    for d in range(1, terms.shape[0]):
        total = total + terms[d].astype(f32)
    total = total.astype(bf16)
    for p in range(shard.shape[0]):
        shard[p] = total


def summed(terms):
    spec = pl.BlockSpec((terms.shape[0], 32, 128), lambda i: (0, i, 0))
    return pl.pallas_call(
        sum_body,
        grid=(terms.shape[1] // 32,),
        in_specs=[spec],
        out_specs=spec,
        out_shape=jax.ShapeDtypeStruct(terms.shape, bf16),
        compiler_params=pltpu.CompilerParams(vmem_limit_bytes=67000000),
    )(terms)


def place_early_body(core, own, other, out):
    first = core[0] == 0
    for q in range(2):
        a, b = own[:, q].reshape(512, 128), other[:, q].reshape(512, 128)
        out[:, 128 * q : 128 * q + 128] = jnp.where(first, a, b)
        out[:, 256 + 128 * q : 384 + 128 * q] = jnp.where(first, b, a)


def place_late_body(core, own, other, kept, out):
    del kept
    place_early_body(core, own, other, out)


def swapped(value):
    return lax.ppermute(value, "core", [(0, 1), (1, 0)])


def scaled(body, scales):
    return functools.partial(body, scales)


def on_device(
    grid_latent, mesh_latent, edge_latent, mesh_cotangent, edge_cotangent, grid_send, grid_slot, grid_target,
    mesh_halo, mesh_send, mesh_slot, mesh_target, weights,
):
    peers = lax.axis_size(AXES)
    mesh_rows, latent = mesh_latent.shape
    edges = grid_slot.shape[0]
    grid_scale = 1.0 / (edges * peers) ** 0.5
    edge_scale = 1.0 / (mesh_slot.shape[0] * peers) ** 0.5
    node_scale = 1.0 / (mesh_rows * peers) ** 0.5
    grid_table = grid_send
    core = lax.axis_index("core").reshape(1)
    halo_table = mesh_halo.reshape(2, 128)
    far_table = mesh_send[0].T
    gslot, gtarget = grid_slot.reshape(8, 128), grid_target.reshape(8, 128)
    mslot, mtarget = mesh_slot.reshape(8, 128), mesh_target.reshape(8, 128)
    big, small, halo = (edges, latent), (mesh_rows, latent), (64, latent)
    vm = pltpu.VMEM

    project, *outgoing = call(
        project_body, [((512, latent), bf16)] + [((256, latent), bf16)] * 4,
        (grid_latent, grid_table), weights, (0,),
    )
    arrived = outgoing_rows(outgoing)
    (own,) = call(
        encode_own_body, [(big, f32)], (project, gslot, gtarget, mesh_latent),
        weights, (1,), scratch=(vm((768, latent), bf16),), flops=10**9,
    )
    pre, linear, hidden, middle, sender, *halos, far_out = call(
        encode_body,
        [(big, f32), (big, f32), (big, bf16), (small, bf16), (small, bf16)] + [(halo, bf16)] * 4 + [((2048, 128), bf16)],
        (own, *arrived, gslot, gtarget, mesh_latent, halo_table, far_table), weights, (2, 4),
        scratch=(vm(small, f32), vm((2048, 128), f32)), flops=2 * 10**9,
    )
    far_in = lax.all_to_all(far_out.reshape(peers, 16, 128), AXES, 0, 0, tiled=True).reshape(2048, 128)
    halo_in = outgoing_rows(halos)
    own, update_own = call(
        process_own_body, [(big, f32), (small, f32)], (middle, sender, edge_latent, mslot, mtarget),
        weights, (3, 5, 7), scratch=(vm((384, latent), bf16),), flops=2 * 10**9,
    )
    (
        mesh_update, phidden, rounded, uhidden, cot_linear, cot_update, plinear, cround, receive, sender_own,
        *halos, far_out,
    ) = call(
        process_body,
        [(small, bf16), (big, bf16)] + [(small, bf16)] * 4 + [(big, bf16)] * 2
        + [(small, bf16), (small, f32)] + [(halo, bf16)] * 4 + [((2048, 128), bf16)],
        (own, *halo_in, far_in, mslot, mtarget, middle, update_own, mesh_cotangent, edge_cotangent),
        weights, (6, 8, 9),
        scratch=(
            vm((768, latent), bf16), vm(big, f32), vm(big, f32), vm((edges, 128), f32),
            vm(small, f32), vm((2048, 128), f32), vm((8, 128), jnp.int32),
        ),
        flops=8 * 10**9,
    )
    far_back = lax.all_to_all(far_out.reshape(peers, 16, 128), AXES, 0, 0, tiled=True).reshape(2048, 128)
    halo_back = returned_rows(halos)

    def blocks(count):
        return ((32, 2, count, 16, 128), bf16)

    held = vm((latent, latent), bf16)
    early_own, early_other = call(
        scaled(process_grads_body, [edge_scale] * 3 + [node_scale] * 3),
        [blocks(6), blocks(6)],
        (core, edge_latent, cround, phidden, plinear, middle, receive, cot_update, rounded, uhidden, cot_linear),
        scratch=(held,), flops=2 * 10**9,
    )
    early_other = swapped(early_other)
    edge_grad, middle_part = call(
        edge_back_body, [(big, bf16), (small, f32)], (cround, edge_cotangent, receive, cot_update, mesh_cotangent),
        weights, (3, 5, 7),
    )
    early = (early_own.astype(f32) + early_other.astype(f32)).astype(bf16)
    early, _ = lax.optimization_barrier((early, (halo_back, far_back)))
    early = lax.all_to_all(early.reshape(64, 96, 128), CHIPS, 0, 0, tiled=True)
    cot_sender, cot_middle, elinear, upper, *partials = call(
        encode_back_body,
        [(small, bf16), (small, f32), (big, bf16), (big, bf16)] + [((256, latent), bf16)] * 4,
        (*halo_back, far_back, halo_table, far_table, sender_own, middle_part, pre, linear, gslot, gtarget),
        weights, (2, 4), scratch=(vm((768, latent), bf16), vm((2048, 128), f32)), flops=4 * 10**9,
    )
    partials = returned_rows(partials)
    grid_own, mesh_grad, late_own, late_other = call(
        scaled(encode_grads_body, [grid_scale, grid_scale, edge_scale]),
        [((512, latent), f32), (small, bf16), blocks(3), blocks(3)],
        (core, upper, gslot, gtarget, cot_middle, mesh_latent, middle, cot_sender, hidden, elinear),
        weights, (1,), scratch=(held,), flops=2 * 10**9,
    )
    early = summed(early)
    early = lax.all_to_all(early, CHIPS, 0, 0, tiled=True)
    grid_grad, last_own, last_other = call(
        scaled(grid_back_body, [grid_scale]), [((512, latent), bf16), blocks(1), blocks(1)],
        (core, grid_own, *partials, grid_table, grid_latent), weights, (0,),
        scratch=(vm((512, latent), bf16), held),
    )
    (late,) = call(
        pair_body, [blocks(4)], (last_own, swapped(last_other), late_own, swapped(late_other)),
        flops=10**6,
    )
    late, early = lax.optimization_barrier((late, early))
    late = lax.all_to_all(late.reshape(64, 64, 128), CHIPS, 0, 0, tiled=True)
    early_swapped = swapped(early).reshape(blocks(6)[0])
    early = early.reshape(blocks(6)[0])
    placed = pl.pallas_call(
        place_early_body,
        grid_spec=pltpu.PrefetchScalarGridSpec(
            num_scalar_prefetch=1,
            grid=(6,),
            in_specs=[pl.BlockSpec((32, 2, None, 16, 128), lambda i, c: (0, 0, i, 0, 0))] * 2,
            out_specs=pl.BlockSpec((None, latent, latent), lambda i, c: (i + 3 + (i + 5) // 6, 0, 0)),
        ),
        out_shape=jax.ShapeDtypeStruct(weights.shape, bf16),
        compiler_params=pltpu.CompilerParams(vmem_limit_bytes=67000000),
        name="place_early",
    )(core, early, early_swapped)
    late = summed(late)
    late = lax.all_to_all(late, CHIPS, 0, 0, tiled=True)
    other = swapped(late).reshape(blocks(4)[0])
    late = late.reshape(blocks(4)[0])
    weight_grads = pl.pallas_call(
        place_late_body,
        grid_spec=pltpu.PrefetchScalarGridSpec(
            num_scalar_prefetch=1,
            grid=(4,),
            in_specs=[pl.BlockSpec((32, 2, None, 16, 128), lambda i, c: (0, 0, i, 0, 0))] * 2
            + [pl.BlockSpec(memory_space=pl.ANY)],
            out_specs=pl.BlockSpec((None, latent, latent), lambda i, c: (i + i // 3, 0, 0)),
        ),
        out_shape=jax.ShapeDtypeStruct(weights.shape, bf16),
        input_output_aliases={3: 0},
        compiler_params=pltpu.CompilerParams(vmem_limit_bytes=12 << 20),
        name="place_late",
    )(core, late, other, placed)
    return (mesh_update, grid_grad, mesh_grad, edge_grad, weight_grads)


def solution(mesh):
    row = P(AXES, None)
    wide = jax.sharding.Mesh(mesh.devices.reshape(4, 2, 4, 4), AXES)

    return jax.shard_map(
        on_device,
        mesh=wide,
        in_specs=(row, row, row, row, row, P(AXES, None, None), P(AXES), P(AXES), P(AXES, None, None),
                  P(AXES, None, None), P(AXES), P(AXES), P()),
        out_specs=(row, row, row, row, P()),
        check_vma=False,
    )
```

```python
import functools

import jax
import jax.numpy as jnp
from jax import lax
from jax.experimental import pallas as pl
from jax.experimental.pallas import tpu as pltpu
from jax.sharding import PartitionSpec as P


norm_eps = 1e-05
f32 = jnp.float32
bf16 = jnp.bfloat16
AXES = ("x", "core", "y", "z")
CHIPS = ("x", "y", "z")
FACE = ("x", "core")
SUB = ("y", "z")
CHUNK = 512
ROWS = CHUNK // 128


def shifted(value, axis, steps):
    count = lax.axis_size(axis)
    pairs = [(source, (source + steps) % count) for source in range(count)]
    return lax.ppermute(value, axis, pairs)


def outgoing_rows(blocks):
    routes = ((SUB, 1), (SUB, -1), (FACE, 1), (FACE, -1))
    return [shifted(block, axis, step) for block, (axis, step) in zip(blocks, routes)]


def returned_rows(blocks):
    routes = ((SUB, -1), (SUB, 1), (FACE, -1), (FACE, 1))
    return [shifted(block, axis, step) for block, (axis, step) in zip(blocks, routes)]


def dot(a, b):
    return jnp.dot(a, b, preferred_element_type=f32)


def dot_nt(a, b):
    return lax.dot_general(a, b, (((1,), (1,)), ((), ())), preferred_element_type=f32)


def dot_tn(a, b):
    return lax.dot_general(a, b, (((0,), (0,)), ((), ())), preferred_element_type=f32)


def halves(values):
    upper = values.astype(bf16)
    return upper, (values - upper.astype(f32)).astype(bf16)


def mean(values):
    return jnp.sum(values, axis=-1, keepdims=True) * (1.0 / values.shape[-1])


def norm_parts(values):
    centre = values - mean(values)
    inverse = lax.rsqrt(mean(centre * centre) + norm_eps)
    return centre * inverse, inverse


def norm_back(normed, inverse, upstream):
    return inverse * (upstream - mean(upstream) - normed * mean(upstream * normed))


def sigmoid(values):
    return 0.5 + 0.5 * jnp.tanh(0.5 * values)


def silu(values):
    return values * sigmoid(values)


def slope(values):
    s = sigmoid(values)
    return s * (1.0 + values * (1.0 - s))


def pick_rows(row, offset, count):
    column = jnp.transpose(jnp.broadcast_to(row, (128, 128))) - offset
    lane = lax.broadcasted_iota(jnp.int32, (128, 128), 1)
    return jnp.concatenate(
        [jnp.where(column == lane + 128 * b, 1.0, 0.0).astype(bf16) for b in range(count // 128)],
        axis=1,
    )


def pick(ref, first, rows, offset, count):
    return jnp.concatenate(
        [pick_rows(ref[pl.ds(first + r, 1), :], offset, count) for r in range(rows)], axis=0
    )


def put(ref, first, rows, offset, count):
    return put_rows([ref[pl.ds(first + r, 1), :] for r in range(rows)], offset, count)


def table_rows(table, k):
    return [table[0, k : k + 1, 128 * h : 128 * h + 128] for h in range(2)]


def put_rows(rows, offset, count):
    place = lax.broadcasted_iota(jnp.int32, (count, 128), 0) + offset
    return jnp.concatenate(
        [jnp.where(place == jnp.broadcast_to(row, (count, 128)), 1.0, 0.0).astype(bf16) for row in rows], axis=1
    )


def stack_halves(values):
    return jnp.concatenate(halves(values), axis=0)


def twice(values):
    return jnp.concatenate([values, values], axis=1)


def chunks(count, body):
    def step(i, carry):
        body(i, pl.ds(pl.multiple_of(i * CHUNK, CHUNK), CHUNK))
        return carry

    lax.fori_loop(0, count, step, 0)


def call(body, outs, args, weights=None, picks=(), scratch=(), flops=10**9, vmem=67000000):
    def whole(shape):
        return pl.BlockSpec(shape, lambda i: (0,) * len(shape))

    in_specs = [pl.BlockSpec(memory_space=pltpu.SMEM) if a.shape == (1,) else whole(a.shape) for a in args]
    for k in picks:
        in_specs.append(
            pl.BlockSpec((None, weights.shape[1], weights.shape[2]), functools.partial(lambda k, i: (k, 0, 0), k))
        )
    shapes = [jax.ShapeDtypeStruct(s, d) for s, d in outs]
    total = sum(a.size * a.dtype.itemsize for a in args) + sum(s.size * s.dtype.itemsize for s in shapes)
    total += len(picks) * 512 * 1024
    return pl.pallas_call(
        body,
        grid=(1,),
        out_shape=shapes,
        in_specs=in_specs,
        out_specs=[whole(s.shape) for s in shapes],
        scratch_shapes=list(scratch),
        compiler_params=pltpu.CompilerParams(vmem_limit_bytes=vmem),
        cost_estimate=pl.CostEstimate(flops=flops, bytes_accessed=total, transcendentals=0),
    )(*args, *([weights] * len(picks)))


def project_body(grid, table, w0, project, out0, out1, out2, out3):
    chunks(512 // CHUNK, lambda i, s: project.__setitem__((s, slice(None)), dot(grid[s, :], w0[...]).astype(bf16)))
    for k, out in enumerate((out0, out1, out2, out3)):
        picked = jnp.concatenate([pick_rows(row, 0, 512) for row in table_rows(table, k)], axis=0)
        out[...] = dot(picked, project[...]).astype(bf16)


def encode_own_body(project, slot, target, mesh, w1, own, source):
    source[0:512, :] = project[...]
    source[512:768, :] = stack_halves(dot(mesh[...], w1[...]))

    def step(i, s):
        receiver = pick(target, ROWS * i, ROWS, 0, 128)
        own[s, :] = dot(jnp.concatenate([pick(slot, ROWS * i, ROWS, 0, 512), twice(receiver)], axis=1), source[...])

    chunks(1024 // CHUNK, step)


def far_slots(slot):
    far = slot - 384
    return jnp.where(slot < 384, slot, 384 + (far & 3) * 128 + (far >> 2))


def encode_body(
    own, in0, in1, in2, in3, slot, target, mesh, halo, far, w2, w4,
    pre_out, linear_out, hidden_out, middle_out, sender_out, h0, h1, h2, h3, far_out,
    total, wide,
):
    total[...] = jnp.zeros_like(total)

    def step(i, s):
        pre = own[s, :]
        for k, block in enumerate((in0, in1, in2, in3)):
            pre = pre + dot(pick(slot, ROWS * i, ROWS, 512 + 256 * k, 256), block[...])
        pre_out[s, :] = pre
        hidden = silu(pre).astype(bf16)
        hidden_out[s, :] = hidden
        linear = dot(hidden, w2[...])
        linear_out[s, :] = linear
        message = norm_parts(linear)[0].astype(bf16)
        total[...] += dot(put(target, ROWS * i, ROWS, 0, 128), message)

    chunks(1024 // CHUNK, step)
    middle = (mesh[...].astype(f32) + total[...]).astype(bf16)
    middle_out[...] = middle
    sender = dot(middle, w4[...]).astype(bf16)
    sender_out[...] = sender
    rows = dot(pick(halo, 0, 2, 0, 128), sender).astype(bf16)
    for k, out in enumerate((h0, h1, h2, h3)):
        out[...] = rows[64 * k : 64 * k + 64, :]
    for r in range(4):
        picked = dot(pick(far, r, 1, 0, 128), sender)
        for c in range(4):
            wide[pl.ds(4 * c + r, 128, stride=16), :] = picked[:, 128 * c : 128 * c + 128]
    far_out[...] = wide[...].astype(bf16)


def process_own_body(middle, sender, edge, slot, target, w3, w5, w7, own, update_own, source):
    source[0:128, :] = sender[...]
    source[128:384, :] = stack_halves(dot(middle[...], w5[...]))
    update_own[...] = dot(middle[...], w7[...])

    def step(i, s):
        receiver = pick(target, ROWS * i, ROWS, 0, 128)
        picked = jnp.concatenate([pick(slot, ROWS * i, ROWS, 0, 128), twice(receiver)], axis=1)
        own[s, :] = dot(edge[s, :], w3[...]) + dot(picked, source[...])

    chunks(1024 // CHUNK, step)


def gather_far(wide, source, first):
    for r in range(4):
        for c in range(4):
            source[first + 128 * r : first + 128 * r + 128, 128 * c : 128 * c + 128] = wide[
                pl.ds(4 * c + r, 128, stride=16), :
            ].astype(bf16)


def process_body(
    own, in0, in1, in2, in3, far_in, slot, target, middle, update_own, mesh_cot, edge_cot, w6, w8, w9,
    mesh_update, hidden_out, round_out, uhidden_out, cot_linear_out, cot_update_out, plinear_out, cround_out,
    receive_out, sender_own, h0, h1, h2, h3, far_out,
    source, pre_s, normed_s, inverse_s, total, wide, slots,
):
    slots[...] = far_slots(slot[...])
    for k, block in enumerate((in0, in1, in2, in3)):
        source[64 * k : 64 * k + 64, :] = block[...]
    wide[...] = far_in[...].astype(f32)
    gather_far(wide, source, 256)
    total[...] = jnp.zeros_like(total)

    def forward(i, s):
        pre = own[s, :] + dot(pick(slots, ROWS * i, ROWS, 128, 768), source[...])
        pre_s[s, :] = pre
        hidden = silu(pre).astype(bf16)
        hidden_out[s, :] = hidden
        normed, inverse = norm_parts(dot(hidden, w6[...]))
        normed_s[s, :] = normed
        inverse_s[s, :] = jnp.broadcast_to(inverse, (CHUNK, 128))
        total[...] += dot(put(target, ROWS * i, ROWS, 0, 128), normed.astype(bf16))

    chunks(1024 // CHUNK, forward)
    rounded = total[...].astype(bf16)
    round_out[...] = rounded
    pre = update_own[...] + dot(rounded, w8[...])
    uhidden = silu(pre).astype(bf16)
    uhidden_out[...] = uhidden
    normed, inverse = norm_parts(dot(uhidden, w9[...]))
    mesh_update[...] = (middle[...].astype(f32) + normed).astype(bf16)
    cot_linear = norm_back(normed, inverse, mesh_cot[...].astype(f32)).astype(bf16)
    cot_linear_out[...] = cot_linear
    cot_update = (dot_nt(cot_linear, w9[...]) * slope(pre)).astype(bf16)
    cot_update_out[...] = cot_update
    cot_total = stack_halves(dot_nt(cot_update, w8[...]))

    def backward(i, s):
        receiver = pick(target, ROWS * i, ROWS, 0, 128)
        upstream = dot(twice(receiver), cot_total) + edge_cot[s, :].astype(f32)
        cot = norm_back(normed_s[s, :], inverse_s[s, 0:1], upstream).astype(bf16)
        plinear_out[s, :] = cot
        cround_out[s, :] = (dot_nt(cot, w6[...]) * slope(pre_s[s, :])).astype(bf16)

    chunks(1024 // CHUNK, backward)
    kept = jnp.concatenate([put(target, 0, 8, 0, 128), put(slots, 0, 8, 0, 128)], axis=0)
    kept = dot(kept, cround_out[...])
    receive_out[...] = kept[0:128, :].astype(bf16)
    sender_own[...] = kept[128:256, :]
    spread = put(slots, 0, 8, 128, 256)
    spread = dot(spread, cround_out[...]).astype(bf16)
    for k, out in enumerate((h0, h1, h2, h3)):
        out[...] = spread[64 * k : 64 * k + 64, :]
    for half in range(2):
        spread = put(slots, 0, 8, 384 + 256 * half, 256)
        spread = dot(spread, cround_out[...])
        for q in range(2):
            for c in range(4):
                wide[pl.ds(4 * c + 2 * half + q, 128, stride=16), :] = spread[
                    128 * q : 128 * q + 128, 128 * c : 128 * c + 128
                ]
    far_out[...] = wide[...].astype(bf16)


def store_blocks(own, other, k, term, held, core):
    held[...] = term.astype(bf16)
    for q in range(2):
        for out, c in ((own, core[0]), (other, 1 - core[0])):
            columns = pl.ds(pl.multiple_of(256 * c + 128 * q, 128), 128)
            out[:, q, k, :, :] = held[:, columns].reshape(32, 16, 128)


def process_grads_body(
    scales, core, edge, cround, hidden, plinear, middle, receive, cot_update, rounded, uhidden, cot_linear,
    grads_own, grads_other, held,
):
    pairs = ((edge, cround), (middle, receive), (hidden, plinear), (middle, cot_update), (rounded, cot_update), (uhidden, cot_linear))
    for k, (x, y) in enumerate(pairs):
        store_blocks(grads_own, grads_other, k, dot_tn(x[...], y[...]) * scales[k], held, core)


def edge_back_body(cround, edge_cot, receive, cot_update, mesh_cot, w3, w5, w7, edge_grad, middle_part):
    middle_part[...] = mesh_cot[...].astype(f32) + dot_nt(cot_update[...], w7[...]) + dot_nt(receive[...], w5[...])

    def step(i, s):
        edge_grad[s, :] = (edge_cot[s, :].astype(f32) + dot_nt(cround[s, :], w3[...])).astype(bf16)

    chunks(1024 // CHUNK, step)


def encode_back_body(
    in0, in1, in2, in3, far_in, halo, far, sender_own, middle_part, pre, linear, slot, target, w2, w4,
    cot_sender_out, cot_middle_out, elinear_out, upper_out, g0, g1, g2, g3,
    source, wide,
):
    for k, block in enumerate((in0, in1, in2, in3)):
        source[64 * k : 64 * k + 64, :] = block[...]
    wide[...] = far_in[...].astype(f32)
    gather_far(wide, source, 256)
    owners = jnp.concatenate([put(halo, 0, 2, 0, 128), put(far, 0, 4, 0, 128)], axis=1)
    cot_sender = (sender_own[...] + dot(owners, source[...])).astype(bf16)
    cot_sender_out[...] = cot_sender
    cot_middle = middle_part[...] + dot_nt(cot_sender, w4[...])
    cot_middle_out[...] = cot_middle
    cot_middle = stack_halves(cot_middle)

    def step(i, s):
        receiver = pick(target, ROWS * i, ROWS, 0, 128)
        normed, inverse = norm_parts(linear[s, :])
        cot = norm_back(normed, inverse, dot(twice(receiver), cot_middle)).astype(bf16)
        elinear_out[s, :] = cot
        upper_out[s, :] = (dot_nt(cot, w2[...]) * slope(pre[s, :])).astype(bf16)

    chunks(1024 // CHUNK, step)
    for k, out in enumerate((g0, g1, g2, g3)):
        spread = put(slot, 0, 8, 512 + 256 * k, 256)
        out[...] = dot(spread, upper_out[...]).astype(bf16)


def encode_grads_body(
    scales, core, upper, slot, target, cot_middle, mesh, middle, cot_sender, hidden, elinear, w1,
    grid_own, mesh_grad, grads_own, grads_other, held,
):
    def store(k, x, y, scale):
        store_blocks(grads_own, grads_other, k, dot_tn(x, y) * scale, held, core)

    store(1, hidden[...], elinear[...], scales[1])
    store(2, middle[...], cot_sender[...], scales[2])
    receive = dot(put(target, 0, 8, 0, 128), upper[...]).astype(bf16)
    store(0, mesh[...], receive, scales[0])
    mesh_grad[...] = (cot_middle[...] + dot_nt(receive, w1[...])).astype(bf16)
    for k in range(2):
        grid_own[256 * k : 256 * k + 256, :] = dot(put(slot, 0, 8, 256 * k, 256), upper[...])


def grid_back_body(scales, core, grid_own, in0, in1, in2, in3, table, grid, w0, grid_grad, grads_own, grads_other, cot, held):
    for i in range(2):
        s = slice(256 * i, 256 * i + 256)
        total = grid_own[s, :]
        for k, block in enumerate((in0, in1, in2, in3)):
            total = total + dot(put_rows(table_rows(table, k), i * 256, 256), block[...])
        total = total.astype(bf16)
        cot[s, :] = total
        grid_grad[s, :] = dot_nt(total, w0[...]).astype(bf16)
    store_blocks(grads_own, grads_other, 0, dot_tn(grid[...], cot[...]) * scales[0], held, core)


def pair_body(*refs):
    out = refs[-1]
    place = 0
    for own, got in zip(refs[0:-1:2], refs[1:-1:2]):
        for k in range(own.shape[2]):
            out[:, :, place] = (own[:, :, k].astype(f32) + got[:, :, k].astype(f32)).astype(bf16)
            place += 1


def sum_body(terms, shard):
    total = terms[0].astype(f32)
    for d in range(1, terms.shape[0]):
        total = total + terms[d].astype(f32)
    total = total.astype(bf16)
    for p in range(shard.shape[0]):
        shard[p] = total


def summed(terms):
    rows = 32 if terms.shape[1] % 48 else 48
    spec = pl.BlockSpec((terms.shape[0], rows, 128), lambda i: (0, i, 0))
    return pl.pallas_call(
        sum_body,
        grid=(terms.shape[1] // rows,),
        in_specs=[spec],
        out_specs=spec,
        out_shape=jax.ShapeDtypeStruct(terms.shape, bf16),
        compiler_params=pltpu.CompilerParams(vmem_limit_bytes=67000000),
    )(terms)


def place_early_body(core, own, other, out):
    first = core[0] == 0
    for q in range(2):
        a, b = own[:, q].reshape(512, 128), other[:, q].reshape(512, 128)
        out[:, 128 * q : 128 * q + 128] = jnp.where(first, a, b)
        out[:, 256 + 128 * q : 384 + 128 * q] = jnp.where(first, b, a)


def place_late_body(core, own, other, kept, out):
    del kept
    place_early_body(core, own, other, out)


def swapped(value):
    return lax.ppermute(value, "core", [(0, 1), (1, 0)])


def scaled(body, scales):
    return functools.partial(body, scales)


def on_device(
    grid_latent, mesh_latent, edge_latent, mesh_cotangent, edge_cotangent, grid_send, grid_slot, grid_target,
    mesh_halo, mesh_send, mesh_slot, mesh_target, weights,
):
    peers = lax.axis_size(AXES)
    mesh_rows, latent = mesh_latent.shape
    edges = grid_slot.shape[0]
    grid_scale = 1.0 / (edges * peers) ** 0.5
    edge_scale = 1.0 / (mesh_slot.shape[0] * peers) ** 0.5
    node_scale = 1.0 / (mesh_rows * peers) ** 0.5
    grid_table = grid_send
    core = lax.axis_index("core").reshape(1)
    halo_table = mesh_halo.reshape(2, 128)
    far_table = mesh_send[0].T
    gslot, gtarget = grid_slot.reshape(8, 128), grid_target.reshape(8, 128)
    mslot, mtarget = mesh_slot.reshape(8, 128), mesh_target.reshape(8, 128)
    big, small, halo = (edges, latent), (mesh_rows, latent), (64, latent)
    vm = pltpu.VMEM

    project, *outgoing = call(
        project_body, [((512, latent), bf16)] + [((256, latent), bf16)] * 4,
        (grid_latent, grid_table), weights, (0,),
    )
    arrived = outgoing_rows(outgoing)
    (own,) = call(
        encode_own_body, [(big, f32)], (project, gslot, gtarget, mesh_latent),
        weights, (1,), scratch=(vm((768, latent), bf16),), flops=10**9,
    )
    pre, linear, hidden, middle, sender, *halos, far_out = call(
        encode_body,
        [(big, f32), (big, f32), (big, bf16), (small, bf16), (small, bf16)] + [(halo, bf16)] * 4 + [((2048, 128), bf16)],
        (own, *arrived, gslot, gtarget, mesh_latent, halo_table, far_table), weights, (2, 4),
        scratch=(vm(small, f32), vm((2048, 128), f32)), flops=2 * 10**9,
    )
    far_in = lax.all_to_all(far_out.reshape(peers, 16, 128), AXES, 0, 0, tiled=True).reshape(2048, 128)
    halo_in = outgoing_rows(halos)
    own, update_own = call(
        process_own_body, [(big, f32), (small, f32)], (middle, sender, edge_latent, mslot, mtarget),
        weights, (3, 5, 7), scratch=(vm((384, latent), bf16),), flops=2 * 10**9,
    )
    (
        mesh_update, phidden, rounded, uhidden, cot_linear, cot_update, plinear, cround, receive, sender_own,
        *halos, far_out,
    ) = call(
        process_body,
        [(small, bf16), (big, bf16)] + [(small, bf16)] * 4 + [(big, bf16)] * 2
        + [(small, bf16), (small, f32)] + [(halo, bf16)] * 4 + [((2048, 128), bf16)],
        (own, *halo_in, far_in, mslot, mtarget, middle, update_own, mesh_cotangent, edge_cotangent),
        weights, (6, 8, 9),
        scratch=(
            vm((768, latent), bf16), vm(big, f32), vm(big, f32), vm((edges, 128), f32),
            vm(small, f32), vm((2048, 128), f32), vm((8, 128), jnp.int32),
        ),
        flops=8 * 10**9,
    )
    far_back = lax.all_to_all(far_out.reshape(peers, 16, 128), AXES, 0, 0, tiled=True).reshape(2048, 128)
    halo_back = returned_rows(halos)

    def blocks(count):
        return ((32, 2, count, 16, 128), bf16)

    held = vm((latent, latent), bf16)
    early_own, early_other = call(
        scaled(process_grads_body, [edge_scale] * 3 + [node_scale] * 3),
        [blocks(6), blocks(6)],
        (core, edge_latent, cround, phidden, plinear, middle, receive, cot_update, rounded, uhidden, cot_linear),
        scratch=(held,), flops=2 * 10**9,
    )
    early_other = swapped(early_other)
    edge_grad, middle_part = call(
        edge_back_body, [(big, bf16), (small, f32)], (cround, edge_cotangent, receive, cot_update, mesh_cotangent),
        weights, (3, 5, 7),
    )
    early = (early_own.astype(f32) + early_other.astype(f32)).astype(bf16)
    early, _ = lax.optimization_barrier((early, (halo_back, far_back)))
    early = lax.all_to_all(early.reshape(64, 96, 128), CHIPS, 0, 0, tiled=True)
    cot_sender, cot_middle, elinear, upper, *partials = call(
        encode_back_body,
        [(small, bf16), (small, f32), (big, bf16), (big, bf16)] + [((256, latent), bf16)] * 4,
        (*halo_back, far_back, halo_table, far_table, sender_own, middle_part, pre, linear, gslot, gtarget),
        weights, (2, 4), scratch=(vm((768, latent), bf16), vm((2048, 128), f32)), flops=4 * 10**9,
    )
    partials = returned_rows(partials)
    grid_own, mesh_grad, late_own, late_other = call(
        scaled(encode_grads_body, [grid_scale, grid_scale, edge_scale]),
        [((512, latent), f32), (small, bf16), blocks(3), blocks(3)],
        (core, upper, gslot, gtarget, cot_middle, mesh_latent, middle, cot_sender, hidden, elinear),
        weights, (1,), scratch=(held,), flops=2 * 10**9,
    )
    early = summed(early)
    early = lax.all_to_all(early, CHIPS, 0, 0, tiled=True)
    grid_grad, last_own, last_other = call(
        scaled(grid_back_body, [grid_scale]), [((512, latent), bf16), blocks(1), blocks(1)],
        (core, grid_own, *partials, grid_table, grid_latent), weights, (0,),
        scratch=(vm((512, latent), bf16), held),
    )
    (late,) = call(
        pair_body, [blocks(4)], (last_own, swapped(last_other), late_own, swapped(late_other)),
        flops=10**6,
    )
    late, early = lax.optimization_barrier((late, early))
    late = lax.all_to_all(late.reshape(64, 64, 128), CHIPS, 0, 0, tiled=True)
    early_swapped = swapped(early).reshape(blocks(6)[0])
    early = early.reshape(blocks(6)[0])
    placed = pl.pallas_call(
        place_early_body,
        grid_spec=pltpu.PrefetchScalarGridSpec(
            num_scalar_prefetch=1,
            grid=(6,),
            in_specs=[pl.BlockSpec((32, 2, None, 16, 128), lambda i, c: (0, 0, i, 0, 0))] * 2,
            out_specs=pl.BlockSpec((None, latent, latent), lambda i, c: (i + 3 + (i + 5) // 6, 0, 0)),
        ),
        out_shape=jax.ShapeDtypeStruct(weights.shape, bf16),
        compiler_params=pltpu.CompilerParams(vmem_limit_bytes=67000000),
        name="place_early",
    )(core, early, early_swapped)
    late = summed(late)
    late = lax.all_to_all(late, CHIPS, 0, 0, tiled=True)
    other = swapped(late).reshape(blocks(4)[0])
    late = late.reshape(blocks(4)[0])
    weight_grads = pl.pallas_call(
        place_late_body,
        grid_spec=pltpu.PrefetchScalarGridSpec(
            num_scalar_prefetch=1,
            grid=(4,),
            in_specs=[pl.BlockSpec((32, 2, None, 16, 128), lambda i, c: (0, 0, i, 0, 0))] * 2
            + [pl.BlockSpec(memory_space=pl.ANY)],
            out_specs=pl.BlockSpec((None, latent, latent), lambda i, c: (i + i // 3, 0, 0)),
        ),
        out_shape=jax.ShapeDtypeStruct(weights.shape, bf16),
        input_output_aliases={3: 0},
        compiler_params=pltpu.CompilerParams(vmem_limit_bytes=12 << 20),
        name="place_late",
    )(core, late, other, placed)
    return (mesh_update, grid_grad, mesh_grad, edge_grad, weight_grads)


def solution(mesh):
    row = P(AXES, None)
    wide = jax.sharding.Mesh(mesh.devices.reshape(4, 2, 4, 4), AXES)

    return jax.shard_map(
        on_device,
        mesh=wide,
        in_specs=(row, row, row, row, row, P(AXES, None, None), P(AXES), P(AXES), P(AXES, None, None),
                  P(AXES, None, None), P(AXES), P(AXES), P()),
        out_specs=(row, row, row, row, P()),
        check_vma=False,
    )
```
